32 devices in a mesh: dp: 4 (over x, core), tensor: 8 (over z, y).
Axes of the slice: x: 2, y: 2, z: 4, core: 2. Of those that a mesh axis runs over, the one named last changes fastest.
Arguments:
- hidden_in: bfloat16 [24576, 768], P(('dp', 'tensor')), may hold values from -6 to 6
- visual_maps: bfloat16 [4704, 256], P(('dp', 'tensor')), may hold values from -63 to 63
- lengths: int32 [32, 3], P(('dp', 'tensor')), may hold values from 50 to 561, as said below
- box_x: int32 [24576], P(('dp', 'tensor')), may hold values from 0 to 1000
- box_y: int32 [24576], P(('dp', 'tensor')), may hold values from 0 to 1000
- cotangent: bfloat16 [24576, 768], P(('dp', 'tensor')), may hold values from -6 to 6
- vis_weight: float32 [256, 768], P('dp', 'tensor'), may hold values from -0.375 to 0.375
- vis_moments: float32 [2, 256, 768], P(None, 'dp', 'tensor'), may hold values from -31.039934 to 39.81312, as said below
- qkv_weight: float32 [768, 2304], P('dp', 'tensor'), may hold values from -0.21650635 to 0.21650635
- qkv_moments: float32 [2, 768, 2304], P(None, 'dp', 'tensor'), may hold values from -6.8977631 to 6.8977631, as said below
- out_weight: float32 [768, 768], P('dp', 'tensor'), may hold values from -0.61237244 to 0.61237244
- out_moments: float32 [2, 768, 768], P(None, 'dp', 'tensor'), may hold values from -13.7955262 to 13.7955262, as said below
- up_weight: float32 [768, 3072], P('dp', 'tensor'), may hold values from -0.21650635 to 0.21650635
- up_moments: float32 [2, 768, 3072], P(None, 'dp', 'tensor'), may hold values from -17.244408 to 17.244408, as said below
- down_weight: float32 [3072, 768], P('tensor', 'dp'), may hold values from -0.108253175 to 0.108253175
- down_moments: float32 [2, 3072, 768], P(None, 'tensor', 'dp'), may hold values from -27.5910525 to 31.45728, as said below
- up_bias: float32 [3072], replicated, may hold values from -3 to 3
- up_bias_moments: float32 [2, 3072], replicated, may hold values from -17.244408 to 17.244408, as said below
- bn_params: float32 [2, 256], replicated, may hold values from 0.5 to 1.5
- bn_moments: float32 [2, 2, 256], replicated, may hold values from -34.488816 to 49.152, as said below
- norm_params: float32 [4, 768], replicated, may hold values from 0.5 to 1.5
- norm_moments: float32 [2, 4, 768], replicated, may hold values from -55.182105 to 125.82912, as said below
- bias_rows: float32 [5, 768], replicated, may hold values from -3 to 3
- bias_moments: float32 [2, 5, 768], replicated, may hold values from -55.182105 to 125.82912, as said below
- rel_tables: float32 [12, 160], replicated, may hold values from -3 to 3
- table_moments: float32 [2, 12, 160], replicated, may hold values from -13.7955262 to 13.7955262, as said below
Outputs:
- block_out: bfloat16 [24576, 768], P(('dp', 'tensor'))
- grad_hidden: float32 [24576, 768], P(('dp', 'tensor'))
- lamb_norms: float32 [3, 10], replicated
- vis_grad: float32 [256, 768], P('dp', 'tensor')
- vis_new: float32 [256, 768], P('dp', 'tensor')
- vis_moments_new: float32 [2, 256, 768], P(None, 'dp', 'tensor')
- vis_copy: bfloat16 [256, 768], P('dp', 'tensor')
- qkv_grad: float32 [768, 2304], P('dp', 'tensor')
- qkv_new: float32 [768, 2304], P('dp', 'tensor')
- qkv_moments_new: float32 [2, 768, 2304], P(None, 'dp', 'tensor')
- qkv_copy: bfloat16 [768, 2304], P('dp', 'tensor')
- out_grad: float32 [768, 768], P('dp', 'tensor')
- out_new: float32 [768, 768], P('dp', 'tensor')
- out_moments_new: float32 [2, 768, 768], P(None, 'dp', 'tensor')
- out_copy: bfloat16 [768, 768], P('dp', 'tensor')
- up_grad: float32 [768, 3072], P('dp', 'tensor')
- up_new: float32 [768, 3072], P('dp', 'tensor')
- up_moments_new: float32 [2, 768, 3072], P(None, 'dp', 'tensor')
- up_copy: bfloat16 [768, 3072], P('dp', 'tensor')
- down_grad: float32 [3072, 768], P('tensor', 'dp')
- down_new: float32 [3072, 768], P('tensor', 'dp')
- down_moments_new: float32 [2, 3072, 768], P(None, 'tensor', 'dp')
- down_copy: bfloat16 [3072, 768], P('tensor', 'dp')
- up_bias_grad: float32 [3072], replicated
- up_bias_new: float32 [3072], replicated
- up_bias_moments_new: float32 [2, 3072], replicated
- up_bias_copy: bfloat16 [3072], replicated
- bn_grad: float32 [2, 256], replicated
- bn_new: float32 [2, 256], replicated
- bn_moments_new: float32 [2, 2, 256], replicated
- bn_copy: bfloat16 [2, 256], replicated
- norm_grad: float32 [4, 768], replicated
- norm_new: float32 [4, 768], replicated
- norm_moments_new: float32 [2, 4, 768], replicated
- norm_copy: bfloat16 [4, 768], replicated
- bias_grad: float32 [5, 768], replicated
- bias_new: float32 [5, 768], replicated
- bias_moments_new: float32 [2, 5, 768], replicated
- bias_copy: bfloat16 [5, 768], replicated
- table_grad: float32 [12, 160], replicated
- table_new: float32 [12, 160], replicated
- table_moments_new: float32 [2, 12, 160], replicated
- table_copy: bfloat16 [12, 160], replicated
The draws below stay inside these ranges and needn't reach their ends.
Inputs may be any that keep to these rules, and one draw needn't show every extreme that they name: Row b gives the documents of block b in row order; each has at least 50 rows, a row of lengths sums to at most 768, and some document has exactly 561 rows. `vis_moments`: row 1 is positive. `qkv_moments`: row 1 is positive. `out_moments`: row 1 is positive. `up_moments`: row 1 is positive. `down_moments`: row 1 is positive. `up_bias_moments`: row 1 is positive. `bn_moments`: row 1 is positive. `norm_moments`: row 1 is positive. `bias_moments`: row 1 is positive. `table_moments`: row 1 is positive.
All inputs are finite; a program needn't handle non-finite values.
Results may differ from the reference program's by a relative error of at most 0.025.
Values may be sent and summed in bfloat16 or wider, within the bound.
No kernel may reach another device: no remote copies, remote signals or barrier semaphores. Data moves between devices by JAX's collectives and lax.ppermute only.
A program may use at most 448 MiB of HBM per device.

```python
import math
import jax
import jax.numpy as jnp
from jax import lax

D = 768
HEADS = 12
HDIM = 64
FF = 3072
CHANNELS = 256
PATCHES = 49
REL1 = 32
REL2 = 64
DIST1 = 128
DIST2 = 256
COORDS = 1001
MAXLEN = 561
DOCS_DEV = 3
STEP = 10
TOK_DEV = 768
TOKENS = 24576
DOCS = 96
VIS_ROWS = 4704


def rising_weight(key, rows, cols, fan_in, along_rows):
    base = jnp.clip(jax.random.normal(key, (rows, cols), jnp.float32), -4.0, 4.0)
    top_factor = 3.0
    count = rows if along_rows else cols
    position = jnp.arange(count, dtype=jnp.float32) / max(count - 1, 1)
    mean_square = 1.0 + (top_factor - 1.0) + (top_factor - 1.0) ** 2 / 3.0
    factor = (1.0 + (top_factor - 1.0) * position) / math.sqrt(mean_square)
    if along_rows:
        scaled = base * factor[:, None]
    else:
        scaled = base * factor[None, :]
    return scaled * fan_in ** (-0.5)


def draw_vis_weight(key, part):
    return rising_weight(key, CHANNELS, D, CHANNELS, True)


def draw_qkv_weight(key, part):
    return rising_weight(key, D, 3 * D, D, True)


def draw_out_weight(key, part):
    return rising_weight(key, D, D, D // 8, True)


def draw_up_weight(key, part):
    return rising_weight(key, D, FF, D, True)


def draw_down_weight(key, part):
    return rising_weight(key, FF, D, FF, False)


def moment_pair(key, shape, grad_scale):
    sign_key, size_key = jax.random.split(key)
    signed = jnp.clip(jax.random.normal(sign_key, shape, jnp.float32), -4.0, 4.0)
    spread = jnp.exp(jax.random.uniform(size_key, shape, jnp.float32, math.log(0.5), math.log(8.0)))
    return jnp.stack([0.11 * grad_scale * signed, 0.001 * grad_scale * grad_scale * spread])


def draw_vis_moments(key, part):
    return moment_pair(key, (CHANNELS, D), 0.45 * math.sqrt(TOKENS))


def draw_qkv_moments(key, part):
    return moment_pair(key, (D, 3 * D), 0.1 * math.sqrt(TOKENS))


def draw_out_moments(key, part):
    return moment_pair(key, (D, D), 0.2 * math.sqrt(TOKENS))


def draw_up_moments(key, part):
    return moment_pair(key, (D, FF), 0.25 * math.sqrt(TOKENS))


def draw_down_moments(key, part):
    return moment_pair(key, (FF, D), 0.4 * math.sqrt(TOKENS))


def draw_up_bias_moments(key, part):
    return moment_pair(key, (FF,), 0.25 * math.sqrt(TOKENS))


def draw_bn_moments(key, part):
    return moment_pair(key, (2, CHANNELS), 0.5 * math.sqrt(TOKENS))


def draw_norm_moments(key, part):
    return moment_pair(key, (4, D), 0.8 * math.sqrt(TOKENS))


def draw_bias_moments(key, part):
    return moment_pair(key, (5, D), 0.8 * math.sqrt(TOKENS))


def draw_table_moments(key, part):
    return moment_pair(key, (HEADS, REL1 + 2 * REL2), 0.2 * math.sqrt(TOKENS))


def draw_visual_maps(key, part):
    row_total = VIS_ROWS
    keys_list = jax.random.split(key, 3)
    position = jnp.arange(row_total, dtype=jnp.int32).astype(jnp.float32) / max(row_total - 1, 1)
    row_scale = (1.0 + 2.0 * position) * jnp.exp(jax.random.uniform(keys_list[0], (row_total,), jnp.float32, 0.0, math.log(3.0)))
    column_mean = jnp.clip(jax.random.normal(keys_list[1], (CHANNELS,), jnp.float32), -3.0, 3.0)
    column_mean = 0.5 * column_mean
    noise_part = jnp.clip(jax.random.normal(keys_list[2], (row_total, CHANNELS), jnp.float32), -4.0, 4.0)
    return ((column_mean[None, :] + noise_part) * row_scale[:, None]).astype(jnp.bfloat16)


def draw_lengths(key, part):
    device_count = DOCS // DOCS_DEV
    keys_list = jax.random.split(key, 4 + DOCS_DEV)
    least_len = PATCHES + 1
    extra_most = MAXLEN - least_len
    upper_one = jax.random.randint(keys_list[0], (device_count,), 0, extra_most + 1)
    upper_two = jax.random.randint(keys_list[1], (device_count,), 0, extra_most + 1)
    long_doc = least_len + upper_one * upper_two // extra_most
    chosen = jax.random.randint(keys_list[2], (), 0, device_count)
    long_doc = jnp.where(jnp.arange(device_count, dtype=jnp.int32) == chosen, MAXLEN, long_doc)
    room_left = TOK_DEV - long_doc - (DOCS_DEV - 1) * least_len
    columns = [long_doc]
    for doc_number in range(DOCS_DEV - 1):
        share_part = jax.random.randint(keys_list[4 + doc_number], (device_count,), 0, 1001)
        extra_rows = jnp.minimum(room_left * share_part // 1000, extra_most)
        columns.append(least_len + extra_rows)
        room_left = room_left - extra_rows
    stacked = jnp.stack(columns, axis=1)
    ranking = jax.random.randint(keys_list[3], (device_count, DOCS_DEV), 0, 1 << 20) * DOCS_DEV + jnp.arange(DOCS_DEV, dtype=jnp.int32)[None, :]
    doc_order = jnp.argsort(ranking, axis=1)
    return jnp.take_along_axis(stacked, doc_order, axis=1).astype(jnp.int32)


def set_ends(drawn, rng, least, largest):
    place = [jax.random.randint(jax.random.fold_in(rng, axis), (), 0, length) for axis, length in enumerate(drawn.shape)]
    main_axis = drawn.shape.index(max(drawn.shape))
    neighbour = place[:main_axis] + [(place[main_axis] + 1) % drawn.shape[main_axis]] + place[main_axis + 1:]
    return drawn.at[tuple(place)].set(least).at[tuple(neighbour)].set(largest)


def shard_levels(stream_key, dims, cuts, smallest, top_value):
    gain, own = 1.0, jax.random.fold_in(stream_key, 6)
    for dim, blocks in cuts:
        heights = jnp.exp(jax.random.uniform(jax.random.fold_in(own, dim), (blocks,), jnp.float32, smallest / len(cuts), top_value / len(cuts)))
        gain = gain * jnp.repeat(heights, dims[dim] // blocks).reshape([-1 if axis == dim else 1 for axis in range(len(dims))])
    return gain


def gaussian(stream_key, shape, deviation, reach, cuts=(), held_as=jnp.bfloat16):
    result = jax.random.normal(stream_key, shape, jnp.float32) * deviation
    if len(cuts) > 0:
        result = shard_levels(stream_key, shape, cuts, -0.22, 0.18) * result
    return jnp.clip(result, min=-reach, max=reach).astype(held_as)


def setup_inputs(seed: int = 0) -> dict:
    streams_of = jax.random.split(jax.random.key(seed), 27)
    hidden_in = gaussian(streams_of[0], (TOKENS, D), 1.0, 6.0, ((0, 32),))
    visual_maps = draw_visual_maps(jax.random.fold_in(streams_of[26], 71), 0)
    lengths = draw_lengths(jax.random.fold_in(streams_of[26], 71), 0)
    box_x = set_ends(jax.random.randint(streams_of[3], (TOKENS,), 0, COORDS), jax.random.fold_in(streams_of[3], 1), 0, COORDS - 1).astype(jnp.int32)
    box_y = set_ends(jax.random.randint(streams_of[4], (TOKENS,), 0, COORDS), jax.random.fold_in(streams_of[4], 1), 0, COORDS - 1).astype(jnp.int32)
    cotangent = gaussian(streams_of[5], (TOKENS, D), 1.0, 6.0, ((0, 32),))
    vis_weight = draw_vis_weight(jax.random.fold_in(streams_of[26], 71), 0)
    vis_moments = draw_vis_moments(jax.random.fold_in(streams_of[26], 71), 0)
    qkv_weight = draw_qkv_weight(jax.random.fold_in(streams_of[26], 71), 0)
    qkv_moments = draw_qkv_moments(jax.random.fold_in(streams_of[26], 71), 0)
    out_weight = draw_out_weight(jax.random.fold_in(streams_of[26], 71), 0)
    out_moments = draw_out_moments(jax.random.fold_in(streams_of[26], 71), 0)
    up_weight = draw_up_weight(jax.random.fold_in(streams_of[26], 71), 0)
    up_moments = draw_up_moments(jax.random.fold_in(streams_of[26], 71), 0)
    down_weight = draw_down_weight(jax.random.fold_in(streams_of[26], 71), 0)
    down_moments = draw_down_moments(jax.random.fold_in(streams_of[26], 71), 0)
    up_bias = gaussian(streams_of[16], (FF,), 0.5, 3.0, (), jnp.float32)
    up_bias_moments = draw_up_bias_moments(jax.random.fold_in(streams_of[26], 71), 0)
    bn_params = jnp.clip(jax.random.uniform(streams_of[18], (2, CHANNELS), jnp.float32, 0.5, 1.5), 0.5, 1.5)
    bn_moments = draw_bn_moments(jax.random.fold_in(streams_of[26], 71), 0)
    norm_params = jnp.clip(jax.random.uniform(streams_of[20], (4, D), jnp.float32, 0.5, 1.5), 0.5, 1.5)
    norm_moments = draw_norm_moments(jax.random.fold_in(streams_of[26], 71), 0)
    bias_rows = gaussian(streams_of[22], (5, D), 0.5, 3.0, (), jnp.float32)
    bias_moments = draw_bias_moments(jax.random.fold_in(streams_of[26], 71), 0)
    rel_tables = gaussian(streams_of[24], (HEADS, REL1 + 2 * REL2), 0.5, 3.0, (), jnp.float32)
    table_moments = draw_table_moments(jax.random.fold_in(streams_of[26], 71), 0)
    return dict(hidden_in=hidden_in, visual_maps=visual_maps, lengths=lengths, box_x=box_x, box_y=box_y, cotangent=cotangent, vis_weight=vis_weight, vis_moments=vis_moments, qkv_weight=qkv_weight, qkv_moments=qkv_moments, out_weight=out_weight, out_moments=out_moments, up_weight=up_weight, up_moments=up_moments, down_weight=down_weight, down_moments=down_moments, up_bias=up_bias, up_bias_moments=up_bias_moments, bn_params=bn_params, bn_moments=bn_moments, norm_params=norm_params, norm_moments=norm_moments, bias_rows=bias_rows, bias_moments=bias_moments, rel_tables=rel_tables, table_moments=table_moments)


@jax.custom_vjp
def low(v):
    return lax.optimization_barrier(v.astype(jnp.bfloat16)).astype(jnp.float32)

@jax.custom_vjp
def low_back(v):
    return v

def low_keep(v):
    return (low(v), None)

def low_pass(kept, grad):
    return (grad,)

def back_keep(v):
    return (v, None)

def back_low(kept, grad):
    return (low(grad),)
low.defvjp(low_keep, low_pass)
low_back.defvjp(back_keep, back_low)
layer_eps = 1e-06
batch_eps = 1e-05
beta_first = 0.9
beta_second = 0.999
adam_eps = 1e-06
weight_decay = 0.01
learn_rate = 0.4
masked_score = -1000000000.0

def dense_product(left, right):
    return jnp.dot(left, right, precision=lax.Precision.HIGHEST, preferred_element_type=jnp.float32)

def layer_norm(values, gain_row, shift_row):
    centre = values - lax.optimization_barrier(jnp.mean(values, axis=-1, keepdims=True))
    spread = lax.rsqrt(lax.optimization_barrier(jnp.mean(centre * centre, axis=-1, keepdims=True)) + layer_eps)
    return centre * spread * gain_row + shift_row

def bucket_edges(bucket_count, max_distance):
    half = bucket_count // 2
    exact = half // 2
    edges = []
    for level in range(1, half):
        if level < exact:
            edges.append(level)
        else:
            found = max_distance
            for distance in range(exact, max_distance + 1):
                if exact + int(math.log(distance / exact) / math.log(max_distance / exact) * (half - exact)) >= level:
                    found = distance
                    break
            edges.append(found)
    return edges

def bucket_index(delta, bucket_count, max_distance):
    half = bucket_count // 2
    distance = jnp.abs(delta)
    level = jnp.zeros(delta.shape, jnp.int32)
    for edge in bucket_edges(bucket_count, max_distance):
        level = level + (distance >= edge).astype(jnp.int32)
    return (jnp.where(delta > 0, half, 0) + level).astype(jnp.int32)

def doc_layout(doc_lengths, row_count):
    doc_ends = jnp.cumsum(doc_lengths).astype(jnp.int32)
    doc_count = doc_lengths.shape[0]
    row_index = jnp.arange(row_count, dtype=jnp.int32)
    doc_index = lax.optimization_barrier(jnp.sum((row_index[:, None] >= doc_ends[None, :]).astype(jnp.int32), axis=1))
    is_valid = doc_index < doc_count
    doc_numbers = jnp.arange(doc_count, dtype=jnp.int32)
    own_end = lax.optimization_barrier(jnp.sum(jnp.where(doc_index[:, None] == doc_numbers[None, :], doc_ends[None, :], 0), axis=1))
    offset = row_index - (own_end - PATCHES)
    is_visual = is_valid & (offset >= 0)
    visual_index = jnp.where(is_visual, doc_index * PATCHES + offset, 0).astype(jnp.int32)
    return (doc_index, is_valid, is_visual, visual_index)

def visual_rows(doc_lengths):
    doc_ends = jnp.cumsum(doc_lengths).astype(jnp.int32)
    slot_index = jnp.arange(doc_lengths.shape[0] * PATCHES, dtype=jnp.int32)
    return (jnp.repeat(doc_ends, PATCHES) - PATCHES + slot_index % PATCHES).astype(jnp.int32)

def pair_bias(tables, box_x, box_y, row_count):
    row_index = jnp.arange(row_count, dtype=jnp.int32)
    linear = bucket_index(row_index[None, :] - row_index[:, None], REL1, DIST1)
    across = bucket_index(box_x[None, :] - box_x[:, None], REL2, DIST2) + REL1
    downward = bucket_index(box_y[None, :] - box_y[:, None], REL2, DIST2) + REL1 + REL2
    return jnp.take(tables, linear, axis=1) + jnp.take(tables, across, axis=1) + jnp.take(tables, downward, axis=1)

def attend_block(inputs, qkv_low, out_low, bias_rows, rel_tables):
    hidden, doc_index, box_x, box_y = inputs
    row_count = hidden.shape[0]
    qkv_bias = jnp.concatenate([bias_rows[1], jnp.zeros_like(bias_rows[1]), bias_rows[2]])
    projected = low(low_back(dense_product(low(hidden), qkv_low) + qkv_bias))
    queries = projected[:, :D].reshape(row_count, HEADS, HDIM)
    keys_all = projected[:, D:2 * D].reshape(row_count, HEADS, HDIM)
    values_all = projected[:, 2 * D:].reshape(row_count, HEADS, HDIM)
    plain_scores = jnp.einsum('qhd,khd->hqk', queries, keys_all, precision=lax.Precision.HIGHEST) * HDIM ** (-0.5)
    scores = plain_scores + pair_bias(rel_tables, box_x, box_y, row_count)
    same_doc = (doc_index[:, None] == doc_index[None, :])[None]
    scores = low_back(jnp.where(same_doc, scores, masked_score))
    attn_probs = jax.nn.softmax(scores, axis=-1)
    context = jnp.einsum('hqk,khd->qhd', low(attn_probs), values_all, precision=lax.Precision.HIGHEST).reshape(row_count, D)
    context = low(low_back(context))
    return low_back(dense_product(context, out_low) + bias_rows[3])

def forward(hidden, vis_weight, qkv_weight, out_weight, up_weight, down_weight, up_bias, bn_params, norm_params, bias_rows, rel_tables, visual_value, lengths, box_x, box_y):
    vis_mean = lax.optimization_barrier(jnp.mean(visual_value, axis=0))
    vis_var = lax.optimization_barrier(jnp.mean(visual_value * visual_value, axis=0)) - vis_mean * vis_mean
    normed = (visual_value - vis_mean) * lax.rsqrt(vis_var + batch_eps) * bn_params[0] + bn_params[1]
    embedded = low_back(dense_product(low(normed), low(vis_weight)) + bias_rows[0])
    device_count = lengths.shape[0]
    token_rows = jax.vmap(visual_rows)(lengths) + (jnp.arange(device_count, dtype=jnp.int32) * TOK_DEV)[:, None]
    mixed_rows = hidden.at[token_rows.reshape(-1)].add(embedded)
    doc_index = jax.vmap(lambda doc_row: doc_layout(doc_row, TOK_DEV)[0])(lengths)
    blocks = (mixed_rows.reshape(device_count, TOK_DEV, D), doc_index, box_x.reshape(device_count, TOK_DEV), box_y.reshape(device_count, TOK_DEV))
    qkv_low = low(qkv_weight)
    out_low = low(out_weight)
    attended = lax.map(jax.checkpoint(lambda inputs: attend_block(inputs, qkv_low, out_low, bias_rows, rel_tables)), blocks).reshape(-1, D)
    first_norm = layer_norm(mixed_rows + attended, norm_params[0], norm_params[1])
    pre_act = low_back(dense_product(low(first_norm), low(up_weight)) + up_bias)
    ffn_out = low_back(dense_product(low(jax.nn.gelu(pre_act, approximate=False)), low(down_weight)))
    return layer_norm(first_norm + ffn_out + bias_rows[4], norm_params[2], norm_params[3])

def lamb_direction(weight, moments, gradient):
    first_moment = beta_first * moments[0] + (1.0 - beta_first) * gradient
    second_moment = beta_second * moments[1] + (1.0 - beta_second) * gradient * gradient
    direction = first_moment / (1.0 - beta_first ** STEP) / (jnp.sqrt(second_moment / (1.0 - beta_second ** STEP)) + adam_eps) + weight_decay * weight
    return (jnp.stack([first_moment, second_moment]), direction)

def reference(hidden_in, visual_maps, lengths, box_x, box_y, cotangent, vis_weight, vis_moments, qkv_weight, qkv_moments, out_weight, out_moments, up_weight, up_moments, down_weight, down_moments, up_bias, up_bias_moments, bn_params, bn_moments, norm_params, norm_moments, bias_rows, bias_moments, rel_tables, table_moments):
    visual_value = visual_maps.astype(jnp.float32)

    def whole_forward(hidden_value, vis_value, qkv_value, out_value, up_value, down_value, up_bias_value, bn_value, norm_value, bias_value, table_value):
        return forward(hidden_value, vis_value, qkv_value, out_value, up_value, down_value, up_bias_value, bn_value, norm_value, bias_value, table_value, visual_value, lengths, box_x, box_y)
    block_norm, pullback = jax.vjp(whole_forward, hidden_in.astype(jnp.float32), vis_weight, qkv_weight, out_weight, up_weight, down_weight, up_bias, bn_params, norm_params, bias_rows, rel_tables)
    is_valid = jax.vmap(lambda doc_row: doc_layout(doc_row, TOK_DEV)[1])(lengths).reshape(-1)
    gradients = pullback(cotangent.astype(jnp.float32) * is_valid[:, None].astype(jnp.float32))
    masters = [vis_weight, qkv_weight, out_weight, up_weight, down_weight, up_bias, bn_params, norm_params, bias_rows, rel_tables]
    moment_list = [vis_moments, qkv_moments, out_moments, up_moments, down_moments, up_bias_moments, bn_moments, norm_moments, bias_moments, table_moments]
    steps_made = [lamb_direction(masters[number], moment_list[number], gradients[number + 1]) for number in range(10)]
    weight_norms = jnp.stack([jnp.sqrt(jnp.sum(weight * weight)) for weight in masters])
    update_norms = jnp.stack([jnp.sqrt(jnp.sum(made[1] * made[1])) for made in steps_made])
    trust_ratio = weight_norms / update_norms
    lamb_norms = jnp.stack([weight_norms, update_norms, trust_ratio])
    results = []
    for number in range(10):
        new_weight = masters[number] - learn_rate * trust_ratio[number] * steps_made[number][1]
        results.extend([gradients[number + 1], new_weight, steps_made[number][0], new_weight.astype(jnp.bfloat16)])
    return (block_norm.astype(jnp.bfloat16), gradients[0], lamb_norms, results[0], results[1], results[2], results[3], results[4], results[5], results[6], results[7], results[8], results[9], results[10], results[11], results[12], results[13], results[14], results[15], results[16], results[17], results[18], results[19], results[20], results[21], results[22], results[23], results[24], results[25], results[26], results[27], results[28], results[29], results[30], results[31], results[32], results[33], results[34], results[35], results[36], results[37], results[38], results[39])
```

```python
import functools
import math

import jax
import jax.numpy as jnp
import numpy as np
from jax import lax
from jax.experimental import pallas as pl
from jax.experimental.pallas import tpu as pltpu
from jax.sharding import PartitionSpec as P

HEADS = 12
HDIM = 64
PATCHES = 49
REL1 = 32
REL2 = 64
DIST1 = 128
DIST2 = 256
STEP = 10
LANES = 128

layer_eps = 1e-06
batch_eps = 1e-05
beta_first = 0.9
beta_second = 0.999
adam_eps = 1e-06
weight_decay = 0.01
learn_rate = 0.4
masked_score = -1000000000.0
f32 = jnp.float32
bf16 = jnp.bfloat16
SMEM_SPEC = pl.BlockSpec(memory_space=pltpu.SMEM)


def dot_nn(left, right):
    return lax.dot_general(left, right, (((1,), (0,)), ((), ())), preferred_element_type=f32)


def dot_nt(left, right):
    return lax.dot_general(left, right, (((1,), (1,)), ((), ())), preferred_element_type=f32)


def dot_tn(left, right):
    return lax.dot_general(left, right, (((0,), (0,)), ((), ())), preferred_element_type=f32)


def whole_spec(shape):
    zeros = (0,) * len(shape)
    return pl.BlockSpec(tuple(shape), lambda *_: zeros)


def struct(shape, dtype):
    return jax.ShapeDtypeStruct(tuple(shape), dtype)


def bucket_edges(bucket_count, max_distance):
    half = bucket_count // 2
    exact = half // 2
    edges = []
    for level in range(1, half):
        if level < exact:
            edges.append(level)
        else:
            found = max_distance
            for distance in range(exact, max_distance + 1):
                if (
                    exact
                    + int(
                        math.log(distance / exact) / math.log(max_distance / exact) * (half - exact)
                    )
                    >= level
                ):
                    found = distance
                    break
            edges.append(found)
    return edges


EDGES1 = bucket_edges(REL1, DIST1)
EDGES2 = bucket_edges(REL2, DIST2)


def bucket_index(delta, bucket_count, edges):
    half = bucket_count // 2
    exact = half // 2
    distance = jnp.abs(delta)
    level = jnp.minimum(distance, exact)
    for edge in edges[exact:]:
        level = level + (distance >= edge).astype(jnp.int32)
    return jnp.where(delta > 0, half, 0) + level


def doc_ends(lens_ref):
    ends = []
    total = None
    for k in range(lens_ref.shape[1]):
        total = lens_ref[0, k] if total is None else total + lens_ref[0, k]
        ends.append(total)
    return ends


def doc_of(rows, ends):
    found = jnp.zeros(rows.shape, jnp.int32)
    for end in ends:
        found = found + (rows >= end).astype(jnp.int32)
    return found


def visual_mask(rows, ends):
    hit = None
    for end in ends:
        inside = (rows >= end - PATCHES) & (rows < end)
        hit = inside if hit is None else hit | inside
    return hit


def column_of(row_block):
    return jnp.transpose(jnp.broadcast_to(row_block, (LANES, LANES)))


def bias_kernel(lens_ref, xs_ref, ys_ref, xt_ref, yt_ref, tab_ref, out_ref):
    tile = out_ref.shape[1]
    cols_total = out_ref.shape[2]
    ends = doc_ends(lens_ref)
    start = pl.program_id(0) * tile
    rows = lax.broadcasted_iota(jnp.int32, (tile, LANES), 0) + start
    lanes = lax.broadcasted_iota(jnp.int32, (tile, LANES), 1)
    row_doc = doc_of(rows, ends)
    x_col = column_of(xt_ref[...])
    y_col = column_of(yt_ref[...])
    table = tab_ref[...]
    table_lin = jnp.concatenate(
        [table[:, :REL1], jnp.zeros((HEADS, LANES - REL1), f32)], axis=1
    )
    table_xy = table[:, REL1:]

    def one_chunk(c, carry):
        offset = pl.multiple_of(c * LANES, LANES)
        cols = lanes + offset
        lin = bucket_index(cols - rows, REL1, EDGES1)
        across = bucket_index(xs_ref[:, pl.ds(offset, LANES)] - x_col, REL2, EDGES2)
        down = bucket_index(ys_ref[:, pl.ds(offset, LANES)] - y_col, REL2, EDGES2) + REL2
        same = row_doc == doc_of(cols, ends)
        for h in range(HEADS):
            flat_lin = jnp.broadcast_to(table_lin[h : h + 1, :], (tile, LANES))
            flat_xy = jnp.broadcast_to(table_xy[h : h + 1, :], (tile, LANES))
            total = (
                jnp.take_along_axis(flat_lin, lin, axis=1)
                + jnp.take_along_axis(flat_xy, across, axis=1)
                + jnp.take_along_axis(flat_xy, down, axis=1)
            )
            out_ref[h, :, pl.ds(offset, LANES)] = jnp.where(same, total, masked_score).astype(
                out_ref.dtype
            )
        return carry

    lax.fori_loop(0, cols_total // LANES, one_chunk, 0)


def relative_bias(lengths, box_x, box_y, tables):
    rows = box_x.shape[1]
    tile = LANES
    row_spec = pl.BlockSpec((1, tile), lambda i: (0, i))
    return pl.pallas_call(
        bias_kernel,
        grid=(rows // tile,),
        in_specs=[
            SMEM_SPEC,
            whole_spec((1, rows)),
            whole_spec((1, rows)),
            row_spec,
            row_spec,
            whole_spec(tables.shape),
        ],
        out_specs=pl.BlockSpec((HEADS, tile, rows), lambda i: (0, i, 0)),
        out_shape=struct((HEADS, rows, rows), f32),
        name="relative_bias",
    )(lengths, box_x, box_y, box_x, box_y, tables)


def front_kernel(
    lens_ref,
    hidden_ref,
    maps_ref,
    stats_ref,
    bn_ref,
    qo_ref,
    vis_ref,
    bias_ref,
    mixed_ref,
    mixed_b_ref,
    proj_ref,
    wqkv_ref,
    wout_ref,
    normed_ref,
    hat_ref,
    *,
    total_rows,
    qkv_n,
    part_rows,
):
    tile = hidden_ref.shape[0]
    width = hidden_ref.shape[1]
    parts, dp_parts, _, block_n = qo_ref.shape
    out_n = block_n - qkv_n

    @pl.when(pl.program_id(0) == 0)
    def _():
        def one_part(d, carry):
            place = pl.ds(pl.multiple_of(d * part_rows, 16), part_rows)
            for t in range(parts):
                block = qo_ref[t, d, :part_rows, :]
                wqkv_ref[place, t * qkv_n : (t + 1) * qkv_n] = block[:, :qkv_n]
                wout_ref[place, t * out_n : (t + 1) * out_n] = block[:, qkv_n:]
            return carry

        lax.fori_loop(0, dp_parts, one_part, 0)

    ends = doc_ends(lens_ref)
    start = pl.program_id(0) * tile
    visual_total, channels = maps_ref.shape
    rows = lax.broadcasted_iota(jnp.int32, (tile, visual_total), 0) + start
    slots = lax.broadcasted_iota(jnp.int32, (tile, visual_total), 1)
    target = slots
    for k, end in enumerate(ends):
        target = jnp.where(slots >= k * PATCHES, slots - (k + 1) * PATCHES + end, target)
    select = (rows == target).astype(f32).astype(bf16)
    picked = dot_nn(select, maps_ref[...])
    is_visual = visual_mask(
        lax.broadcasted_iota(jnp.int32, (tile, channels), 0) + start, ends
    )
    mean = stats_ref[0:1, :] / total_rows
    var = stats_ref[1:2, :] / total_rows - mean * mean
    hat = (picked - mean) * lax.rsqrt(var + batch_eps)
    hat = jnp.where(is_visual, hat, 0.0)
    hat_ref[...] = hat
    normed = jnp.where(is_visual, hat * bn_ref[0:1, :] + bn_ref[1:2, :], 0.0).astype(bf16)
    normed_ref[...] = normed
    embedded = dot_nn(normed, vis_ref[...]) + bias_ref[0:1, :]
    row_visual = visual_mask(lax.broadcasted_iota(jnp.int32, (tile, width), 0) + start, ends)
    mixed = hidden_ref[...].astype(f32) + jnp.where(row_visual, embedded, 0.0)
    mixed_ref[...] = mixed
    mixed_b = mixed.astype(bf16)
    mixed_b_ref[...] = mixed_b
    for part in range(3):
        columns = slice(part * width, (part + 1) * width)
        piece = dot_nn(mixed_b, wqkv_ref[:, columns])
        if part == 0:
            piece = piece + bias_ref[1:2, :]
        if part == 2:
            piece = piece + bias_ref[2:3, :]
        proj_ref[:, columns] = piece.astype(bf16)


def front(lengths, hidden, maps, stats, bn_params, qo_all, vis_full, bias_rows, total_rows, qkv_n, part_rows):
    rows, width = hidden.shape
    channels = maps.shape[1]
    tile = rows // 3 if rows % 384 == 0 else rows
    row_block = lambda n: pl.BlockSpec((tile, n), lambda i: (i, 0))
    return pl.pallas_call(
        functools.partial(
            front_kernel, total_rows=total_rows, qkv_n=qkv_n, part_rows=part_rows
        ),
        grid=(rows // tile,),
        in_specs=[
            SMEM_SPEC,
            row_block(width),
            whole_spec(maps.shape),
            whole_spec(stats.shape),
            whole_spec(bn_params.shape),
            whole_spec(qo_all.shape),
            whole_spec(vis_full.shape),
            whole_spec(bias_rows.shape),
        ],
        out_specs=[
            row_block(width),
            row_block(width),
            row_block(3 * width),
            whole_spec((width, 3 * width)),
            whole_spec((width, width)),
            row_block(channels),
            row_block(channels),
        ],
        out_shape=[
            struct((rows, width), f32),
            struct((rows, width), bf16),
            struct((rows, 3 * width), bf16),
            struct((width, 3 * width), bf16),
            struct((width, width), bf16),
            struct((rows, channels), bf16),
            struct((rows, channels), f32),
        ],
        name="front",
    )(lengths, hidden, maps, stats, bn_params, qo_all, vis_full, bias_rows)


def pair_mask(shape, h):
    lane = lax.broadcasted_iota(jnp.int32, shape, len(shape) - 1)
    return (lane >= HDIM) if h else (lane < HDIM)


def attend_kernel(q_ref, k_ref, v_ref, bias_ref, ctx_ref, probs_ref):
    queries = q_ref[...].astype(f32) * (HDIM**-0.5)
    context = None
    for h in range(2):
        mask = pair_mask(queries.shape, h)
        query_h = jnp.where(mask, queries, 0.0).astype(bf16)
        scores = dot_nt(query_h, k_ref[...]) + bias_ref[h]
        exps = jnp.exp(scores - jnp.max(scores, axis=-1, keepdims=True))
        probs = (exps * (1.0 / jnp.sum(exps, axis=-1, keepdims=True))).astype(bf16)
        probs_ref[h] = probs
        piece = dot_nn(probs, v_ref[...])
        context = piece if context is None else jnp.where(mask, piece, context)
    ctx_ref[...] = context.astype(bf16)


def attend(projected, bias, rows, width):
    pairs = width // LANES
    tile = rows // 3
    return pl.pallas_call(
        attend_kernel,
        grid=(pairs, rows // tile),
        in_specs=[
            pl.BlockSpec((tile, LANES), lambda p, i: (i, p)),
            pl.BlockSpec((rows, LANES), lambda p, i: (0, pairs + p)),
            pl.BlockSpec((rows, LANES), lambda p, i: (0, 2 * pairs + p)),
            pl.BlockSpec((2, tile, rows), lambda p, i: (p, i, 0)),
        ],
        out_specs=[
            pl.BlockSpec((tile, LANES), lambda p, i: (i, p)),
            pl.BlockSpec((2, tile, rows), lambda p, i: (p, i, 0)),
        ],
        out_shape=[struct((rows, width), bf16), struct((HEADS, rows, rows), bf16)],
        name="attend",
    )(projected, projected, projected, bias)


def attend_back_kernel(q_ref, k_ref, v_ref, ctx_ref, gctx_ref, probs_ref, dq_ref, dk_ref, dv_ref, gs_ref):
    rows = q_ref.shape[0]
    tile = rows // 3
    scale = HDIM**-0.5
    keys_h = []
    for h in range(2):
        mask = pair_mask(k_ref.shape, h)
        keys_h.append(jnp.where(mask, k_ref[...].astype(f32), 0.0).astype(bf16))
    grad_k = None
    grad_v = None
    for i in range(rows // tile):
        place = slice(i * tile, (i + 1) * tile)
        queries = q_ref[place, :].astype(f32) * scale
        grads = gctx_ref[place, :].astype(f32)
        inner = grads * ctx_ref[place, :].astype(f32)
        grad_q = None
        for h in range(2):
            mask = pair_mask(queries.shape, h)
            query_h = jnp.where(mask, queries, 0.0).astype(bf16)
            grad_h = jnp.where(mask, grads, 0.0).astype(bf16)
            total = jnp.sum(jnp.where(mask, inner, 0.0), axis=-1, keepdims=True)
            grad_probs = dot_nt(grad_h, v_ref[...])
            probs = probs_ref[h, place, :]
            grad_scores = (probs.astype(f32) * (grad_probs - total)).astype(bf16)
            gs_ref[h, place, :] = grad_scores
            piece_q = dot_nn(grad_scores, keys_h[h])
            piece_k = dot_tn(grad_scores, query_h)
            piece_v = dot_tn(probs, grad_h)
            grad_q = piece_q if grad_q is None else grad_q + piece_q
            grad_k = piece_k if grad_k is None else grad_k + piece_k
            grad_v = piece_v if grad_v is None else grad_v + piece_v
        dq_ref[place, :] = (grad_q * scale).astype(bf16)
    dk_ref[...] = grad_k.astype(bf16)
    dv_ref[...] = grad_v.astype(bf16)


def attend_back(projected, context, grad_context, probs, first_pair, pair_count):
    rows, width = context.shape
    pairs = width // LANES
    column = lambda shift: pl.BlockSpec((rows, LANES), lambda p: (0, shift + first_pair + p))
    plain = pl.BlockSpec((rows, LANES), lambda p: (0, p))
    n = pair_count
    return pl.pallas_call(
        attend_back_kernel,
        grid=(n,),
        in_specs=[
            column(0),
            column(pairs),
            column(2 * pairs),
            column(0),
            column(0),
            pl.BlockSpec((2, rows, rows), lambda p: (first_pair + p, 0, 0)),
        ],
        out_specs=[plain, plain, plain, pl.BlockSpec((2, rows, rows), lambda p: (p, 0, 0))],
        out_shape=[
            struct((rows, n * LANES), bf16),
            struct((rows, n * LANES), bf16),
            struct((rows, n * LANES), bf16),
            struct((2 * n, rows, rows), bf16),
        ],
        name="attend_back",
    )(projected, projected, projected, context, grad_context, probs)


def table_thetas():
    limits = list(EDGES2) + [1 - edge for edge in EDGES2]
    limits = limits + [5000] * (REL2 - len(limits))
    return np.asarray(limits + limits, np.int32)[None, :]


def table_mix():
    count = len(EDGES2)
    mix = np.zeros((2 * REL2, 2 * REL2), np.float32)
    for side in range(2):
        base = side * REL2
        every = base + 2 * count
        above = lambda m: base + m - 1
        below = lambda m: base + count + m - 1
        for m in range(1, count + 1):
            mix[above(m), base + REL2 // 2 + m] -= 1.0
            if m < count:
                mix[above(m + 1), base + REL2 // 2 + m] += 1.0
            else:
                mix[every, base + REL2 // 2 + m] += 1.0
            mix[below(m), base + m] += 1.0
            if m < count:
                mix[below(m + 1), base + m] -= 1.0
        mix[above(1), base] += 1.0
        mix[below(1), base] -= 1.0
    return mix


def table_plan_kernel(xs_ref, ys_ref, theta_ref, order_ref, spot_ref):
    rows = xs_ref.shape[1]
    chunks = rows // LANES
    lane = lax.broadcasted_iota(jnp.int32, (LANES, LANES), 1)
    sub = lax.broadcasted_iota(jnp.int32, (LANES, LANES), 0)
    wide = 8 * LANES
    for side, line_ref in enumerate((xs_ref, ys_ref)):
        line = line_ref[...]
        below = jnp.zeros((1, wide), f32)
        for c in range(chunks):
            column = column_of(line[:, c * LANES : (c + 1) * LANES])
            rank = jnp.zeros((LANES, 1), f32)
            for e in range(chunks):
                other = line[:, e * LANES : (e + 1) * LANES]
                earlier = (other < column) | (
                    (other == column) & (lane + e * LANES < sub + c * LANES)
                )
                rank = rank + jnp.sum(earlier.astype(f32), axis=1, keepdims=True)
            level = lax.broadcasted_iota(jnp.int32, (LANES, rows), 1).astype(f32)
            order_ref[c * LANES : (c + 1) * LANES, side * rows : (side + 1) * rows] = (
                (rank <= level).astype(f32).astype(bf16)
            )
            steps = lax.broadcasted_iota(jnp.int32, (LANES, wide), 1)
            wide_column = jnp.concatenate([column] * 8, axis=1)
            below = below + jnp.sum((wide_column < steps).astype(f32), axis=0, keepdims=True)
        below_i = below.astype(jnp.int32)
        for c in range(chunks):
            column = column_of(line[:, c * LANES : (c + 1) * LANES])
            limit = jnp.clip(column + theta_ref[...], 0, wide - 1)
            found = jnp.zeros((LANES, LANES), jnp.int32)
            for e in range(8):
                piece = jnp.broadcast_to(below_i[:, e * LANES : (e + 1) * LANES], (LANES, LANES))
                got = jnp.take_along_axis(piece, limit & (LANES - 1), axis=1)
                found = jnp.where((limit >> 7) == e, got, found)
            place = slice(c * LANES, (c + 1) * LANES)
            if side == 0:
                spot_ref[place, :] = found - 1
            else:
                spot_ref[place, :] = jnp.where(lane < REL2, spot_ref[place, :], found - 1)


def table_plan(box_x, box_y):
    rows = box_x.shape[1]
    thetas = jnp.asarray(table_thetas())
    return pl.pallas_call(
        table_plan_kernel,
        grid=(1,),
        in_specs=[whole_spec((1, rows)), whole_spec((1, rows)), whole_spec((1, LANES))],
        out_specs=[whole_spec((rows, 2 * rows)), whole_spec((rows, LANES))],
        out_shape=[struct((rows, 2 * rows), bf16), struct((rows, LANES), jnp.int32)],
        name="table_plan",
    )(box_x, box_y, thetas)


def table_kernel(order_ref, spot_ref, gs_ref, xy_ref, diag_ref):
    rows = gs_ref.shape[1]
    chunks = rows // LANES
    lane = lax.broadcasted_iota(jnp.int32, (LANES, LANES), 1)
    sub = lax.broadcasted_iota(jnp.int32, (LANES, LANES), 0)
    flip = (lane + sub == LANES - 1).astype(f32).astype(bf16)
    total = jnp.zeros((8, LANES), f32)
    diag_ref[...] = jnp.zeros(diag_ref.shape, f32)
    pad = jnp.zeros((LANES, LANES), f32)
    for c in range(chunks):
        place = slice(c * LANES, (c + 1) * LANES)
        grads = gs_ref[0, place, :]
        prefix = dot_nn(grads, order_ref[...])
        spot = spot_ref[place, :]
        low = spot & (LANES - 1)
        high = spot >> 7
        found = jnp.zeros((LANES, LANES), f32)
        for e in range(chunks):
            got_x = jnp.take_along_axis(prefix[:, e * LANES : (e + 1) * LANES], low, axis=1)
            got_y = jnp.take_along_axis(
                prefix[:, rows + e * LANES : rows + (e + 1) * LANES], low, axis=1
            )
            found = jnp.where(high == e, jnp.where(lane < REL2, got_x, got_y), found)
        total = total + jnp.sum(found.reshape(LANES // 8, 8, LANES), axis=0)
        turned = jnp.concatenate([dot_nn(flip, grads), pad], axis=1)
        turned = pltpu.roll(turned, 0, 1, stride=1, stride_axis=0)
        lined = jnp.sum(turned.reshape(LANES // 8, 8, rows + LANES), axis=0)
        first = rows - LANES - c * LANES
        diag_ref[0, :, first : first + rows + LANES] += lined
    xy_ref[0] = total


def table_sums(order, spot, grad_scores, first, heads):
    rows = grad_scores.shape[1]
    return pl.pallas_call(
        table_kernel,
        grid=(heads,),
        in_specs=[
            whole_spec(order.shape),
            whole_spec(spot.shape),
            pl.BlockSpec((1, rows, rows), lambda h: (first + h, 0, 0)),
        ],
        out_specs=[
            pl.BlockSpec((1, 8, LANES), lambda h: (h, 0, 0)),
            pl.BlockSpec((1, 8, 2 * rows), lambda h: (h, 0, 0)),
        ],
        out_shape=[struct((heads, 8, LANES), f32), struct((heads, 8, 2 * rows), f32)],
        name="table_sums",
    )(order, spot, grad_scores)


def table_gradient(xy, diag):
    rows = diag.shape[2] // 2
    sums_xy = jnp.sum(xy, axis=1)
    sums_diag = jnp.sum(diag, axis=1)
    delta = lax.broadcasted_iota(jnp.int32, (2 * rows, REL1), 0) - (rows - 1)
    hot = (
        bucket_index(delta, REL1, EDGES1)
        == lax.broadcasted_iota(jnp.int32, (2 * rows, REL1), 1)
    ).astype(f32)
    exact = functools.partial(
        jnp.dot, precision=lax.Precision.HIGHEST, preferred_element_type=f32
    )
    return jnp.concatenate(
        [exact(sums_diag, hot), exact(sums_xy, jnp.asarray(table_mix()))], axis=1
    )


def row_mean(values):
    return jnp.mean(values, axis=-1, keepdims=True)


def after_kernel(ctx_ref, mixed_ref, wout_ref, bias_ref, norm_ref, first_ref, hat_ref, inv_ref):
    values = mixed_ref[...] + dot_nn(ctx_ref[...], wout_ref[...]) + bias_ref[3:4, :]
    centred = values - row_mean(values)
    inverse = lax.rsqrt(row_mean(centred * centred) + layer_eps)
    hat = centred * inverse
    hat_ref[...] = hat
    inv_ref[...] = inverse
    first_ref[...] = (hat * norm_ref[0:1, :] + norm_ref[1:2, :]).astype(bf16)


def after_attention(context, mixed, w_out, bias_rows, norm_params):
    rows, width = mixed.shape
    tile = rows // 3
    row_block = lambda n: pl.BlockSpec((tile, n), lambda i: (i, 0))
    return pl.pallas_call(
        after_kernel,
        grid=(rows // tile,),
        in_specs=[
            row_block(width),
            row_block(width),
            whole_spec(w_out.shape),
            whole_spec(bias_rows.shape),
            whole_spec(norm_params.shape),
        ],
        out_specs=[row_block(width), row_block(width), row_block(1)],
        out_shape=[
            struct((rows, width), bf16),
            struct((rows, width), f32),
            struct((rows, 1), f32),
        ],
        name="after_attention",
    )(context, mixed, w_out, bias_rows, norm_params)


def joined(ref, width):
    columns = ref.shape[-1]
    return jnp.concatenate([ref[g, :, 0].reshape(width, columns) for g in range(2)], axis=1)


def ffn_kernel(
    lens_ref,
    first_ref,
    up_ref,
    down_ref,
    ubias_ref,
    hat_ref,
    cot_ref,
    norm_ref,
    bias_ref,
    act_ref,
    slope_ref,
    out_ref,
    g2_ref,
    g2b_ref,
    red_ref,
    acc_ref,
):
    step = pl.program_id(0)
    rows, width = first_ref.shape
    block_n = up_ref.shape[-1]
    pre = dot_nn(first_ref[...], joined(up_ref, width)) + ubias_ref[0]
    cdf = 0.5 + 0.5 * lax.erf(pre * (2.0**-0.5))
    act = (pre * cdf).astype(bf16)
    act_ref[0] = act
    slope_ref[0] = (cdf + pre * (jnp.exp(-0.5 * pre * pre) * ((2.0 * math.pi) ** -0.5))).astype(
        bf16
    )
    piece = dot_nt(act, joined(down_ref, width))

    @pl.when(step == 0)
    def _():
        acc_ref[...] = piece

    @pl.when(step > 0)
    def _():
        acc_ref[...] += piece

    @pl.when(step == pl.num_programs(0) - 1)
    def _():
        ends = doc_ends(lens_ref)
        tile = LANES
        red_ref[...] = jnp.zeros(red_ref.shape, f32)

        def one_tile(i, carry):
            place = pl.ds(pl.multiple_of(i * tile, tile), tile)
            values = (
                hat_ref[place, :] * norm_ref[0:1, :]
                + norm_ref[1:2, :]
                + acc_ref[place, :]
                + bias_ref[4:5, :]
            )
            centred = values - row_mean(values)
            inverse = lax.rsqrt(row_mean(centred * centred) + layer_eps)
            hat = centred * inverse
            out_ref[place, :] = (hat * norm_ref[2:3, :] + norm_ref[3:4, :]).astype(bf16)
            row = lax.broadcasted_iota(jnp.int32, (tile, width), 0) + i * tile
            grad = jnp.where(row < ends[-1], cot_ref[place, :].astype(f32), 0.0)
            scaled = grad * norm_ref[2:3, :]
            g2 = inverse * (scaled - row_mean(scaled) - hat * row_mean(scaled * hat))
            g2_ref[place, :] = g2
            g2b_ref[place, :] = g2.astype(bf16)
            red_ref[0:1, :] += jnp.sum(grad * hat, axis=0, keepdims=True)
            red_ref[1:2, :] += jnp.sum(grad, axis=0, keepdims=True)
            red_ref[2:3, :] += jnp.sum(g2, axis=0, keepdims=True)
            return carry

        lax.fori_loop(0, rows // tile, one_tile, 0)


def ffn(lengths, first_b, ud_all, up_bias, hat1, cotangent, norm_params, bias_rows):
    rows, width = first_b.shape
    parts, dp_parts, _, part_rows, block_n = ud_all.shape
    weight = lambda which: pl.BlockSpec(
        (2, dp_parts, 1, part_rows, block_n), lambda t: (t, 0, which, 0, 0)
    )
    block = pl.BlockSpec((1, rows, 2 * block_n), lambda t: (t, 0, 0))
    return pl.pallas_call(
        ffn_kernel,
        grid=(parts // 2,),
        in_specs=[
            SMEM_SPEC,
            whole_spec(first_b.shape),
            weight(0),
            weight(1),
            pl.BlockSpec((1, 1, 2 * block_n), lambda t: (t, 0, 0)),
            whole_spec(hat1.shape),
            whole_spec(cotangent.shape),
            whole_spec(norm_params.shape),
            whole_spec(bias_rows.shape),
        ],
        out_specs=[
            block,
            block,
            whole_spec((rows, width)),
            whole_spec((rows, width)),
            whole_spec((rows, width)),
            whole_spec((8, width)),
        ],
        out_shape=[
            struct((parts // 2, rows, 2 * block_n), bf16),
            struct((parts // 2, rows, 2 * block_n), bf16),
            struct((rows, width), bf16),
            struct((rows, width), f32),
            struct((rows, width), bf16),
            struct((8, width), f32),
        ],
        scratch_shapes=[pltpu.VMEM((rows, width), f32)],
        name="ffn",
    )(lengths, first_b, ud_all, ud_all, up_bias, hat1, cotangent, norm_params, bias_rows)


def ffn_back_kernel(
    me_ref,
    first_ref,
    g2b_ref,
    up_ref,
    down_ref,
    act_ref,
    slope_ref,
    g2_ref,
    hat_ref,
    inv_ref,
    norm_ref,
    keep_ref,
    send_ref,
    ub_ref,
    g1_ref,
    g1b_ref,
    red_ref,
    acc_ref,
    first_t_ref,
    g2_t_ref,
    grad_ref,
):
    step = pl.program_id(0)
    rows, width = first_ref.shape
    _, dp_parts, _, part_rows, block_n = up_ref.shape
    mine = me_ref[1]

    @pl.when(step == 0)
    def _():
        first_t_ref[...] = jnp.transpose(first_ref[...])
        g2_t_ref[...] = jnp.transpose(g2b_ref[...])

    grad_act = dot_nn(g2b_ref[...], joined(down_ref, width))
    grad_pre = (slope_ref[0].astype(f32) * grad_act).astype(bf16)
    ub_ref[0] = jnp.sum(grad_pre.astype(f32), axis=0, keepdims=True)
    grad_ref[0] = dot_nn(first_t_ref[...], grad_pre).astype(bf16)
    grad_ref[1] = dot_nn(g2_t_ref[...], act_ref[0]).astype(bf16)
    for slot in range(dp_parts):
        place = pl.ds(pl.multiple_of((mine ^ slot) * part_rows, 16), part_rows)
        target = send_ref if slot % 2 else keep_ref
        for which in range(2):
            for g in range(2):
                target[(me_ref[0] & 1) ^ g, slot // 2, which] = grad_ref[
                    which, place, g * block_n : (g + 1) * block_n
                ]
    piece = dot_nt(grad_pre, joined(up_ref, width))

    @pl.when(step == 0)
    def _():
        acc_ref[...] = piece

    @pl.when(step > 0)
    def _():
        acc_ref[...] += piece

    @pl.when(step == pl.num_programs(0) - 1)
    def _():
        tile = LANES
        red_ref[...] = jnp.zeros(red_ref.shape, f32)

        def one_tile(i, carry):
            place = pl.ds(pl.multiple_of(i * tile, tile), tile)
            grad = g2_ref[place, :] + acc_ref[place, :]
            hat = hat_ref[place, :]
            scaled = grad * norm_ref[0:1, :]
            g1 = inv_ref[place, :] * (
                scaled - row_mean(scaled) - hat * row_mean(scaled * hat)
            )
            g1b = g1.astype(bf16)
            g1_ref[place, :] = g1
            g1b_ref[place, :] = g1b
            red_ref[0:1, :] += jnp.sum(grad * hat, axis=0, keepdims=True)
            red_ref[1:2, :] += jnp.sum(grad, axis=0, keepdims=True)
            red_ref[2:3, :] += jnp.sum(g1b.astype(f32), axis=0, keepdims=True)
            return carry

        lax.fori_loop(0, rows // tile, one_tile, 0)


def ffn_back(me, first_b, g2b, ud_all, act, slope, g2, hat1, inv1, norm_params):
    rows, width = first_b.shape
    parts, dp_parts, _, part_rows, block_n = ud_all.shape
    weight = lambda which: pl.BlockSpec(
        (2, dp_parts, 1, part_rows, block_n), lambda t, me: (t, 0, which, 0, 0)
    )
    block = pl.BlockSpec((1, rows, 2 * block_n), lambda t, me: (t, 0, 0))
    half = pl.BlockSpec(
        (2, dp_parts // 2, 2, part_rows, block_n), lambda t, me: (t ^ (me[0] >> 1), 0, 0, 0, 0)
    )
    half_shape = struct((parts, dp_parts // 2, 2, part_rows, block_n), bf16)
    return pl.pallas_call(
        ffn_back_kernel,
        grid_spec=pltpu.PrefetchScalarGridSpec(
            num_scalar_prefetch=1,
            grid=(parts // 2,),
            in_specs=[
                whole_spec(first_b.shape),
                whole_spec(g2b.shape),
                weight(0),
                weight(1),
                block,
                block,
                whole_spec(g2.shape),
                whole_spec(hat1.shape),
                whole_spec(inv1.shape),
                whole_spec(norm_params.shape),
            ],
            out_specs=[
                half,
                half,
                pl.BlockSpec((1, 1, 2 * block_n), lambda t, me: (t, 0, 0)),
                whole_spec((rows, width)),
                whole_spec((rows, width)),
                whole_spec((8, width)),
            ],
            scratch_shapes=[
                pltpu.VMEM((rows, width), f32),
                pltpu.VMEM((width, rows), bf16),
                pltpu.VMEM((width, rows), bf16),
                pltpu.VMEM((2, width, 2 * block_n), bf16),
            ],
        ),
        out_shape=[
            half_shape,
            half_shape,
            struct((parts // 2, 1, 2 * block_n), f32),
            struct((rows, width), f32),
            struct((rows, width), bf16),
            struct((8, width), f32),
        ],
        name="ffn_back",
    )(me, first_b, g2b, ud_all, ud_all, act, slope, g2, hat1, inv1, norm_params)


def qkv_grad_kernel(me_ref, mixed_ref, ctx_ref, g1b_ref, dq_ref, dk_ref, dv_ref, dq2_ref, dk2_ref, dv2_ref, keep_ref, send_ref, gq_ref, go_ref, *, qkv_n, part_rows):
    width = mixed_ref.shape[1]
    parts = keep_ref.shape[0]
    block_n = keep_ref.shape[-1]
    out_n = block_n - qkv_n
    mixed_t = jnp.transpose(mixed_ref[...])
    for part, refs in enumerate(((dq_ref, dq2_ref), (dk_ref, dk2_ref), (dv_ref, dv2_ref))):
        right = jnp.concatenate([ref[...] for ref in refs], axis=1)
        gq_ref[:, part * width : (part + 1) * width] = dot_nn(mixed_t, right).astype(bf16)
    go_ref[...] = dot_tn(ctx_ref[...], g1b_ref[...]).astype(bf16)
    my_t = me_ref[0]
    my_d = me_ref[1]

    def one_half(s, carry):
        for core, target in ((0, keep_ref), (1, send_ref)):
            place = pl.ds(pl.multiple_of((my_d ^ (2 * s + core)) * part_rows, 16), part_rows)
            for t in range(parts):
                slot = my_t ^ t
                target[slot, s, :, :qkv_n] = gq_ref[place, t * qkv_n : (t + 1) * qkv_n]
                target[slot, s, :, qkv_n:] = go_ref[place, t * out_n : (t + 1) * out_n]
        return carry

    lax.fori_loop(0, keep_ref.shape[1], one_half, 0)


def qkv_gradient(me, mixed_b, context, g1b, heads, parts, dp_parts, qkv_n, block_n):
    rows, width = mixed_b.shape
    part_rows = width // dp_parts
    half = (parts, dp_parts // 2, part_rows, block_n)
    return pl.pallas_call(
        functools.partial(qkv_grad_kernel, qkv_n=qkv_n, part_rows=part_rows),
        grid=(1,),
        in_specs=[SMEM_SPEC] + [whole_spec((rows, width))] * 3 + [whole_spec((rows, width // 2))] * 6,
        out_specs=[whole_spec(half), whole_spec(half)],
        out_shape=[struct(half, bf16), struct(half, bf16)],
        scratch_shapes=[pltpu.VMEM((width, 3 * width), bf16), pltpu.VMEM((width, width), bf16)],
        name="qkv_gradient",
    )(me, mixed_b, context, g1b, *heads)


def tail_kernel(
    lens_ref,
    me_ref,
    dq_ref,
    dk_ref,
    dv_ref,
    dq2_ref,
    dk2_ref,
    dv2_ref,
    wqkv_ref,
    g1_ref,
    vis_ref,
    normed_ref,
    hat_ref,
    grad_ref,
    keep_ref,
    send_ref,
    red_ref,
    bn_ref,
    vgrad_ref,
    *,
    vis_n,
    groups,
):
    step = pl.program_id(0)
    tile, width = g1_ref.shape
    ends = doc_ends(lens_ref)
    grad = g1_ref[...]
    heads = [
        jnp.concatenate([a[...], b[...]], axis=1)
        for a, b in ((dq_ref, dq2_ref), (dk_ref, dk2_ref), (dv_ref, dv2_ref))
    ]
    for part, left in enumerate(heads):
        grad = grad + dot_nt(left, wqkv_ref[:, part * width : (part + 1) * width])
    grad_ref[...] = grad
    rows = lax.broadcasted_iota(jnp.int32, (tile, width), 0) + step * tile
    grad_b = jnp.where(visual_mask(rows, ends), grad, 0.0).astype(bf16)

    @pl.when(step == 0)
    def _():
        red_ref[...] = jnp.zeros(red_ref.shape, f32)
        bn_ref[...] = jnp.zeros(bn_ref.shape, f32)
        vgrad_ref[...] = jnp.zeros(vgrad_ref.shape, f32)

    vgrad_ref[...] += dot_tn(normed_ref[...], grad_b)
    back = dot_nt(grad_b, vis_ref[...])
    bn_ref[0:1, :] += jnp.sum(back * hat_ref[...], axis=0, keepdims=True)
    bn_ref[1:2, :] += jnp.sum(back, axis=0, keepdims=True)
    red_ref[0:1, :] += jnp.sum(grad_b.astype(f32), axis=0, keepdims=True)
    red_ref[1:2, :] += jnp.sum(heads[0].astype(f32), axis=0, keepdims=True)
    red_ref[2:3, :] += jnp.sum(heads[2].astype(f32), axis=0, keepdims=True)

    @pl.when(step == pl.num_programs(0) - 1)
    def _():
        parts, halves, group_rows, _ = keep_ref.shape
        my_t = me_ref[0]
        my_d = me_ref[1]
        part_rows = group_rows * groups

        def one_half(s, carry):
            for core, target in ((0, keep_ref), (1, send_ref)):
                first = (my_d ^ (2 * s + core)) * part_rows
                for g in range(groups):
                    place = pl.ds(pl.multiple_of(first + g * group_rows, 8), group_rows)
                    for t in range(parts):
                        target[my_t ^ t, s, :, g * vis_n : (g + 1) * vis_n] = vgrad_ref[
                            place, t * vis_n : (t + 1) * vis_n
                        ].astype(bf16)
            return carry

        lax.fori_loop(0, halves, one_half, 0)


def tail(lengths, me, heads, w_qkv, g1, vis_full, normed, hat_v, parts, dp_parts, block_n):
    rows, width = g1.shape
    channels = normed.shape[1]
    tile = rows // 3
    vis_n = width // parts
    groups = block_n // vis_n
    group_rows = channels // dp_parts // groups
    half = (parts, dp_parts // 2, group_rows, block_n)
    row_block = lambda n: pl.BlockSpec((tile, n), lambda i: (i, 0))
    return pl.pallas_call(
        functools.partial(tail_kernel, vis_n=vis_n, groups=groups),
        grid=(rows // tile,),
        in_specs=[
            SMEM_SPEC,
            SMEM_SPEC,
            *([row_block(width // 2)] * 6),
            whole_spec(w_qkv.shape),
            row_block(width),
            whole_spec(vis_full.shape),
            row_block(channels),
            row_block(channels),
        ],
        out_specs=[
            row_block(width),
            whole_spec(half),
            whole_spec(half),
            whole_spec((8, width)),
            whole_spec((8, channels)),
        ],
        out_shape=[
            struct((rows, width), f32),
            struct(half, bf16),
            struct(half, bf16),
            struct((8, width), f32),
            struct((8, channels), f32),
        ],
        scratch_shapes=[pltpu.VMEM((channels, width), f32)],
        name="tail",
    )(lengths, me, *heads, w_qkv, g1, vis_full, normed, hat_v)


def axis_bits(name, first=0):
    return [(name, bit) for bit in range(first, (lax.axis_size(name) - 1).bit_length())]


def flip_permute(values, axis_bit):
    name, bit = axis_bit
    return lax.ppermute(
        values, name, [(i, i ^ (1 << bit)) for i in range(lax.axis_size(name))]
    )


def butterfly_orders():
    bits = axis_bits("dp", 1) + axis_bits("tensor")
    rest, last = bits[:-1], bits[-1:]
    return [rest[shift:] + rest[:shift] + last for shift in range(3)]


class Butterfly:
    def __init__(self, keep, received, order):
        tensor_bits = (lax.axis_size("tensor") - 1).bit_length()
        dp_bits = (lax.axis_size("dp") - 1).bit_length() - 1
        dims = [2] * (tensor_bits + dp_bits) + list(keep.shape[2:])
        self.names = [("tensor", b) for b in reversed(range(tensor_bits))] + [
            ("dp", b) for b in reversed(range(1, dp_bits + 1))
        ]
        self.keep = keep.reshape(dims)
        self.received = received.reshape(dims)
        self.order = list(order)

    def total(self):
        return self.keep.astype(f32) + self.received.astype(f32)

    def sends(self):
        self.axis_bit = self.order.pop(0)
        place = self.names.index(self.axis_bit)
        self.names.pop(place)
        total = self.total().astype(bf16)
        self.keep = lax.index_in_dim(total, 0, place, keepdims=False)
        return lax.index_in_dim(total, 1, place, keepdims=False)


def beside(sums, work, anchor, extra=()):
    sending = [one.sends() for one in sums] + [value for value, _ in extra]
    bits = [one.axis_bit for one in sums] + [bit for _, bit in extra]
    sending, anchor = lax.optimization_barrier((sending, anchor))
    arrived = [flip_permute(value, bit) for value, bit in zip(sending, bits)]
    result = work(anchor)
    arrived, result = lax.optimization_barrier((arrived, result))
    for one, value in zip(sums, arrived):
        one.received = value
    return result, arrived[len(sums) :]


def spread(values):
    count = lax.axis_size("dp") * lax.axis_size("tensor")
    copies = jnp.broadcast_to(values[None], (count,) + values.shape)
    return lax.all_to_all(copies, ("dp", "tensor"), 0, 0, tiled=True)


def lamb_direction(weight, moments, gradient):
    first_moment = beta_first * moments[0] + (1.0 - beta_first) * gradient
    second_moment = beta_second * moments[1] + (1.0 - beta_second) * gradient * gradient
    direction = (
        first_moment
        / (1.0 - beta_first**STEP)
        / (jnp.sqrt(second_moment / (1.0 - beta_second**STEP)) + adam_eps)
        + weight_decay * weight
    )
    return (jnp.stack([first_moment, second_moment]), direction)


def shards(
    hidden_in,
    visual_maps,
    lengths,
    box_x,
    box_y,
    cotangent,
    vis_weight,
    vis_moments,
    qkv_weight,
    qkv_moments,
    out_weight,
    out_moments,
    up_weight,
    up_moments,
    down_weight,
    down_moments,
    up_bias,
    up_bias_moments,
    bn_params,
    bn_moments,
    norm_params,
    norm_moments,
    bias_rows,
    bias_moments,
    rel_tables,
    table_moments,
):
    rows, width = hidden_in.shape
    channels = visual_maps.shape[1]
    dp_parts = lax.axis_size("dp")
    parts = lax.axis_size("tensor")
    device_total = dp_parts * parts
    part_rows, qkv_n = qkv_weight.shape
    out_n = out_weight.shape[1]
    block_n = qkv_n + out_n
    vis_rows, vis_n = vis_weight.shape
    groups = block_n // vis_n
    group_rows = vis_rows // groups
    me = jnp.stack([lax.axis_index("tensor"), lax.axis_index("dp")]).astype(jnp.int32)
    box_x = box_x.reshape(1, rows)
    box_y = box_y.reshape(1, rows)

    vis_b = vis_weight.astype(bf16)
    qo_shard = jnp.concatenate(
        [
            jnp.concatenate([qkv_weight.astype(bf16), out_weight.astype(bf16)], axis=1),
            jnp.concatenate(
                [vis_b[g * group_rows : (g + 1) * group_rows] for g in range(groups)], axis=1
            ),
        ],
        axis=0,
    )
    qo_all = lax.all_gather(qo_shard, ("tensor", "dp"), axis=0, tiled=False).reshape(
        parts, dp_parts, part_rows + group_rows, block_n
    )
    ud_shard = jnp.stack([up_weight.astype(bf16), down_weight.astype(bf16).T])
    ud_all = lax.all_gather(ud_shard, ("tensor", "dp"), axis=0, tiled=False).reshape(
        parts, dp_parts, 2, part_rows, block_n
    )
    vis_full = (
        qo_all[:, :, part_rows:, :]
        .reshape(parts, dp_parts, group_rows, groups, vis_n)
        .transpose(1, 3, 2, 0, 4)
        .reshape(channels, width)
    )

    visual_value = visual_maps.astype(f32)
    sums = jnp.stack([jnp.sum(visual_value, axis=0), jnp.sum(visual_value * visual_value, axis=0)])
    stats = jnp.sum(spread(sums), axis=0)

    bias = relative_bias(lengths, box_x, box_y, rel_tables)
    order, spot = table_plan(box_x, box_y)
    mixed, mixed_b, projected, w_qkv, w_out, normed, hat_v = front(
        lengths,
        hidden_in,
        visual_maps,
        stats,
        bn_params,
        qo_all,
        vis_full,
        bias_rows,
        float(visual_maps.shape[0] * device_total),
        qkv_n,
        part_rows,
    )
    context, probs = attend(projected, bias, rows, width)
    first_b, hat1, inv1 = after_attention(context, mixed, w_out, bias_rows, norm_params)
    act, slope, block_out, g2, g2b, red2 = ffn(
        lengths,
        first_b,
        ud_all,
        up_bias.reshape(parts // 2, 1, 2 * block_n),
        hat1,
        cotangent,
        norm_params,
        bias_rows,
    )
    keep_ud, send_ud, up_bias_part, g1, g1b, red1 = ffn_back(
        me, first_b, g2b, ud_all, act, slope, g2, hat1, inv1, norm_params
    )
    core = ("dp", 0)
    orders = butterfly_orders()
    flat = lambda v: v.reshape(parts, dp_parts // 2, 2 * part_rows, block_n)

    def thirds(keep, received):
        count = keep.shape[2] // 3
        return [
            Butterfly(
                keep[:, :, c * count : (c + 1) * count],
                received[:, :, c * count : (c + 1) * count],
                orders[c],
            )
            for c in range(3)
        ]

    pairs = width // LANES
    grad_context, (received_ud,) = beside(
        [], lambda g: dot_nt(g, w_out).astype(bf16), g1b, [(send_ud, core)]
    )
    ud_sums = thirds(flat(keep_ud), flat(received_ud))
    back_a, _ = beside(
        ud_sums,
        lambda g: attend_back(projected, context, g, probs, 0, pairs // 2),
        grad_context,
    )
    back_b, _ = beside(
        ud_sums,
        lambda g: attend_back(projected, context, g, probs, pairs // 2, pairs // 2),
        grad_context,
    )
    heads = tuple(back_a[:3]) + tuple(back_b[:3])
    (keep_qo, send_qo), _ = beside(
        ud_sums,
        lambda h: qkv_gradient(
            me, mixed_b, context, g1b, h, parts, dp_parts, qkv_n, block_n
        ),
        heads,
    )
    rest = ud_sums if ud_sums[0].order else []
    (grad_mixed, keep_v, send_v, red3, red_bn), (received_qo,) = beside(
        rest,
        lambda h: tail(
            lengths, me, h, w_qkv, g1, vis_full, normed, hat_v, parts, dp_parts, block_n
        ),
        heads,
        [(send_qo, core)],
    )
    qo_sums = thirds(keep_qo, received_qo)
    table_parts = []
    vis_sums = []
    for part in range(4):
        source, first = ((back_a, back_b)[part // 2][3], (part % 2) * 3)
        extra = [(send_v, core)] if part == 0 else []
        sums = [one for one in ud_sums + qo_sums + vis_sums if one.order]
        made, got = beside(
            sums, lambda g: table_sums(order, spot, g, first, 3), source, extra
        )
        if part == 0:
            vis_sums = [Butterfly(keep_v, got[0], orders[1])]
        table_parts.append(made)
    while any(one.order for one in ud_sums + qo_sums + vis_sums):
        sums = [one for one in ud_sums + qo_sums + vis_sums if one.order]
        for one in sums:
            one.received = flip_permute(one.sends(), one.axis_bit)
    table_part = table_gradient(
        jnp.concatenate([made[0] for made in table_parts]),
        jnp.concatenate([made[1] for made in table_parts]),
    )
    ud_grad = jnp.concatenate([one.total() for one in ud_sums], axis=0)
    up_shard = ud_grad[:part_rows]
    down_shard = ud_grad[part_rows:].T
    qo_grad = jnp.concatenate([one.total() for one in qo_sums], axis=0)
    qkv_shard, out_shard = qo_grad[:, :qkv_n], qo_grad[:, qkv_n:]
    vis_piece = vis_sums[0].total()
    vis_shard = jnp.concatenate(
        [vis_piece[:, g * vis_n : (g + 1) * vis_n] for g in range(groups)], axis=0
    )

    small = [
        up_bias_part.reshape(-1),
        red_bn[0:2].reshape(-1),
        jnp.concatenate([red1[0:2], red2[0:2]]).reshape(-1),
        jnp.concatenate([red3[0:3], red1[2:3], red2[2:3]]).reshape(-1),
        table_part.reshape(-1),
    ]
    small_shapes = [
        up_bias.shape,
        bn_params.shape,
        norm_params.shape,
        bias_rows.shape,
        rel_tables.shape,
    ]
    sizes = [piece.shape[0] for piece in small]
    piece_n = -(-sum(sizes) // device_total)
    padding = jnp.zeros((piece_n * device_total - sum(sizes),), f32)
    packed = jnp.concatenate(small + [padding]).reshape(device_total, piece_n)
    own_piece = jnp.sum(
        lax.all_to_all(packed, ("dp", "tensor"), 0, 0, tiled=True), axis=0
    )

    sharded = [
        (vis_weight, vis_moments, vis_shard),
        (qkv_weight, qkv_moments, qkv_shard),
        (out_weight, out_moments, out_shard),
        (up_weight, up_moments, up_shard),
        (down_weight, down_moments, down_shard),
    ]
    sharded_updates = [lamb_direction(triple[0], triple[1], triple[2]) for triple in sharded]
    local_sums = jnp.stack(
        [jnp.sum(triple[0] * triple[0]) for triple in sharded]
        + [jnp.sum(update[1] * update[1]) for update in sharded_updates]
    )
    shared = spread(jnp.concatenate([own_piece, local_sums]))
    totals = shared[:, :piece_n].reshape(-1)
    global_sums = jnp.sum(shared[:, piece_n:], axis=0).reshape(2, 5)
    small_grads = []
    start = 0
    for size, shape in zip(sizes, small_shapes):
        small_grads.append(totals[start : start + size].reshape(shape))
        start += size
    whole = [
        (up_bias, up_bias_moments, small_grads[0]),
        (bn_params, bn_moments, small_grads[1]),
        (norm_params, norm_moments, small_grads[2]),
        (bias_rows, bias_moments, small_grads[3]),
        (rel_tables, table_moments, small_grads[4]),
    ]
    whole_updates = [lamb_direction(triple[0], triple[1], triple[2]) for triple in whole]
    whole_sums = jnp.stack(
        [
            jnp.stack([jnp.sum(triple[0] * triple[0]) for triple in whole]),
            jnp.stack([jnp.sum(update[1] * update[1]) for update in whole_updates]),
        ]
    )
    all_sums = jnp.concatenate([global_sums, whole_sums], axis=1)
    weight_norms = jnp.sqrt(all_sums[0])
    update_norms = jnp.sqrt(all_sums[1])
    trust_ratio = weight_norms / update_norms
    lamb_norms = jnp.stack([weight_norms, update_norms, trust_ratio])
    outputs = [block_out, grad_mixed, lamb_norms]
    triples = sharded + whole
    updates = sharded_updates + whole_updates
    for number in range(10):
        new_weight = triples[number][0] - learn_rate * trust_ratio[number] * updates[number][1]
        outputs.extend(
            [triples[number][2], new_weight, updates[number][0], new_weight.astype(bf16)]
        )
    return tuple(outputs)


def solution(mesh):
    in_specs = (
        P(("dp", "tensor"), None),
        P(("dp", "tensor"), None),
        P(("dp", "tensor"), None),
        P(("dp", "tensor")),
        P(("dp", "tensor")),
        P(("dp", "tensor"), None),
        P("dp", "tensor"),
        P(None, "dp", "tensor"),
        P("dp", "tensor"),
        P(None, "dp", "tensor"),
        P("dp", "tensor"),
        P(None, "dp", "tensor"),
        P("dp", "tensor"),
        P(None, "dp", "tensor"),
        P("tensor", "dp"),
        P(None, "tensor", "dp"),
        P(),
        P(),
        P(),
        P(),
        P(),
        P(),
        P(),
        P(),
        P(),
        P(),
    )
    out_specs = (
        P(("dp", "tensor"), None),
        P(("dp", "tensor"), None),
        P(),
        P("dp", "tensor"),
        P("dp", "tensor"),
        P(None, "dp", "tensor"),
        P("dp", "tensor"),
        P("dp", "tensor"),
        P("dp", "tensor"),
        P(None, "dp", "tensor"),
        P("dp", "tensor"),
        P("dp", "tensor"),
        P("dp", "tensor"),
        P(None, "dp", "tensor"),
        P("dp", "tensor"),
        P("dp", "tensor"),
        P("dp", "tensor"),
        P(None, "dp", "tensor"),
        P("dp", "tensor"),
        P("tensor", "dp"),
        P("tensor", "dp"),
        P(None, "tensor", "dp"),
        P("tensor", "dp"),
        P(),
        P(),
        P(),
        P(),
        P(),
        P(),
        P(),
        P(),
        P(),
        P(),
        P(),
        P(),
        P(),
        P(),
        P(),
        P(),
        P(),
        P(),
        P(),
        P(),
    )
    return jax.shard_map(shards, mesh=mesh, in_specs=in_specs, out_specs=out_specs, check_vma=False)
```

```python
import functools
import math

import jax
import jax.numpy as jnp
import numpy as np
from jax import lax
from jax.experimental import pallas as pl
from jax.experimental.pallas import tpu as pltpu
from jax.sharding import PartitionSpec as P

HEADS = 12
HDIM = 64
PATCHES = 49
REL1 = 32
REL2 = 64
DIST1 = 128
DIST2 = 256
STEP = 10
LANES = 128

layer_eps = 1e-06
batch_eps = 1e-05
beta_first = 0.9
beta_second = 0.999
adam_eps = 1e-06
weight_decay = 0.01
learn_rate = 0.4
masked_score = -1000000000.0
f32 = jnp.float32
bf16 = jnp.bfloat16
SMEM_SPEC = pl.BlockSpec(memory_space=pltpu.SMEM)


def dot_nn(left, right):
    return lax.dot_general(left, right, (((1,), (0,)), ((), ())), preferred_element_type=f32)


def dot_nt(left, right):
    return lax.dot_general(left, right, (((1,), (1,)), ((), ())), preferred_element_type=f32)


def dot_tn(left, right):
    return lax.dot_general(left, right, (((0,), (0,)), ((), ())), preferred_element_type=f32)


def whole_spec(shape):
    zeros = (0,) * len(shape)
    return pl.BlockSpec(tuple(shape), lambda *_: zeros)


def struct(shape, dtype):
    return jax.ShapeDtypeStruct(tuple(shape), dtype)


def bucket_edges(bucket_count, max_distance):
    half = bucket_count // 2
    exact = half // 2
    edges = []
    for level in range(1, half):
        if level < exact:
            edges.append(level)
        else:
            found = max_distance
            for distance in range(exact, max_distance + 1):
                if (
                    exact
                    + int(
                        math.log(distance / exact) / math.log(max_distance / exact) * (half - exact)
                    )
                    >= level
                ):
                    found = distance
                    break
            edges.append(found)
    return edges


EDGES1 = bucket_edges(REL1, DIST1)
EDGES2 = bucket_edges(REL2, DIST2)


def bucket_index(delta, bucket_count, edges):
    half = bucket_count // 2
    exact = half // 2
    distance = jnp.abs(delta)
    level = jnp.minimum(distance, exact)
    for edge in edges[exact:]:
        level = level + (distance >= edge).astype(jnp.int32)
    return jnp.where(delta > 0, half, 0) + level


def doc_ends(lens_ref):
    ends = []
    total = None
    for k in range(lens_ref.shape[1]):
        total = lens_ref[0, k] if total is None else total + lens_ref[0, k]
        ends.append(total)
    return ends


def doc_of(rows, ends):
    found = jnp.zeros(rows.shape, jnp.int32)
    for end in ends:
        found = found + (rows >= end).astype(jnp.int32)
    return found


def visual_mask(rows, ends):
    hit = None
    for end in ends:
        inside = (rows >= end - PATCHES) & (rows < end)
        hit = inside if hit is None else hit | inside
    return hit


def column_of(row_block):
    return jnp.transpose(jnp.broadcast_to(row_block, (LANES, LANES)))


def bias_kernel(
    lens_ref, xs_ref, ys_ref, xt_ref, yt_ref, tab_ref, out_ref, near_ref, x_ref, y_ref
):
    tile = out_ref.shape[1]
    cols_total = out_ref.shape[2]
    ends = doc_ends(lens_ref)
    step = pl.program_id(0)
    table = tab_ref[...]
    table_lin = jnp.concatenate(
        [table[:, :REL1], jnp.zeros((HEADS, LANES - REL1), f32)], axis=1
    )
    table_xy = table[:, REL1:]
    lanes = lax.broadcasted_iota(jnp.int32, (8, LANES), 1)
    subs = lax.broadcasted_iota(jnp.int32, (8, LANES), 0)

    def lookup(flat, h, index):
        return jnp.take_along_axis(
            jnp.broadcast_to(flat[h : h + 1, :], (8, LANES)), index, axis=1
        )

    @pl.when(step == 0)
    def _():
        def one_group(g, carry):
            place = pl.ds(pl.multiple_of(g * 8, 8), 8)
            for o in range(3):
                delta = lanes + (o - 1) * LANES - subs - g * 8
                lin = bucket_index(delta, REL1, EDGES1)
                for h in range(HEADS):
                    near_ref[h, o, place, :] = lookup(table_lin, h, lin)
            return carry

        lax.fori_loop(0, tile // 8, one_group, 0)

    x_ref[...] = column_of(xt_ref[...])
    y_ref[...] = column_of(yt_ref[...])
    far = [
        [jnp.broadcast_to(table[h : h + 1, b : b + 1], (8, LANES)) for h in range(HEADS)]
        for b in (REL1 // 2 - 1, REL1 - 1)
    ]

    def one_group(g, carry):
        place = pl.ds(pl.multiple_of(g * 8, 8), 8)
        row_doc = doc_of(subs + (step * tile + g * 8), ends)
        x_col = x_ref[place, :]
        y_col = y_ref[place, :]
        for c in range(cols_total // LANES):
            piece = slice(c * LANES, (c + 1) * LANES)
            across = bucket_index(xs_ref[:, piece] - x_col, REL2, EDGES2)
            down = bucket_index(ys_ref[:, piece] - y_col, REL2, EDGES2) + REL2
            same = row_doc == doc_of(lanes + c * LANES, ends)
            offset = jnp.clip(c - step, -1, 1) + 1
            close = jnp.abs(c - step) <= 1
            got_x = [lookup(table_xy, h, across) for h in range(HEADS)]
            got_y = [lookup(table_xy, h, down) for h in range(HEADS)]
            for h in range(HEADS):
                beyond = jnp.where(c > step, far[1][h], far[0][h])
                lin = jnp.where(close, near_ref[h, offset, place, :], beyond)
                out_ref[h, place, piece] = jnp.where(
                    same, got_x[h] + got_y[h] + lin, masked_score
                )
        return carry

    lax.fori_loop(0, tile // 8, one_group, 0)


def relative_bias(lengths, box_x, box_y, tables):
    rows = box_x.shape[1]
    tile = LANES
    row_spec = pl.BlockSpec((1, tile), lambda i: (0, i))
    return pl.pallas_call(
        bias_kernel,
        grid=(rows // tile,),
        in_specs=[
            SMEM_SPEC,
            whole_spec((1, rows)),
            whole_spec((1, rows)),
            row_spec,
            row_spec,
            whole_spec(tables.shape),
        ],
        out_specs=pl.BlockSpec((HEADS, tile, rows), lambda i: (0, i, 0)),
        out_shape=struct((HEADS, rows, rows), f32),
        scratch_shapes=[
            pltpu.VMEM((HEADS, 3, tile, LANES), f32),
            pltpu.VMEM((tile, LANES), jnp.int32),
            pltpu.VMEM((tile, LANES), jnp.int32),
        ],
        name="relative_bias",
    )(lengths, box_x, box_y, box_x, box_y, tables)


def front_kernel(
    lens_ref,
    hidden_ref,
    maps_ref,
    stats_ref,
    bn_ref,
    qo_ref,
    vis_ref,
    bias_ref,
    mixed_ref,
    mixed_b_ref,
    proj_ref,
    wqkv_ref,
    wout_ref,
    normed_ref,
    hat_ref,
    *,
    total_rows,
    qkv_n,
    part_rows,
):
    tile = hidden_ref.shape[0]
    width = hidden_ref.shape[1]
    parts, dp_parts, _, block_n = qo_ref.shape
    out_n = block_n - qkv_n

    @pl.when(pl.program_id(0) == 0)
    def _():
        def one_part(d, carry):
            place = pl.ds(pl.multiple_of(d * part_rows, 16), part_rows)
            for t in range(parts):
                block = qo_ref[t, d, :part_rows, :]
                wqkv_ref[place, t * qkv_n : (t + 1) * qkv_n] = block[:, :qkv_n]
                wout_ref[place, t * out_n : (t + 1) * out_n] = block[:, qkv_n:]
            return carry

        lax.fori_loop(0, dp_parts, one_part, 0)

    ends = doc_ends(lens_ref)
    start = pl.program_id(0) * tile
    visual_total, channels = maps_ref.shape
    rows = lax.broadcasted_iota(jnp.int32, (tile, visual_total), 0) + start
    slots = lax.broadcasted_iota(jnp.int32, (tile, visual_total), 1)
    target = slots
    for k, end in enumerate(ends):
        target = jnp.where(slots >= k * PATCHES, slots - (k + 1) * PATCHES + end, target)
    select = (rows == target).astype(f32).astype(bf16)
    picked = dot_nn(select, maps_ref[...])
    is_visual = visual_mask(
        lax.broadcasted_iota(jnp.int32, (tile, channels), 0) + start, ends
    )
    mean = stats_ref[0:1, :] / total_rows
    var = stats_ref[1:2, :] / total_rows - mean * mean
    hat = (picked - mean) * lax.rsqrt(var + batch_eps)
    hat = jnp.where(is_visual, hat, 0.0)
    hat_ref[...] = hat
    normed = jnp.where(is_visual, hat * bn_ref[0:1, :] + bn_ref[1:2, :], 0.0).astype(bf16)
    normed_ref[...] = normed
    embedded = dot_nn(normed, vis_ref[...]) + bias_ref[0:1, :]
    row_visual = visual_mask(lax.broadcasted_iota(jnp.int32, (tile, width), 0) + start, ends)
    mixed = hidden_ref[...].astype(f32) + jnp.where(row_visual, embedded, 0.0)
    mixed_ref[...] = mixed
    mixed_b = mixed.astype(bf16)
    mixed_b_ref[...] = mixed_b
    for part in range(3):
        columns = slice(part * width, (part + 1) * width)
        piece = dot_nn(mixed_b, wqkv_ref[:, columns])
        if part == 0:
            piece = piece + bias_ref[1:2, :]
        if part == 2:
            piece = piece + bias_ref[2:3, :]
        proj_ref[:, columns] = piece.astype(bf16)


def front(lengths, hidden, maps, stats, bn_params, qo_all, vis_full, bias_rows, total_rows, qkv_n, part_rows):
    rows, width = hidden.shape
    channels = maps.shape[1]
    tile = rows // 3 if rows % 384 == 0 else rows
    row_block = lambda n: pl.BlockSpec((tile, n), lambda i: (i, 0))
    return pl.pallas_call(
        functools.partial(
            front_kernel, total_rows=total_rows, qkv_n=qkv_n, part_rows=part_rows
        ),
        grid=(rows // tile,),
        in_specs=[
            SMEM_SPEC,
            row_block(width),
            whole_spec(maps.shape),
            whole_spec(stats.shape),
            whole_spec(bn_params.shape),
            whole_spec(qo_all.shape),
            whole_spec(vis_full.shape),
            whole_spec(bias_rows.shape),
        ],
        out_specs=[
            row_block(width),
            row_block(width),
            row_block(3 * width),
            whole_spec((width, 3 * width)),
            whole_spec((width, width)),
            row_block(channels),
            row_block(channels),
        ],
        out_shape=[
            struct((rows, width), f32),
            struct((rows, width), bf16),
            struct((rows, 3 * width), bf16),
            struct((width, 3 * width), bf16),
            struct((width, width), bf16),
            struct((rows, channels), bf16),
            struct((rows, channels), f32),
        ],
        name="front",
    )(lengths, hidden, maps, stats, bn_params, qo_all, vis_full, bias_rows)


def pair_mask(shape, h):
    lane = lax.broadcasted_iota(jnp.int32, shape, len(shape) - 1)
    return (lane >= HDIM) if h else (lane < HDIM)


def attend_kernel(q_ref, k_ref, v_ref, bias_ref, ctx_ref, probs_ref):
    queries = q_ref[...].astype(f32) * (HDIM**-0.5)
    context = None
    for h in range(2):
        mask = pair_mask(queries.shape, h)
        query_h = jnp.where(mask, queries, 0.0).astype(bf16)
        scores = dot_nt(query_h, k_ref[...]) + bias_ref[h]
        exps = jnp.exp(scores - jnp.max(scores, axis=-1, keepdims=True))
        probs = (exps * (1.0 / jnp.sum(exps, axis=-1, keepdims=True))).astype(bf16)
        probs_ref[h] = probs
        piece = dot_nn(probs, v_ref[...])
        context = piece if context is None else jnp.where(mask, piece, context)
    ctx_ref[...] = context.astype(bf16)


def attend(projected, bias, rows, width):
    pairs = width // LANES
    tile = rows // 3
    return pl.pallas_call(
        attend_kernel,
        grid=(pairs, rows // tile),
        in_specs=[
            pl.BlockSpec((tile, LANES), lambda p, i: (i, p)),
            pl.BlockSpec((rows, LANES), lambda p, i: (0, pairs + p)),
            pl.BlockSpec((rows, LANES), lambda p, i: (0, 2 * pairs + p)),
            pl.BlockSpec((2, tile, rows), lambda p, i: (p, i, 0)),
        ],
        out_specs=[
            pl.BlockSpec((tile, LANES), lambda p, i: (i, p)),
            pl.BlockSpec((2, tile, rows), lambda p, i: (p, i, 0)),
        ],
        out_shape=[struct((rows, width), bf16), struct((HEADS, rows, rows), bf16)],
        name="attend",
    )(projected, projected, projected, bias)


def attend_back_kernel(q_ref, k_ref, v_ref, ctx_ref, gctx_ref, probs_ref, dq_ref, dk_ref, dv_ref, gs_ref):
    rows = q_ref.shape[0]
    tile = rows // 3
    scale = HDIM**-0.5
    keys_h = []
    for h in range(2):
        mask = pair_mask(k_ref.shape, h)
        keys_h.append(jnp.where(mask, k_ref[...].astype(f32), 0.0).astype(bf16))
    grad_k = None
    grad_v = None
    for i in range(rows // tile):
        place = slice(i * tile, (i + 1) * tile)
        queries = q_ref[place, :].astype(f32) * scale
        grads = gctx_ref[place, :].astype(f32)
        inner = grads * ctx_ref[place, :].astype(f32)
        grad_q = None
        for h in range(2):
            mask = pair_mask(queries.shape, h)
            query_h = jnp.where(mask, queries, 0.0).astype(bf16)
            grad_h = jnp.where(mask, grads, 0.0).astype(bf16)
            total = jnp.sum(jnp.where(mask, inner, 0.0), axis=-1, keepdims=True)
            grad_probs = dot_nt(grad_h, v_ref[...])
            probs = probs_ref[h, place, :]
            grad_scores = (probs.astype(f32) * (grad_probs - total)).astype(bf16)
            gs_ref[h, place, :] = grad_scores
            piece_q = dot_nn(grad_scores, keys_h[h])
            piece_k = dot_tn(grad_scores, query_h)
            piece_v = dot_tn(probs, grad_h)
            grad_q = piece_q if grad_q is None else grad_q + piece_q
            grad_k = piece_k if grad_k is None else grad_k + piece_k
            grad_v = piece_v if grad_v is None else grad_v + piece_v
        dq_ref[place, :] = (grad_q * scale).astype(bf16)
    dk_ref[...] = grad_k.astype(bf16)
    dv_ref[...] = grad_v.astype(bf16)


def attend_back(projected, context, grad_context, probs, first_pair, pair_count):
    rows, width = context.shape
    pairs = width // LANES
    column = lambda shift: pl.BlockSpec((rows, LANES), lambda p: (0, shift + first_pair + p))
    plain = pl.BlockSpec((rows, LANES), lambda p: (0, p))
    n = pair_count
    return pl.pallas_call(
        attend_back_kernel,
        grid=(n,),
        in_specs=[
            column(0),
            column(pairs),
            column(2 * pairs),
            column(0),
            column(0),
            pl.BlockSpec((2, rows, rows), lambda p: (first_pair + p, 0, 0)),
        ],
        out_specs=[plain, plain, plain, pl.BlockSpec((2, rows, rows), lambda p: (p, 0, 0))],
        out_shape=[
            struct((rows, n * LANES), bf16),
            struct((rows, n * LANES), bf16),
            struct((rows, n * LANES), bf16),
            struct((2 * n, rows, rows), bf16),
        ],
        name="attend_back",
    )(projected, projected, projected, context, grad_context, probs)


def table_thetas():
    limits = list(EDGES2) + [1 - edge for edge in EDGES2]
    limits = limits + [5000] * (REL2 - len(limits))
    return np.asarray(limits + limits, np.int32)[None, :]


def table_mix():
    count = len(EDGES2)
    mix = np.zeros((2 * REL2, 2 * REL2), np.float32)
    for side in range(2):
        base = side * REL2
        every = base + 2 * count
        above = lambda m: base + m - 1
        below = lambda m: base + count + m - 1
        for m in range(1, count + 1):
            mix[above(m), base + REL2 // 2 + m] -= 1.0
            if m < count:
                mix[above(m + 1), base + REL2 // 2 + m] += 1.0
            else:
                mix[every, base + REL2 // 2 + m] += 1.0
            mix[below(m), base + m] += 1.0
            if m < count:
                mix[below(m + 1), base + m] -= 1.0
        mix[above(1), base] += 1.0
        mix[below(1), base] -= 1.0
    return mix


def table_plan_kernel(xs_ref, ys_ref, theta_ref, order_ref, spot_ref):
    rows = xs_ref.shape[1]
    chunks = rows // LANES
    lane = lax.broadcasted_iota(jnp.int32, (LANES, LANES), 1)
    sub = lax.broadcasted_iota(jnp.int32, (LANES, LANES), 0)
    wide = 8 * LANES
    for side, line_ref in enumerate((xs_ref, ys_ref)):
        line = line_ref[...]
        below = jnp.zeros((1, wide), f32)
        for c in range(chunks):
            column = column_of(line[:, c * LANES : (c + 1) * LANES])
            rank = jnp.zeros((LANES, 1), f32)
            for e in range(chunks):
                other = line[:, e * LANES : (e + 1) * LANES]
                earlier = (other < column) | (
                    (other == column) & (lane + e * LANES < sub + c * LANES)
                )
                rank = rank + jnp.sum(earlier.astype(f32), axis=1, keepdims=True)
            level = lax.broadcasted_iota(jnp.int32, (LANES, rows), 1).astype(f32)
            order_ref[c * LANES : (c + 1) * LANES, side * rows : (side + 1) * rows] = (
                (rank <= level).astype(f32).astype(bf16)
            )
            steps = lax.broadcasted_iota(jnp.int32, (LANES, wide), 1)
            wide_column = jnp.concatenate([column] * 8, axis=1)
            below = below + jnp.sum((wide_column < steps).astype(f32), axis=0, keepdims=True)
        below_i = below.astype(jnp.int32)
        for c in range(chunks):
            column = column_of(line[:, c * LANES : (c + 1) * LANES])
            limit = jnp.clip(column + theta_ref[...], 0, wide - 1)
            found = jnp.zeros((LANES, LANES), jnp.int32)
            for e in range(8):
                piece = jnp.broadcast_to(below_i[:, e * LANES : (e + 1) * LANES], (LANES, LANES))
                got = jnp.take_along_axis(piece, limit & (LANES - 1), axis=1)
                found = jnp.where((limit >> 7) == e, got, found)
            place = slice(c * LANES, (c + 1) * LANES)
            if side == 0:
                spot_ref[place, :] = found - 1
            else:
                spot_ref[place, :] = jnp.where(lane < REL2, spot_ref[place, :], found - 1)


def table_plan(box_x, box_y):
    rows = box_x.shape[1]
    thetas = jnp.asarray(table_thetas())
    return pl.pallas_call(
        table_plan_kernel,
        grid=(1,),
        in_specs=[whole_spec((1, rows)), whole_spec((1, rows)), whole_spec((1, LANES))],
        out_specs=[whole_spec((rows, 2 * rows)), whole_spec((rows, LANES))],
        out_shape=[struct((rows, 2 * rows), bf16), struct((rows, LANES), jnp.int32)],
        name="table_plan",
    )(box_x, box_y, thetas)


def table_kernel(order_ref, spot_ref, gs_ref, xy_ref, diag_ref, *prefix_refs):
    rows = gs_ref.shape[1]
    chunks = rows // LANES
    lane8 = lax.broadcasted_iota(jnp.int32, (8, LANES), 1)
    lane = lax.broadcasted_iota(jnp.int32, (LANES, LANES), 1)
    sub = lax.broadcasted_iota(jnp.int32, (LANES, LANES), 0)
    flip = (lane + sub == LANES - 1).astype(f32).astype(bf16)
    pad = jnp.zeros((LANES, LANES), f32)
    zero = jnp.zeros((8, LANES), f32)
    total = zero
    near = jnp.zeros((8, 4 * LANES), f32)
    far = [zero, zero]
    for c in range(chunks):
        prefix_refs[c][...] = dot_nn(gs_ref[0, c * LANES : (c + 1) * LANES, :], order_ref[...])
    for c in range(chunks):
        for g in range(LANES // 8):
            here = slice(g * 8, g * 8 + 8)
            spot = spot_ref[c * LANES + g * 8 : c * LANES + g * 8 + 8, :]
            low = spot & (LANES - 1)
            high = spot >> 7
            found = zero
            for e in range(chunks):
                got_x, got_y = [
                    jnp.take_along_axis(
                        prefix_refs[c][here, side + e * LANES : side + (e + 1) * LANES], low, axis=1
                    )
                    for side in (0, rows)
                ]
                found = jnp.where(high == e, jnp.where(lane8 < REL2, got_x, got_y), found)
            total = total + found
        place = slice(c * LANES, (c + 1) * LANES)
        left, right = max(c - 1, 0), min(c + 2, chunks)
        turned = [dot_nn(flip, gs_ref[0, place, left * LANES : right * LANES])]
        if c == 0:
            turned = [pad] + turned
        if right == c + 1:
            turned = turned + [pad]
        turned = pltpu.roll(
            jnp.concatenate(turned + [pad], axis=1), 0, 1, stride=1, stride_axis=0
        )
        near = near + jnp.sum(turned.reshape(LANES // 8, 8, 4 * LANES), axis=0)
        for e in range(chunks):
            if abs(e - c) > 1:
                piece = gs_ref[0, place, e * LANES : (e + 1) * LANES].astype(f32)
                far[e > c] = far[e > c] + jnp.sum(piece.reshape(LANES // 8, 8, LANES), axis=0)
    xy_ref[0] = total
    diag_ref[...] = jnp.zeros(diag_ref.shape, f32)
    diag_ref[0, :, rows - 2 * LANES : rows + 2 * LANES] = near
    diag_ref[0, :, :LANES] += far[0]
    diag_ref[0, :, 2 * rows - LANES :] += far[1]


def table_sums(order, spot, grad_scores, first, heads):
    rows = grad_scores.shape[1]
    return pl.pallas_call(
        table_kernel,
        grid=(heads,),
        in_specs=[
            whole_spec(order.shape),
            whole_spec(spot.shape),
            pl.BlockSpec((1, rows, rows), lambda h: (first + h, 0, 0)),
        ],
        out_specs=[
            pl.BlockSpec((1, 8, LANES), lambda h: (h, 0, 0)),
            pl.BlockSpec((1, 8, 2 * rows), lambda h: (h, 0, 0)),
        ],
        out_shape=[struct((heads, 8, LANES), f32), struct((heads, 8, 2 * rows), f32)],
        scratch_shapes=[pltpu.VMEM((LANES, 2 * rows), f32)] * (rows // LANES),
        name="table_sums",
    )(order, spot, grad_scores)


def table_gradient(xy, diag):
    rows = diag.shape[2] // 2
    sums_xy = jnp.sum(xy, axis=1)
    sums_diag = jnp.sum(diag, axis=1)
    delta = lax.broadcasted_iota(jnp.int32, (2 * rows, REL1), 0) - (rows - 1)
    hot = (
        bucket_index(delta, REL1, EDGES1)
        == lax.broadcasted_iota(jnp.int32, (2 * rows, REL1), 1)
    ).astype(f32)
    exact = functools.partial(
        jnp.dot, precision=lax.Precision.HIGHEST, preferred_element_type=f32
    )
    return jnp.concatenate(
        [exact(sums_diag, hot), exact(sums_xy, jnp.asarray(table_mix()))], axis=1
    )


def row_mean(values):
    return jnp.mean(values, axis=-1, keepdims=True)


def after_kernel(ctx_ref, mixed_ref, wout_ref, bias_ref, norm_ref, first_ref, hat_ref, inv_ref):
    values = mixed_ref[...] + dot_nn(ctx_ref[...], wout_ref[...]) + bias_ref[3:4, :]
    centred = values - row_mean(values)
    inverse = lax.rsqrt(row_mean(centred * centred) + layer_eps)
    hat = centred * inverse
    hat_ref[...] = hat
    inv_ref[...] = inverse
    first_ref[...] = (hat * norm_ref[0:1, :] + norm_ref[1:2, :]).astype(bf16)


def after_attention(context, mixed, w_out, bias_rows, norm_params):
    rows, width = mixed.shape
    tile = rows // 3
    row_block = lambda n: pl.BlockSpec((tile, n), lambda i: (i, 0))
    return pl.pallas_call(
        after_kernel,
        grid=(rows // tile,),
        in_specs=[
            row_block(width),
            row_block(width),
            whole_spec(w_out.shape),
            whole_spec(bias_rows.shape),
            whole_spec(norm_params.shape),
        ],
        out_specs=[row_block(width), row_block(width), row_block(1)],
        out_shape=[
            struct((rows, width), bf16),
            struct((rows, width), f32),
            struct((rows, 1), f32),
        ],
        name="after_attention",
    )(context, mixed, w_out, bias_rows, norm_params)


def joined(ref, width):
    columns = ref.shape[-1]
    return jnp.concatenate([ref[g, :, 0].reshape(width, columns) for g in range(2)], axis=1)


def ffn_kernel(
    lens_ref,
    first_ref,
    up_ref,
    down_ref,
    ubias_ref,
    hat_ref,
    cot_ref,
    norm_ref,
    bias_ref,
    act_ref,
    slope_ref,
    out_ref,
    g2_ref,
    g2b_ref,
    red_ref,
    acc_ref,
):
    step = pl.program_id(0)
    rows, width = first_ref.shape
    block_n = up_ref.shape[-1]
    pre = dot_nn(first_ref[...], joined(up_ref, width)) + ubias_ref[0]
    cdf = 0.5 + 0.5 * lax.erf(pre * (2.0**-0.5))
    act = (pre * cdf).astype(bf16)
    act_ref[0] = act
    slope_ref[0] = (cdf + pre * (jnp.exp(-0.5 * pre * pre) * ((2.0 * math.pi) ** -0.5))).astype(
        bf16
    )
    piece = dot_nt(act, joined(down_ref, width))

    @pl.when(step == 0)
    def _():
        acc_ref[...] = piece

    @pl.when(step > 0)
    def _():
        acc_ref[...] += piece

    @pl.when(step == pl.num_programs(0) - 1)
    def _():
        ends = doc_ends(lens_ref)
        tile = LANES
        red_ref[...] = jnp.zeros(red_ref.shape, f32)

        def one_tile(i, carry):
            place = pl.ds(pl.multiple_of(i * tile, tile), tile)
            values = (
                hat_ref[place, :] * norm_ref[0:1, :]
                + norm_ref[1:2, :]
                + acc_ref[place, :]
                + bias_ref[4:5, :]
            )
            centred = values - row_mean(values)
            inverse = lax.rsqrt(row_mean(centred * centred) + layer_eps)
            hat = centred * inverse
            out_ref[place, :] = (hat * norm_ref[2:3, :] + norm_ref[3:4, :]).astype(bf16)
            row = lax.broadcasted_iota(jnp.int32, (tile, width), 0) + i * tile
            grad = jnp.where(row < ends[-1], cot_ref[place, :].astype(f32), 0.0)
            scaled = grad * norm_ref[2:3, :]
            g2 = inverse * (scaled - row_mean(scaled) - hat * row_mean(scaled * hat))
            g2_ref[place, :] = g2
            g2b_ref[place, :] = g2.astype(bf16)
            red_ref[0:1, :] += jnp.sum(grad * hat, axis=0, keepdims=True)
            red_ref[1:2, :] += jnp.sum(grad, axis=0, keepdims=True)
            red_ref[2:3, :] += jnp.sum(g2, axis=0, keepdims=True)
            return carry

        lax.fori_loop(0, rows // tile, one_tile, 0)


def ffn(lengths, first_b, ud_all, up_bias, hat1, cotangent, norm_params, bias_rows):
    rows, width = first_b.shape
    parts, dp_parts, _, part_rows, block_n = ud_all.shape
    weight = lambda which: pl.BlockSpec(
        (2, dp_parts, 1, part_rows, block_n), lambda t: (t, 0, which, 0, 0)
    )
    block = pl.BlockSpec((1, rows, 2 * block_n), lambda t: (t, 0, 0))
    return pl.pallas_call(
        ffn_kernel,
        grid=(parts // 2,),
        in_specs=[
            SMEM_SPEC,
            whole_spec(first_b.shape),
            weight(0),
            weight(1),
            pl.BlockSpec((1, 1, 2 * block_n), lambda t: (t, 0, 0)),
            whole_spec(hat1.shape),
            whole_spec(cotangent.shape),
            whole_spec(norm_params.shape),
            whole_spec(bias_rows.shape),
        ],
        out_specs=[
            block,
            block,
            whole_spec((rows, width)),
            whole_spec((rows, width)),
            whole_spec((rows, width)),
            whole_spec((8, width)),
        ],
        out_shape=[
            struct((parts // 2, rows, 2 * block_n), bf16),
            struct((parts // 2, rows, 2 * block_n), bf16),
            struct((rows, width), bf16),
            struct((rows, width), f32),
            struct((rows, width), bf16),
            struct((8, width), f32),
        ],
        scratch_shapes=[pltpu.VMEM((rows, width), f32)],
        name="ffn",
    )(lengths, first_b, ud_all, ud_all, up_bias, hat1, cotangent, norm_params, bias_rows)


def ffn_back_kernel(
    me_ref,
    first_ref,
    g2b_ref,
    up_ref,
    down_ref,
    act_ref,
    slope_ref,
    g2_ref,
    hat_ref,
    inv_ref,
    norm_ref,
    keep_ref,
    send_ref,
    ub_ref,
    g1_ref,
    g1b_ref,
    red_ref,
    acc_ref,
    first_t_ref,
    g2_t_ref,
    grad_ref,
):
    step = pl.program_id(0)
    rows, width = first_ref.shape
    _, dp_parts, _, part_rows, block_n = up_ref.shape
    mine = me_ref[1]

    @pl.when(step == 0)
    def _():
        first_t_ref[...] = jnp.transpose(first_ref[...])
        g2_t_ref[...] = jnp.transpose(g2b_ref[...])

    grad_act = dot_nn(g2b_ref[...], joined(down_ref, width))
    grad_pre = (slope_ref[0].astype(f32) * grad_act).astype(bf16)
    ub_ref[0] = jnp.sum(grad_pre.astype(f32), axis=0, keepdims=True)
    grad_ref[0] = dot_nn(first_t_ref[...], grad_pre).astype(bf16)
    grad_ref[1] = dot_nn(g2_t_ref[...], act_ref[0]).astype(bf16)
    for slot in range(dp_parts):
        place = pl.ds(pl.multiple_of((mine ^ slot) * part_rows, 16), part_rows)
        target = send_ref if slot % 2 else keep_ref
        for which in range(2):
            for g in range(2):
                target[(me_ref[0] & 1) ^ g, slot // 2, which] = grad_ref[
                    which, place, g * block_n : (g + 1) * block_n
                ]
    piece = dot_nt(grad_pre, joined(up_ref, width))

    @pl.when(step == 0)
    def _():
        acc_ref[...] = piece

    @pl.when(step > 0)
    def _():
        acc_ref[...] += piece

    @pl.when(step == pl.num_programs(0) - 1)
    def _():
        tile = LANES
        red_ref[...] = jnp.zeros(red_ref.shape, f32)

        def one_tile(i, carry):
            place = pl.ds(pl.multiple_of(i * tile, tile), tile)
            grad = g2_ref[place, :] + acc_ref[place, :]
            hat = hat_ref[place, :]
            scaled = grad * norm_ref[0:1, :]
            g1 = inv_ref[place, :] * (
                scaled - row_mean(scaled) - hat * row_mean(scaled * hat)
            )
            g1b = g1.astype(bf16)
            g1_ref[place, :] = g1
            g1b_ref[place, :] = g1b
            red_ref[0:1, :] += jnp.sum(grad * hat, axis=0, keepdims=True)
            red_ref[1:2, :] += jnp.sum(grad, axis=0, keepdims=True)
            red_ref[2:3, :] += jnp.sum(g1b.astype(f32), axis=0, keepdims=True)
            return carry

        lax.fori_loop(0, rows // tile, one_tile, 0)


def ffn_back(me, first_b, g2b, ud_all, act, slope, g2, hat1, inv1, norm_params):
    rows, width = first_b.shape
    parts, dp_parts, _, part_rows, block_n = ud_all.shape
    weight = lambda which: pl.BlockSpec(
        (2, dp_parts, 1, part_rows, block_n), lambda t, me: (t, 0, which, 0, 0)
    )
    block = pl.BlockSpec((1, rows, 2 * block_n), lambda t, me: (t, 0, 0))
    half = pl.BlockSpec(
        (2, dp_parts // 2, 2, part_rows, block_n), lambda t, me: (t ^ (me[0] >> 1), 0, 0, 0, 0)
    )
    half_shape = struct((parts, dp_parts // 2, 2, part_rows, block_n), bf16)
    return pl.pallas_call(
        ffn_back_kernel,
        grid_spec=pltpu.PrefetchScalarGridSpec(
            num_scalar_prefetch=1,
            grid=(parts // 2,),
            in_specs=[
                whole_spec(first_b.shape),
                whole_spec(g2b.shape),
                weight(0),
                weight(1),
                block,
                block,
                whole_spec(g2.shape),
                whole_spec(hat1.shape),
                whole_spec(inv1.shape),
                whole_spec(norm_params.shape),
            ],
            out_specs=[
                half,
                half,
                pl.BlockSpec((1, 1, 2 * block_n), lambda t, me: (t, 0, 0)),
                whole_spec((rows, width)),
                whole_spec((rows, width)),
                whole_spec((8, width)),
            ],
            scratch_shapes=[
                pltpu.VMEM((rows, width), f32),
                pltpu.VMEM((width, rows), bf16),
                pltpu.VMEM((width, rows), bf16),
                pltpu.VMEM((2, width, 2 * block_n), bf16),
            ],
        ),
        out_shape=[
            half_shape,
            half_shape,
            struct((parts // 2, 1, 2 * block_n), f32),
            struct((rows, width), f32),
            struct((rows, width), bf16),
            struct((8, width), f32),
        ],
        name="ffn_back",
    )(me, first_b, g2b, ud_all, ud_all, act, slope, g2, hat1, inv1, norm_params)


def qkv_grad_kernel(me_ref, mixed_ref, ctx_ref, g1b_ref, dq_ref, dk_ref, dv_ref, dq2_ref, dk2_ref, dv2_ref, vgrad_ref, keep_ref, send_ref, gq_ref, go_ref, *, qkv_n, part_rows, vis_n):
    width = mixed_ref.shape[1]
    parts = keep_ref.shape[0]
    block_n = keep_ref.shape[-1]
    out_n = block_n - qkv_n
    groups = block_n // vis_n
    group_rows = keep_ref.shape[2] - part_rows
    mixed_t = jnp.transpose(mixed_ref[...])
    for part, refs in enumerate(((dq_ref, dq2_ref), (dk_ref, dk2_ref), (dv_ref, dv2_ref))):
        right = jnp.concatenate([ref[...] for ref in refs], axis=1)
        gq_ref[:, part * width : (part + 1) * width] = dot_nn(mixed_t, right).astype(bf16)
    go_ref[...] = dot_tn(ctx_ref[...], g1b_ref[...]).astype(bf16)
    my_t = me_ref[0]
    my_d = me_ref[1]

    def one_half(s, carry):
        for core, target in ((0, keep_ref), (1, send_ref)):
            owner = my_d ^ (2 * s + core)
            place = pl.ds(pl.multiple_of(owner * part_rows, 16), part_rows)
            for t in range(parts):
                slot = my_t ^ t
                target[slot, s, :part_rows, :qkv_n] = gq_ref[place, t * qkv_n : (t + 1) * qkv_n]
                target[slot, s, :part_rows, qkv_n:] = go_ref[place, t * out_n : (t + 1) * out_n]
            for g in range(groups):
                first = owner * (group_rows * groups) + g * group_rows
                place = pl.ds(pl.multiple_of(first, 8), group_rows)
                for t in range(parts):
                    target[my_t ^ t, s, part_rows:, g * vis_n : (g + 1) * vis_n] = vgrad_ref[
                        place, t * vis_n : (t + 1) * vis_n
                    ].astype(bf16)
        return carry

    lax.fori_loop(0, keep_ref.shape[1], one_half, 0)


def qkv_gradient(me, mixed_b, context, g1b, heads, vgrad, parts, dp_parts, qkv_n, block_n):
    rows, width = mixed_b.shape
    part_rows = width // dp_parts
    vis_n = width // parts
    group_rows = vgrad.shape[0] // dp_parts // (block_n // vis_n)
    half = (parts, dp_parts // 2, part_rows + group_rows, block_n)
    return pl.pallas_call(
        functools.partial(qkv_grad_kernel, qkv_n=qkv_n, part_rows=part_rows, vis_n=vis_n),
        grid=(1,),
        in_specs=[SMEM_SPEC]
        + [whole_spec((rows, width))] * 3
        + [whole_spec((rows, width // 2))] * 6
        + [whole_spec(vgrad.shape)],
        out_specs=[whole_spec(half), whole_spec(half)],
        out_shape=[struct(half, bf16), struct(half, bf16)],
        scratch_shapes=[pltpu.VMEM((width, 3 * width), bf16), pltpu.VMEM((width, width), bf16)],
        name="qkv_gradient",
    )(me, mixed_b, context, g1b, *heads, vgrad)


def tail_kernel(
    lens_ref,
    dq_ref,
    dk_ref,
    dv_ref,
    dq2_ref,
    dk2_ref,
    dv2_ref,
    wqkv_ref,
    g1_ref,
    vis_ref,
    normed_ref,
    hat_ref,
    grad_ref,
    vgrad_ref,
    red_ref,
    bn_ref,
):
    step = pl.program_id(0)
    tile, width = g1_ref.shape
    ends = doc_ends(lens_ref)
    grad = g1_ref[...]
    heads = [
        jnp.concatenate([a[...], b[...]], axis=1)
        for a, b in ((dq_ref, dq2_ref), (dk_ref, dk2_ref), (dv_ref, dv2_ref))
    ]
    for part, left in enumerate(heads):
        grad = grad + dot_nt(left, wqkv_ref[:, part * width : (part + 1) * width])
    grad_ref[...] = grad
    rows = lax.broadcasted_iota(jnp.int32, (tile, width), 0) + step * tile
    grad_b = jnp.where(visual_mask(rows, ends), grad, 0.0).astype(bf16)

    @pl.when(step == 0)
    def _():
        red_ref[...] = jnp.zeros(red_ref.shape, f32)
        bn_ref[...] = jnp.zeros(bn_ref.shape, f32)
        vgrad_ref[...] = jnp.zeros(vgrad_ref.shape, f32)

    vgrad_ref[...] += dot_tn(normed_ref[...], grad_b)
    back = dot_nt(grad_b, vis_ref[...])
    bn_ref[0:1, :] += jnp.sum(back * hat_ref[...], axis=0, keepdims=True)
    bn_ref[1:2, :] += jnp.sum(back, axis=0, keepdims=True)
    red_ref[0:1, :] += jnp.sum(grad_b.astype(f32), axis=0, keepdims=True)
    red_ref[1:2, :] += jnp.sum(heads[0].astype(f32), axis=0, keepdims=True)
    red_ref[2:3, :] += jnp.sum(heads[2].astype(f32), axis=0, keepdims=True)


def tail(lengths, heads, w_qkv, g1, vis_full, normed, hat_v):
    rows, width = g1.shape
    channels = normed.shape[1]
    tile = rows // 3
    row_block = lambda n: pl.BlockSpec((tile, n), lambda i: (i, 0))
    return pl.pallas_call(
        tail_kernel,
        grid=(rows // tile,),
        in_specs=[
            SMEM_SPEC,
            *([row_block(width // 2)] * 6),
            whole_spec(w_qkv.shape),
            row_block(width),
            whole_spec(vis_full.shape),
            row_block(channels),
            row_block(channels),
        ],
        out_specs=[
            row_block(width),
            whole_spec((channels, width)),
            whole_spec((8, width)),
            whole_spec((8, channels)),
        ],
        out_shape=[
            struct((rows, width), f32),
            struct((channels, width), f32),
            struct((8, width), f32),
            struct((8, channels), f32),
        ],
        name="tail",
    )(lengths, *heads, w_qkv, g1, vis_full, normed, hat_v)


def axis_bits(name, first=0):
    return [(name, bit) for bit in range(first, (lax.axis_size(name) - 1).bit_length())]


class Reduction:
    def __init__(self, keep, received, cut):
        tensor_bits = axis_bits("tensor")
        dp_bits = axis_bits("dp", 1)
        names = tensor_bits[::-1] + dp_bits[::-1]
        head = dp_bits + tensor_bits[:1]
        self.heads = [head, head[-1:] + head[:-1]]
        self.rest = tensor_bits[1:]
        self.cut = cut
        self.pieces = []
        for place in (slice(0, cut), slice(cut, None)):
            shape = lambda v: v[:, :, place].reshape(
                [2] * len(names) + [v[:, :, place].shape[2], v.shape[3]]
            )
            self.pieces.append([shape(keep), shape(received), list(names)])

    def left(self):
        return len(self.heads[0]) + len(self.rest)

    def split(self, piece, bit):
        keep, received, names = piece
        place = names.index(bit)
        halves = [
            (
                lax.index_in_dim(keep, side, place, keepdims=False).astype(f32)
                + lax.index_in_dim(received, side, place, keepdims=False).astype(f32)
            ).astype(bf16)
            for side in range(2)
        ]
        piece[0] = halves[0]
        piece[2] = names[:place] + names[place + 1 :]
        return halves[1]

    def sends(self):
        if self.heads[0]:
            self.bits = [order[0] for order in self.heads]
            self.heads = [order[1:] for order in self.heads]
            return [self.split(piece, bit) for piece, bit in zip(self.pieces, self.bits)]
        self.bits = self.rest[:1]
        self.rest = self.rest[1:]
        return [jnp.concatenate([self.split(piece, self.bits[0]) for piece in self.pieces], axis=-2)]

    def arrive(self, values):
        self.received = values[0]
        if len(values) == 1:
            values = [values[0][..., : self.cut, :], values[0][..., self.cut :, :]]
        for piece, value in zip(self.pieces, values):
            piece[1] = value


def flip_permute(values, axis_bit):
    name, bit = axis_bit
    return lax.ppermute(
        values, name, [(i, i ^ (1 << bit)) for i in range(lax.axis_size(name))]
    )


def beside(sums, work, anchor, extra=()):
    sums = [one for one in sums if one.left()]
    sent = [one.sends() for one in sums]
    counts = [len(values) for values in sent]
    sending = sum(sent, []) + [value for value, _ in extra]
    bits = sum([one.bits for one in sums], []) + [bit for _, bit in extra]
    sending, anchor = lax.optimization_barrier((sending, anchor))
    arrived = [flip_permute(value, bit) for value, bit in zip(sending, bits)]
    result = work(anchor)
    arrived, result = lax.optimization_barrier((arrived, result))
    for one, count in zip(sums, counts):
        one.arrive(arrived[:count])
        arrived = arrived[count:]
    return result, arrived


def spread(values):
    count = lax.axis_size("dp") * lax.axis_size("tensor")
    copies = jnp.broadcast_to(values[None], (count,) + values.shape)
    return lax.all_to_all(copies, ("dp", "tensor"), 0, 0, tiled=True)


def lamb_direction(weight, first_moment, second_moment, gradient):
    first_moment = beta_first * first_moment + (1.0 - beta_first) * gradient
    second_moment = beta_second * second_moment + (1.0 - beta_second) * gradient * gradient
    direction = (
        first_moment
        / (1.0 - beta_first**STEP)
        / (jnp.sqrt(second_moment / (1.0 - beta_second**STEP)) + adam_eps)
        + weight_decay * weight
    )
    return first_moment, second_moment, direction


def sum_all(values):
    return jnp.sum(jnp.sum(values, axis=1, keepdims=True), axis=0, keepdims=True)


def up_down_pieces(total, part_rows):
    count, columns = total.shape[0] - part_rows, total.shape[1]
    down = jnp.pad(total[part_rows:], ((0, -count % LANES), (0, -columns % LANES)))
    return [total[:part_rows], jnp.transpose(down)[:columns, :count]]


def qkv_out_vis_pieces(total, part_rows, qkv_n, vis_n):
    block = total[:part_rows]
    rest = total[part_rows:]
    vis = [rest[:, g * vis_n : (g + 1) * vis_n] for g in range(total.shape[1] // vis_n)]
    return [block[:, :qkv_n], block[:, qkv_n:], jnp.concatenate(vis, axis=0)]


def lamb_first_kernel(left_ref, right_ref, received_ref, *refs, pieces, lanes_of):
    count = len(lanes_of)
    total = jnp.concatenate(
        [left_ref[...].astype(f32), right_ref[...].astype(f32)], axis=0
    ) + received_ref[...].astype(f32)
    lane = lax.broadcasted_iota(jnp.int32, (1, LANES), 1)
    sums = jnp.zeros((1, LANES), f32)
    ins, outs = refs[: 2 * count], refs[2 * count :]
    for number, gradient in enumerate(pieces(total)):
        weight_ref, moments_ref = ins[2 * number : 2 * number + 2]
        grad_ref, new_ref, direction_ref = outs[3 * number : 3 * number + 3]
        weight = weight_ref[...]
        first, second, direction = lamb_direction(weight, moments_ref[0], moments_ref[1], gradient)
        grad_ref[...] = gradient
        new_ref[0] = first
        new_ref[1] = second
        direction_ref[...] = direction
        place = lanes_of[number]
        sums = jnp.where(lane == place, sum_all(weight * weight), sums)
        sums = jnp.where(lane == place + 16, sum_all(direction * direction), sums)
    outs[-1][...] = sums


def lamb_first(reduction, arrays, pieces, lanes_of):
    (left, _, _), (right, _, _) = reduction.pieces
    received = reduction.received
    flat = sum([list(pair) for pair in arrays], [])
    shapes = []
    for weight, moments in arrays:
        shapes += [struct(weight.shape, f32), struct(moments.shape, f32), struct(weight.shape, f32)]
    shapes.append(struct((1, LANES), f32))
    made = pl.pallas_call(
        functools.partial(lamb_first_kernel, pieces=pieces, lanes_of=lanes_of),
        out_shape=shapes,
        name="lamb_first",
    )(left, right, received, *flat)
    return [made[3 * k : 3 * k + 3] for k in range(len(arrays))], made[-1]


def lamb_last_kernel(totals_ref, sums_ref, *refs, cuts, big):
    small = len(cuts)
    lane = lax.broadcasted_iota(jnp.int32, (1, LANES), 1)
    sums = jnp.sum(sums_ref[...], axis=0, keepdims=True)
    squares = jnp.where(lane < big, sums, 0.0)
    moved = jnp.where(lane < big, pltpu.roll(sums, LANES - 16, 1), 0.0)
    ins = refs[: 2 * small + 2 * big]
    outs = refs[2 * small + 2 * big :]
    kept = []
    for k, (row, height, columns) in enumerate(cuts):
        weight_ref, moments_ref = ins[2 * k : 2 * k + 2]
        gradient = totals_ref[row : row + height, :columns]
        if weight_ref.shape[0] == 1:
            gradient = jnp.concatenate([gradient[r : r + 1] for r in range(height)], axis=1)
        weight = weight_ref[...]
        first, second, direction = lamb_direction(weight, moments_ref[0], moments_ref[1], gradient)
        outs[4 * k][...] = gradient
        outs[4 * k + 2][0] = first
        outs[4 * k + 2][1] = second
        squares = jnp.where(lane == big + k, sum_all(weight * weight), squares)
        moved = jnp.where(lane == big + k, sum_all(direction * direction), moved)
        kept.append((weight, direction))
    weight_norms = jnp.sqrt(squares)
    update_norms = jnp.sqrt(moved)
    ratios = weight_norms / jnp.where(lane < big + small, update_norms, 1.0)
    norms = jnp.concatenate([weight_norms, update_norms, ratios], axis=0)
    outs[-1][...] = norms[:, : big + small]

    def step_of(k):
        return learn_rate * jnp.sum(jnp.where(lane == k, ratios, 0.0), axis=1, keepdims=True)

    for k, (weight, direction) in enumerate(kept):
        new = weight - step_of(big + k) * direction
        outs[4 * k + 1][...] = new
        outs[4 * k + 3][...] = new.astype(bf16)
    for k in range(big):
        weight_ref, direction_ref = ins[2 * small + 2 * k : 2 * small + 2 * k + 2]
        new = weight_ref[...] - step_of(k) * direction_ref[...]
        outs[4 * small + 2 * k][...] = new
        outs[4 * small + 2 * k + 1][...] = new.astype(bf16)


def lamb_last(totals, sums, small, cuts, big):
    shapes = []
    for weight, moments in small:
        shapes += [
            struct(weight.shape, f32),
            struct(weight.shape, f32),
            struct(moments.shape, f32),
            struct(weight.shape, bf16),
        ]
    for weight, _ in big:
        shapes += [struct(weight.shape, f32), struct(weight.shape, bf16)]
    shapes.append(struct((3, len(small) + len(big)), f32))
    flat = sum([list(pair) for pair in small + big], [])
    return pl.pallas_call(
        functools.partial(lamb_last_kernel, cuts=cuts, big=len(big)),
        out_shape=shapes,
        name="lamb_last",
    )(totals, sums, *flat)


def shards(
    hidden_in,
    visual_maps,
    lengths,
    box_x,
    box_y,
    cotangent,
    vis_weight,
    vis_moments,
    qkv_weight,
    qkv_moments,
    out_weight,
    out_moments,
    up_weight,
    up_moments,
    down_weight,
    down_moments,
    up_bias,
    up_bias_moments,
    bn_params,
    bn_moments,
    norm_params,
    norm_moments,
    bias_rows,
    bias_moments,
    rel_tables,
    table_moments,
):
    rows, width = hidden_in.shape
    channels = visual_maps.shape[1]
    dp_parts = lax.axis_size("dp")
    parts = lax.axis_size("tensor")
    device_total = dp_parts * parts
    part_rows, qkv_n = qkv_weight.shape
    out_n = out_weight.shape[1]
    block_n = qkv_n + out_n
    vis_rows, vis_n = vis_weight.shape
    groups = block_n // vis_n
    group_rows = vis_rows // groups
    me = jnp.stack([lax.axis_index("tensor"), lax.axis_index("dp")]).astype(jnp.int32)
    box_x = box_x.reshape(1, rows)
    box_y = box_y.reshape(1, rows)

    vis_b = vis_weight.astype(bf16)
    qo_shard = jnp.concatenate(
        [
            jnp.concatenate([qkv_weight.astype(bf16), out_weight.astype(bf16)], axis=1),
            jnp.concatenate(
                [vis_b[g * group_rows : (g + 1) * group_rows] for g in range(groups)], axis=1
            ),
        ],
        axis=0,
    )
    qo_all = lax.all_gather(qo_shard, ("tensor", "dp"), axis=0, tiled=False).reshape(
        parts, dp_parts, part_rows + group_rows, block_n
    )
    ud_shard = jnp.stack([up_weight.astype(bf16), down_weight.astype(bf16).T])
    ud_all = lax.all_gather(ud_shard, ("tensor", "dp"), axis=0, tiled=False).reshape(
        parts, dp_parts, 2, part_rows, block_n
    )
    vis_full = (
        qo_all[:, :, part_rows:, :]
        .reshape(parts, dp_parts, group_rows, groups, vis_n)
        .transpose(1, 3, 2, 0, 4)
        .reshape(channels, width)
    )

    visual_value = visual_maps.astype(f32)
    sums = jnp.stack([jnp.sum(visual_value, axis=0), jnp.sum(visual_value * visual_value, axis=0)])
    stats = jnp.sum(spread(sums), axis=0)

    bias = relative_bias(lengths, box_x, box_y, rel_tables)
    order, spot = table_plan(box_x, box_y)
    hidden_in, bias, order, spot = lax.optimization_barrier((hidden_in, bias, order, spot))
    mixed, mixed_b, projected, w_qkv, w_out, normed, hat_v = front(
        lengths,
        hidden_in,
        visual_maps,
        stats,
        bn_params,
        qo_all,
        vis_full,
        bias_rows,
        float(visual_maps.shape[0] * device_total),
        qkv_n,
        part_rows,
    )
    context, probs = attend(projected, bias, rows, width)
    first_b, hat1, inv1 = after_attention(context, mixed, w_out, bias_rows, norm_params)
    act, slope, block_out, g2, g2b, red2 = ffn(
        lengths,
        first_b,
        ud_all,
        up_bias.reshape(parts // 2, 1, 2 * block_n),
        hat1,
        cotangent,
        norm_params,
        bias_rows,
    )
    keep_ud, send_ud, up_bias_part, g1, g1b, red1 = ffn_back(
        me, first_b, g2b, ud_all, act, slope, g2, hat1, inv1, norm_params
    )
    core = ("dp", 0)
    pairs = width // LANES
    flat = lambda v: v.reshape(parts, dp_parts // 2, 2 * part_rows, block_n)

    def first_half(g):
        grad = dot_nt(g, w_out).astype(bf16)
        return grad, attend_back(projected, context, grad, probs, 0, pairs // 2)

    (grad_context, back_a), (received_ud,) = beside([], first_half, g1b, [(send_ud, core)])
    ud_sum = Reduction(flat(keep_ud), flat(received_ud), part_rows)

    def second_half(g):
        back = attend_back(projected, context, g, probs, pairs // 2, pairs // 2)
        heads = tuple(back_a[:3]) + tuple(back[:3])
        return back, heads, tail(lengths, heads, w_qkv, g1, vis_full, normed, hat_v)

    (back_b, heads, (grad_mixed, vgrad, red3, red_bn)), _ = beside(
        [ud_sum], second_half, grad_context
    )
    (keep_qo, send_qo), _ = beside(
        [ud_sum],
        lambda h: qkv_gradient(
            me, mixed_b, context, g1b, h, vgrad, parts, dp_parts, qkv_n, block_n
        ),
        heads,
    )
    table_parts = []

    def table_part(part):
        source, first = ((back_a, back_b)[part // 2][3], (part % 2) * 3)
        return lambda g: table_sums(order, spot, g, first, 3), source

    work, source = table_part(0)
    made, (received_qo,) = beside([ud_sum], work, source, [(send_qo, core)])
    table_parts.append(made)
    half = (part_rows + group_rows) // 32 * 16
    qo_sum = Reduction(keep_qo, received_qo, half)
    for part in range(1, 4):
        work, source = table_part(part)
        made, _ = beside([ud_sum, qo_sum], work, source)
        table_parts.append(made)

    small = [
        (up_bias.reshape(1, -1), up_bias_moments.reshape(2, 1, -1)),
        (bn_params, bn_moments),
        (norm_params, norm_moments),
        (bias_rows, bias_moments),
        (rel_tables, table_moments),
    ]
    ff_rows = up_bias.shape[0] // width
    cuts = []
    total_rows = 0
    for height, columns in [(ff_rows, width)] + [pair[0].shape for pair in small[1:]]:
        cuts.append((total_rows, height, columns))
        total_rows += height

    def small_sum(parts_made):
        table_grad = table_gradient(
            jnp.concatenate([made[0] for made in parts_made]),
            jnp.concatenate([made[1] for made in parts_made]),
        )
        widen = lambda v: jnp.pad(v, ((0, 0), (0, width - v.shape[1])))
        pieces = [
            up_bias_part.reshape(ff_rows, width),
            widen(red_bn[0:2]),
            red1[0:2],
            red2[0:2],
            red3[0:3],
            red1[2:3],
            red2[2:3],
            widen(table_grad),
        ]
        padding = jnp.zeros((-total_rows % 32, width), f32)
        packed = jnp.concatenate(pieces + [padding]).reshape(device_total, -1)
        return jnp.sum(lax.all_to_all(packed, ("dp", "tensor"), 0, 0, tiled=True), axis=0)

    if not ud_sum.left():
        own_piece, _ = beside([qo_sum], small_sum, table_parts)
    else:
        own_piece = small_sum(table_parts)
    for one in (ud_sum, qo_sum):
        while one.left():
            beside([one], lambda v: v, own_piece)
    ud_made, ud_squares = lamb_first(
        ud_sum,
        [(up_weight, up_moments), (down_weight, down_moments)],
        functools.partial(up_down_pieces, part_rows=part_rows),
        (3, 4),
    )
    qo_made, qo_squares = lamb_first(
        qo_sum,
        [(qkv_weight, qkv_moments), (out_weight, out_moments), (vis_weight, vis_moments)],
        functools.partial(qkv_out_vis_pieces, part_rows=part_rows, qkv_n=qkv_n, vis_n=vis_n),
        (1, 2, 0),
    )
    piece_n = own_piece.shape[0]
    shared = spread(jnp.concatenate([own_piece, (ud_squares + qo_squares)[0]]))
    totals = shared[:, :piece_n].reshape(-1, width)
    made_big = [qo_made[2], qo_made[0], qo_made[1], ud_made[0], ud_made[1]]
    weights = [vis_weight, qkv_weight, out_weight, up_weight, down_weight]
    made = lamb_last(
        totals,
        shared[:, piece_n:],
        small,
        cuts,
        [(weight, one[2]) for weight, one in zip(weights, made_big)],
    )
    outputs = [block_out, grad_mixed, made[-1]]
    for k in range(5):
        outputs += [made_big[k][0], made[20 + 2 * k], made_big[k][1], made[20 + 2 * k + 1]]
    shapes = [up_bias.shape, up_bias.shape, up_bias_moments.shape, up_bias.shape]
    outputs += [value.reshape(shape) for value, shape in zip(made[:4], shapes)]
    outputs += list(made[4:20])
    return tuple(outputs)


def solution(mesh):
    in_specs = (
        P(("dp", "tensor"), None),
        P(("dp", "tensor"), None),
        P(("dp", "tensor"), None),
        P(("dp", "tensor")),
        P(("dp", "tensor")),
        P(("dp", "tensor"), None),
        P("dp", "tensor"),
        P(None, "dp", "tensor"),
        P("dp", "tensor"),
        P(None, "dp", "tensor"),
        P("dp", "tensor"),
        P(None, "dp", "tensor"),
        P("dp", "tensor"),
        P(None, "dp", "tensor"),
        P("tensor", "dp"),
        P(None, "tensor", "dp"),
        P(),
        P(),
        P(),
        P(),
        P(),
        P(),
        P(),
        P(),
        P(),
        P(),
    )
    out_specs = (
        P(("dp", "tensor"), None),
        P(("dp", "tensor"), None),
        P(),
        P("dp", "tensor"),
        P("dp", "tensor"),
        P(None, "dp", "tensor"),
        P("dp", "tensor"),
        P("dp", "tensor"),
        P("dp", "tensor"),
        P(None, "dp", "tensor"),
        P("dp", "tensor"),
        P("dp", "tensor"),
        P("dp", "tensor"),
        P(None, "dp", "tensor"),
        P("dp", "tensor"),
        P("dp", "tensor"),
        P("dp", "tensor"),
        P(None, "dp", "tensor"),
        P("dp", "tensor"),
        P("tensor", "dp"),
        P("tensor", "dp"),
        P(None, "tensor", "dp"),
        P("tensor", "dp"),
        P(),
        P(),
        P(),
        P(),
        P(),
        P(),
        P(),
        P(),
        P(),
        P(),
        P(),
        P(),
        P(),
        P(),
        P(),
        P(),
        P(),
        P(),
        P(),
        P(),
    )
    return jax.shard_map(shards, mesh=mesh, in_specs=in_specs, out_specs=out_specs, check_vma=False)
```

```python
import functools
import math

import jax
import jax.numpy as jnp
import numpy as np
from jax import lax
from jax.experimental import pallas as pl
from jax.experimental.pallas import tpu as pltpu
from jax.sharding import PartitionSpec as P

HEADS = 12
HDIM = 64
PATCHES = 49
REL1 = 32
REL2 = 64
DIST1 = 128
DIST2 = 256
STEP = 10
LANES = 128

layer_eps = 1e-06
batch_eps = 1e-05
beta_first = 0.9
beta_second = 0.999
adam_eps = 1e-06
weight_decay = 0.01
learn_rate = 0.4
masked_score = -1000000000.0
f32 = jnp.float32
bf16 = jnp.bfloat16
SMEM_SPEC = pl.BlockSpec(memory_space=pltpu.SMEM)


def dot_nn(left, right):
    return lax.dot_general(left, right, (((1,), (0,)), ((), ())), preferred_element_type=f32)


def dot_nt(left, right):
    return lax.dot_general(left, right, (((1,), (1,)), ((), ())), preferred_element_type=f32)


def dot_tn(left, right):
    return lax.dot_general(left, right, (((0,), (0,)), ((), ())), preferred_element_type=f32)


def whole_spec(shape):
    zeros = (0,) * len(shape)
    return pl.BlockSpec(tuple(shape), lambda *_: zeros)


def struct(shape, dtype):
    return jax.ShapeDtypeStruct(tuple(shape), dtype)


def bucket_edges(bucket_count, max_distance):
    half = bucket_count // 2
    exact = half // 2
    edges = []
    for level in range(1, half):
        if level < exact:
            edges.append(level)
        else:
            found = max_distance
            for distance in range(exact, max_distance + 1):
                if (
                    exact
                    + int(
                        math.log(distance / exact) / math.log(max_distance / exact) * (half - exact)
                    )
                    >= level
                ):
                    found = distance
                    break
            edges.append(found)
    return edges


EDGES1 = bucket_edges(REL1, DIST1)
EDGES2 = bucket_edges(REL2, DIST2)


def bucket_index(delta, bucket_count, edges):
    half = bucket_count // 2
    exact = half // 2
    distance = jnp.abs(delta)
    level = jnp.minimum(distance, exact)
    for edge in edges[exact:]:
        level = level + (distance >= edge).astype(jnp.int32)
    return jnp.where(delta > 0, half, 0) + level


def doc_ends(lens_ref):
    ends = []
    total = None
    for k in range(lens_ref.shape[1]):
        total = lens_ref[0, k] if total is None else total + lens_ref[0, k]
        ends.append(total)
    return ends


def doc_of(rows, ends):
    found = jnp.zeros(rows.shape, jnp.int32)
    for end in ends:
        found = found + (rows >= end).astype(jnp.int32)
    return found


def visual_mask(rows, ends):
    hit = None
    for end in ends:
        inside = (rows >= end - PATCHES) & (rows < end)
        hit = inside if hit is None else hit | inside
    return hit


def column_of(row_block):
    return jnp.transpose(jnp.broadcast_to(row_block, (LANES, LANES)))


def bias_kernel(lens_ref, xs_ref, ys_ref, xt_ref, yt_ref, tab_ref, *refs, first):
    near_ref, out_ref = (refs[1], refs[0]) if first == 0 else (refs[0], refs[2])
    x_ref, y_ref = refs[-2:]
    tile = out_ref.shape[1]
    cols_total = out_ref.shape[2]
    ends = doc_ends(lens_ref)
    step = pl.program_id(0) + first
    table = tab_ref[...]
    table_lin = jnp.concatenate(
        [table[:, :REL1], jnp.zeros((HEADS, LANES - REL1), f32)], axis=1
    )
    table_xy = table[:, REL1:]
    lanes = lax.broadcasted_iota(jnp.int32, (8, LANES), 1)
    subs = lax.broadcasted_iota(jnp.int32, (8, LANES), 0)

    def lookup(flat, h, index):
        return jnp.take_along_axis(
            jnp.broadcast_to(flat[h : h + 1, :], (8, LANES)), index, axis=1
        )

    @pl.when(step == 0)
    def _():
        def one_group(g, carry):
            place = pl.ds(pl.multiple_of(g * 8, 8), 8)
            for o in range(3):
                delta = lanes + (o - 1) * LANES - subs - g * 8
                lin = bucket_index(delta, REL1, EDGES1)
                for h in range(HEADS):
                    near_ref[h, o, place, :] = lookup(table_lin, h, lin)
            return carry

        lax.fori_loop(0, tile // 8, one_group, 0)

    x_ref[...] = column_of(xt_ref[...])
    y_ref[...] = column_of(yt_ref[...])
    far = [
        [jnp.broadcast_to(table[h : h + 1, b : b + 1], (8, LANES)) for h in range(HEADS)]
        for b in (REL1 // 2 - 1, REL1 - 1)
    ]

    def one_group(g, carry):
        place = pl.ds(pl.multiple_of(g * 8, 8), 8)
        row_doc = doc_of(subs + (step * tile + g * 8), ends)
        x_col = x_ref[place, :]
        y_col = y_ref[place, :]
        for c in range(cols_total // LANES):
            piece = slice(c * LANES, (c + 1) * LANES)
            across = bucket_index(xs_ref[:, piece] - x_col, REL2, EDGES2)
            down = bucket_index(ys_ref[:, piece] - y_col, REL2, EDGES2) + REL2
            same = row_doc == doc_of(lanes + c * LANES, ends)
            offset = jnp.clip(c - step, -1, 1) + 1
            close = jnp.abs(c - step) <= 1
            got_x = [lookup(table_xy, h, across) for h in range(HEADS)]
            got_y = [lookup(table_xy, h, down) for h in range(HEADS)]
            for h in range(HEADS):
                beyond = jnp.where(c > step, far[1][h], far[0][h])
                lin = jnp.where(close, near_ref[h, offset, place, :], beyond)
                out_ref[h, place, piece] = jnp.where(
                    same, got_x[h] + got_y[h] + lin, masked_score
                )
        return carry

    lax.fori_loop(0, tile // 8, one_group, 0)


def relative_bias(lengths, box_x, box_y, tables, first, count, before=()):
    rows = box_x.shape[1]
    tile = LANES
    row_spec = pl.BlockSpec((1, tile), lambda i: (0, first + i))
    near_shape = (HEADS, 3, tile, LANES)
    out_spec = pl.BlockSpec((HEADS, tile, rows), lambda i: (0, first + i, 0))
    out_shape = struct((HEADS, rows, rows), f32)
    return pl.pallas_call(
        functools.partial(bias_kernel, first=first),
        grid=(count,),
        in_specs=[
            SMEM_SPEC,
            whole_spec((1, rows)),
            whole_spec((1, rows)),
            row_spec,
            row_spec,
            whole_spec(tables.shape),
        ]
        + ([whole_spec(near_shape), pl.BlockSpec(memory_space=pl.ANY)] if before else []),
        out_specs=out_spec if before else [out_spec, whole_spec(near_shape)],
        out_shape=out_shape if before else [out_shape, struct(near_shape, f32)],
        scratch_shapes=[pltpu.VMEM((tile, LANES), jnp.int32)] * 2,
        input_output_aliases={7: 0} if before else {},
        name="relative_bias",
    )(lengths, box_x, box_y, box_x, box_y, tables, *before)


def front_kernel(
    lens_ref,
    me_ref,
    hidden_ref,
    maps_ref,
    stats_ref,
    bn_ref,
    a_mine_ref,
    a_other_ref,
    b_mine_ref,
    b_other_ref,
    bias_ref,
    mixed_ref,
    mixed_b_ref,
    proj_ref,
    wqkv_ref,
    wout_ref,
    vis_ref,
    normed_ref,
    hat_ref,
    *,
    total_rows,
    qkv_n,
    part_rows,
    parts,
    names,
):
    tile = hidden_ref.shape[0]
    width = hidden_ref.shape[1]
    cut, block_n = a_mine_ref.shape[1:]
    out_n = block_n - qkv_n
    vis_n = width // parts
    groups = block_n // vis_n
    group_rows = cut + b_mine_ref.shape[1] - part_rows
    dp_half = 2 * a_mine_ref.shape[0] // parts

    def place_of(order, tensor_slot, dp_slot):
        index = 0
        for name, bit in order:
            slot = tensor_slot if name == "tensor" else dp_slot
            index = 2 * index + ((slot >> bit) & 1)
        return index

    @pl.when(pl.program_id(0) == 0)
    def _():
        def one_part(d, carry):
            for core in range(2):
                dp_slot = 2 * d + core
                owner = me_ref[1] ^ dp_slot
                refs = ((a_mine_ref, a_other_ref)[core], (b_mine_ref, b_other_ref)[core])
                for t in range(parts):
                    for ref, order, first, count in zip(
                        refs, names, (0, cut), (cut, part_rows - cut)
                    ):
                        block = ref[place_of(order, me_ref[0] ^ t, dp_slot)]
                        place = pl.ds(pl.multiple_of(owner * part_rows + first, 16), count)
                        wqkv_ref[place, t * qkv_n : (t + 1) * qkv_n] = block[:count, :qkv_n]
                        wout_ref[place, t * out_n : (t + 1) * out_n] = block[:count, qkv_n:]
                    for g in range(groups):
                        first = owner * (group_rows * groups) + g * group_rows
                        place = pl.ds(pl.multiple_of(first, group_rows), group_rows)
                        vis_ref[place, t * vis_n : (t + 1) * vis_n] = block[
                            part_rows - cut :, g * vis_n : (g + 1) * vis_n
                        ]
            return carry

        lax.fori_loop(0, dp_half // 2, one_part, 0)

    ends = doc_ends(lens_ref)
    start = pl.program_id(0) * tile
    visual_total, channels = maps_ref.shape
    rows = lax.broadcasted_iota(jnp.int32, (tile, visual_total), 0) + start
    slots = lax.broadcasted_iota(jnp.int32, (tile, visual_total), 1)
    target = slots
    for k, end in enumerate(ends):
        target = jnp.where(slots >= k * PATCHES, slots - (k + 1) * PATCHES + end, target)
    select = (rows == target).astype(f32).astype(bf16)
    picked = dot_nn(select, maps_ref[...])
    is_visual = visual_mask(
        lax.broadcasted_iota(jnp.int32, (tile, channels), 0) + start, ends
    )
    mean = stats_ref[0:1, :] / total_rows
    var = stats_ref[1:2, :] / total_rows - mean * mean
    hat = (picked - mean) * lax.rsqrt(var + batch_eps)
    hat = jnp.where(is_visual, hat, 0.0)
    hat_ref[...] = hat
    normed = jnp.where(is_visual, hat * bn_ref[0:1, :] + bn_ref[1:2, :], 0.0).astype(bf16)
    normed_ref[...] = normed
    embedded = dot_nn(normed, vis_ref[...]) + bias_ref[0:1, :]
    row_visual = visual_mask(lax.broadcasted_iota(jnp.int32, (tile, width), 0) + start, ends)
    mixed = hidden_ref[...].astype(f32) + jnp.where(row_visual, embedded, 0.0)
    mixed_ref[...] = mixed
    mixed_b = mixed.astype(bf16)
    mixed_b_ref[...] = mixed_b
    for part in range(3):
        columns = slice(part * width, (part + 1) * width)
        piece = dot_nn(mixed_b, wqkv_ref[:, columns])
        if part == 0:
            piece = piece + bias_ref[1:2, :]
        if part == 2:
            piece = piece + bias_ref[2:3, :]
        proj_ref[:, columns] = piece.astype(bf16)


def front(lengths, me, hidden, maps, stats, bn_params, shards_of, names, bias_rows, total_rows, qkv_n, part_rows, parts):
    rows, width = hidden.shape
    channels = maps.shape[1]
    tile = rows // 3 if rows % 384 == 0 else rows
    row_block = lambda n: pl.BlockSpec((tile, n), lambda i: (i, 0))
    return pl.pallas_call(
        functools.partial(
            front_kernel,
            total_rows=total_rows,
            qkv_n=qkv_n,
            part_rows=part_rows,
            parts=parts,
            names=names,
        ),
        grid=(rows // tile,),
        in_specs=[
            SMEM_SPEC,
            SMEM_SPEC,
            row_block(width),
            whole_spec(maps.shape),
            whole_spec(stats.shape),
            whole_spec(bn_params.shape),
            *[whole_spec(piece.shape) for piece in shards_of],
            whole_spec(bias_rows.shape),
        ],
        out_specs=[
            row_block(width),
            row_block(width),
            row_block(3 * width),
            whole_spec((width, 3 * width)),
            whole_spec((width, width)),
            whole_spec((channels, width)),
            row_block(channels),
            row_block(channels),
        ],
        out_shape=[
            struct((rows, width), f32),
            struct((rows, width), bf16),
            struct((rows, 3 * width), bf16),
            struct((width, 3 * width), bf16),
            struct((width, width), bf16),
            struct((channels, width), bf16),
            struct((rows, channels), bf16),
            struct((rows, channels), f32),
        ],
        name="front",
    )(lengths, me, hidden, maps, stats, bn_params, *shards_of, bias_rows)


def pair_mask(shape, h):
    lane = lax.broadcasted_iota(jnp.int32, shape, len(shape) - 1)
    return (lane >= HDIM) if h else (lane < HDIM)


def attend_kernel(q_ref, k_ref, v_ref, bias_ref, ctx_ref, probs_ref):
    queries = q_ref[...].astype(f32) * (HDIM**-0.5)
    context = None
    for h in range(2):
        mask = pair_mask(queries.shape, h)
        query_h = jnp.where(mask, queries, 0.0).astype(bf16)
        scores = dot_nt(query_h, k_ref[...]) + bias_ref[h]
        exps = jnp.exp(scores - jnp.max(scores, axis=-1, keepdims=True))
        probs = (exps * (1.0 / jnp.sum(exps, axis=-1, keepdims=True))).astype(bf16)
        probs_ref[h] = probs
        piece = dot_nn(probs, v_ref[...])
        context = piece if context is None else jnp.where(mask, piece, context)
    ctx_ref[...] = context.astype(bf16)


def attend(projected, bias, rows, width):
    pairs = width // LANES
    tile = rows // 3
    return pl.pallas_call(
        attend_kernel,
        grid=(pairs, rows // tile),
        in_specs=[
            pl.BlockSpec((tile, LANES), lambda p, i: (i, p)),
            pl.BlockSpec((rows, LANES), lambda p, i: (0, pairs + p)),
            pl.BlockSpec((rows, LANES), lambda p, i: (0, 2 * pairs + p)),
            pl.BlockSpec((2, tile, rows), lambda p, i: (p, i, 0)),
        ],
        out_specs=[
            pl.BlockSpec((tile, LANES), lambda p, i: (i, p)),
            pl.BlockSpec((2, tile, rows), lambda p, i: (p, i, 0)),
        ],
        out_shape=[struct((rows, width), bf16), struct((HEADS, rows, rows), bf16)],
        name="attend",
    )(projected, projected, projected, bias)


def attend_back_kernel(q_ref, k_ref, v_ref, ctx_ref, gctx_ref, probs_ref, dq_ref, dk_ref, dv_ref, gs_ref):
    rows = q_ref.shape[0]
    tile = rows // 3
    scale = HDIM**-0.5
    keys_h = []
    for h in range(2):
        mask = pair_mask(k_ref.shape, h)
        keys_h.append(jnp.where(mask, k_ref[...].astype(f32), 0.0).astype(bf16))
    grad_k = None
    grad_v = None
    for i in range(rows // tile):
        place = slice(i * tile, (i + 1) * tile)
        queries = q_ref[place, :].astype(f32) * scale
        grads = gctx_ref[place, :].astype(f32)
        inner = grads * ctx_ref[place, :].astype(f32)
        grad_q = None
        for h in range(2):
            mask = pair_mask(queries.shape, h)
            query_h = jnp.where(mask, queries, 0.0).astype(bf16)
            grad_h = jnp.where(mask, grads, 0.0).astype(bf16)
            total = jnp.sum(jnp.where(mask, inner, 0.0), axis=-1, keepdims=True)
            grad_probs = dot_nt(grad_h, v_ref[...])
            probs = probs_ref[h, place, :]
            grad_scores = (probs.astype(f32) * (grad_probs - total)).astype(bf16)
            gs_ref[h, place, :] = grad_scores
            piece_q = dot_nn(grad_scores, keys_h[h])
            piece_k = dot_tn(grad_scores, query_h)
            piece_v = dot_tn(probs, grad_h)
            grad_q = piece_q if grad_q is None else grad_q + piece_q
            grad_k = piece_k if grad_k is None else grad_k + piece_k
            grad_v = piece_v if grad_v is None else grad_v + piece_v
        dq_ref[place, :] = (grad_q * scale).astype(bf16)
    dk_ref[...] = grad_k.astype(bf16)
    dv_ref[...] = grad_v.astype(bf16)


def attend_back(projected, context, grad_context, probs, first_pair, pair_count):
    rows, width = context.shape
    pairs = width // LANES
    column = lambda shift: pl.BlockSpec((rows, LANES), lambda p: (0, shift + first_pair + p))
    plain = pl.BlockSpec((rows, LANES), lambda p: (0, p))
    n = pair_count
    return pl.pallas_call(
        attend_back_kernel,
        grid=(n,),
        in_specs=[
            column(0),
            column(pairs),
            column(2 * pairs),
            column(0),
            column(0),
            pl.BlockSpec((2, rows, rows), lambda p: (first_pair + p, 0, 0)),
        ],
        out_specs=[plain, plain, plain, pl.BlockSpec((2, rows, rows), lambda p: (p, 0, 0))],
        out_shape=[
            struct((rows, n * LANES), bf16),
            struct((rows, n * LANES), bf16),
            struct((rows, n * LANES), bf16),
            struct((2 * n, rows, rows), bf16),
        ],
        name="attend_back",
    )(projected, projected, projected, context, grad_context, probs)


def table_thetas():
    limits = list(EDGES2) + [1 - edge for edge in EDGES2]
    limits = limits + [5000] * (REL2 - len(limits))
    return np.asarray(limits + limits, np.int32)[None, :]


def table_mix():
    count = len(EDGES2)
    mix = np.zeros((2 * REL2, 2 * REL2), np.float32)
    for side in range(2):
        base = side * REL2
        every = base + 2 * count
        above = lambda m: base + m - 1
        below = lambda m: base + count + m - 1
        for m in range(1, count + 1):
            mix[above(m), base + REL2 // 2 + m] -= 1.0
            if m < count:
                mix[above(m + 1), base + REL2 // 2 + m] += 1.0
            else:
                mix[every, base + REL2 // 2 + m] += 1.0
            mix[below(m), base + m] += 1.0
            if m < count:
                mix[below(m + 1), base + m] -= 1.0
        mix[above(1), base] += 1.0
        mix[below(1), base] -= 1.0
    return mix


def table_plan_kernel(xs_ref, ys_ref, theta_ref, order_ref, spot_ref):
    rows = xs_ref.shape[1]
    chunks = rows // LANES
    lane = lax.broadcasted_iota(jnp.int32, (LANES, LANES), 1)
    sub = lax.broadcasted_iota(jnp.int32, (LANES, LANES), 0)
    wide = 8 * LANES
    for side, line_ref in enumerate((xs_ref, ys_ref)):
        line = line_ref[...]
        below = jnp.zeros((1, wide), f32)
        for c in range(chunks):
            column = column_of(line[:, c * LANES : (c + 1) * LANES])
            rank = jnp.zeros((LANES, 1), f32)
            for e in range(chunks):
                other = line[:, e * LANES : (e + 1) * LANES]
                earlier = (other < column) | (
                    (other == column) & (lane + e * LANES < sub + c * LANES)
                )
                rank = rank + jnp.sum(earlier.astype(f32), axis=1, keepdims=True)
            level = lax.broadcasted_iota(jnp.int32, (LANES, rows), 1).astype(f32)
            order_ref[c * LANES : (c + 1) * LANES, side * rows : (side + 1) * rows] = (
                (rank <= level).astype(f32).astype(bf16)
            )
            steps = lax.broadcasted_iota(jnp.int32, (LANES, wide), 1)
            wide_column = jnp.concatenate([column] * 8, axis=1)
            below = below + jnp.sum((wide_column < steps).astype(f32), axis=0, keepdims=True)
        below_i = below.astype(jnp.int32)
        for c in range(chunks):
            column = column_of(line[:, c * LANES : (c + 1) * LANES])
            limit = jnp.clip(column + theta_ref[...], 0, wide - 1)
            found = jnp.zeros((LANES, LANES), jnp.int32)
            for e in range(8):
                piece = jnp.broadcast_to(below_i[:, e * LANES : (e + 1) * LANES], (LANES, LANES))
                got = jnp.take_along_axis(piece, limit & (LANES - 1), axis=1)
                found = jnp.where((limit >> 7) == e, got, found)
            place = slice(c * LANES, (c + 1) * LANES)
            if side == 0:
                spot_ref[place, :] = found - 1
            else:
                spot_ref[place, :] = jnp.where(lane < REL2, spot_ref[place, :], found - 1)


def table_plan(box_x, box_y):
    rows = box_x.shape[1]
    thetas = jnp.asarray(table_thetas())
    return pl.pallas_call(
        table_plan_kernel,
        grid=(1,),
        in_specs=[whole_spec((1, rows)), whole_spec((1, rows)), whole_spec((1, LANES))],
        out_specs=[whole_spec((rows, 2 * rows)), whole_spec((rows, LANES))],
        out_shape=[struct((rows, 2 * rows), bf16), struct((rows, LANES), jnp.int32)],
        name="table_plan",
    )(box_x, box_y, thetas)


def table_kernel(order_ref, spot_ref, gs_ref, xy_ref, diag_ref, *prefix_refs):
    rows = gs_ref.shape[1]
    chunks = rows // LANES
    lane8 = lax.broadcasted_iota(jnp.int32, (8, LANES), 1)
    lane = lax.broadcasted_iota(jnp.int32, (LANES, LANES), 1)
    sub = lax.broadcasted_iota(jnp.int32, (LANES, LANES), 0)
    flip = (lane + sub == LANES - 1).astype(f32).astype(bf16)
    pad = jnp.zeros((LANES, LANES), f32)
    zero = jnp.zeros((8, LANES), f32)
    total = zero
    near = jnp.zeros((8, 4 * LANES), f32)
    far = [zero, zero]
    for c in range(chunks):
        prefix_refs[c][...] = dot_nn(gs_ref[0, c * LANES : (c + 1) * LANES, :], order_ref[...])
    for c in range(chunks):
        for g in range(LANES // 8):
            here = slice(g * 8, g * 8 + 8)
            spot = spot_ref[c * LANES + g * 8 : c * LANES + g * 8 + 8, :]
            low = spot & (LANES - 1)
            high = spot >> 7
            found = zero
            for e in range(chunks):
                got_x, got_y = [
                    jnp.take_along_axis(
                        prefix_refs[c][here, side + e * LANES : side + (e + 1) * LANES], low, axis=1
                    )
                    for side in (0, rows)
                ]
                found = jnp.where(high == e, jnp.where(lane8 < REL2, got_x, got_y), found)
            total = total + found
        place = slice(c * LANES, (c + 1) * LANES)
        left, right = max(c - 1, 0), min(c + 2, chunks)
        turned = [dot_nn(flip, gs_ref[0, place, left * LANES : right * LANES])]
        if c == 0:
            turned = [pad] + turned
        if right == c + 1:
            turned = turned + [pad]
        turned = pltpu.roll(
            jnp.concatenate(turned + [pad], axis=1), 0, 1, stride=1, stride_axis=0
        )
        near = near + jnp.sum(turned.reshape(LANES // 8, 8, 4 * LANES), axis=0)
        for e in range(chunks):
            if abs(e - c) > 1:
                piece = gs_ref[0, place, e * LANES : (e + 1) * LANES].astype(f32)
                far[e > c] = far[e > c] + jnp.sum(piece.reshape(LANES // 8, 8, LANES), axis=0)
    xy_ref[0] = total
    diag_ref[...] = jnp.zeros(diag_ref.shape, f32)
    diag_ref[0, :, rows - 2 * LANES : rows + 2 * LANES] = near
    diag_ref[0, :, :LANES] += far[0]
    diag_ref[0, :, 2 * rows - LANES :] += far[1]


def table_sums(order, spot, grad_scores, first, heads):
    rows = grad_scores.shape[1]
    return pl.pallas_call(
        table_kernel,
        grid=(heads,),
        in_specs=[
            whole_spec(order.shape),
            whole_spec(spot.shape),
            pl.BlockSpec((1, rows, rows), lambda h: (first + h, 0, 0)),
        ],
        out_specs=[
            pl.BlockSpec((1, 8, LANES), lambda h: (h, 0, 0)),
            pl.BlockSpec((1, 8, 2 * rows), lambda h: (h, 0, 0)),
        ],
        out_shape=[struct((heads, 8, LANES), f32), struct((heads, 8, 2 * rows), f32)],
        scratch_shapes=[pltpu.VMEM((LANES, 2 * rows), f32)] * (rows // LANES),
        name="table_sums",
    )(order, spot, grad_scores)


def row_mean(values):
    return jnp.mean(values, axis=-1, keepdims=True)


def after_kernel(ctx_ref, mixed_ref, wout_ref, bias_ref, norm_ref, first_ref, hat_ref, inv_ref):
    values = mixed_ref[...] + dot_nn(ctx_ref[...], wout_ref[...]) + bias_ref[3:4, :]
    centred = values - row_mean(values)
    inverse = lax.rsqrt(row_mean(centred * centred) + layer_eps)
    hat = centred * inverse
    hat_ref[...] = hat
    inv_ref[...] = inverse
    first_ref[...] = (hat * norm_ref[0:1, :] + norm_ref[1:2, :]).astype(bf16)


def after_attention(context, mixed, w_out, bias_rows, norm_params):
    rows, width = mixed.shape
    tile = rows // 3
    row_block = lambda n: pl.BlockSpec((tile, n), lambda i: (i, 0))
    return pl.pallas_call(
        after_kernel,
        grid=(rows // tile,),
        in_specs=[
            row_block(width),
            row_block(width),
            whole_spec(w_out.shape),
            whole_spec(bias_rows.shape),
            whole_spec(norm_params.shape),
        ],
        out_specs=[row_block(width), row_block(width), row_block(1)],
        out_shape=[
            struct((rows, width), bf16),
            struct((rows, width), f32),
            struct((rows, 1), f32),
        ],
        name="after_attention",
    )(context, mixed, w_out, bias_rows, norm_params)


def joined(ref, width):
    columns = ref.shape[-1]
    return jnp.concatenate([ref[g, :, 0].reshape(width, columns) for g in range(2)], axis=1)


def ffn_kernel(
    lens_ref,
    first_ref,
    up_ref,
    down_ref,
    ubias_ref,
    hat_ref,
    cot_ref,
    norm_ref,
    bias_ref,
    act_ref,
    slope_ref,
    out_ref,
    g2_ref,
    g2b_ref,
    red_ref,
    acc_ref,
):
    step = pl.program_id(0)
    rows, width = first_ref.shape
    block_n = up_ref.shape[-1]
    pre = dot_nn(first_ref[...], joined(up_ref, width)) + ubias_ref[0]
    cdf = 0.5 + 0.5 * lax.erf(pre * (2.0**-0.5))
    act = (pre * cdf).astype(bf16)
    act_ref[0] = act
    slope_ref[0] = (cdf + pre * (jnp.exp(-0.5 * pre * pre) * ((2.0 * math.pi) ** -0.5))).astype(
        bf16
    )
    piece = dot_nt(act, joined(down_ref, width))

    @pl.when(step == 0)
    def _():
        acc_ref[...] = piece

    @pl.when(step > 0)
    def _():
        acc_ref[...] += piece

    @pl.when(step == pl.num_programs(0) - 1)
    def _():
        ends = doc_ends(lens_ref)
        tile = LANES
        red_ref[...] = jnp.zeros(red_ref.shape, f32)

        def one_tile(i, carry):
            place = pl.ds(pl.multiple_of(i * tile, tile), tile)
            values = (
                hat_ref[place, :] * norm_ref[0:1, :]
                + norm_ref[1:2, :]
                + acc_ref[place, :]
                + bias_ref[4:5, :]
            )
            centred = values - row_mean(values)
            inverse = lax.rsqrt(row_mean(centred * centred) + layer_eps)
            hat = centred * inverse
            out_ref[place, :] = (hat * norm_ref[2:3, :] + norm_ref[3:4, :]).astype(bf16)
            row = lax.broadcasted_iota(jnp.int32, (tile, width), 0) + i * tile
            grad = jnp.where(row < ends[-1], cot_ref[place, :].astype(f32), 0.0)
            scaled = grad * norm_ref[2:3, :]
            g2 = inverse * (scaled - row_mean(scaled) - hat * row_mean(scaled * hat))
            g2_ref[place, :] = g2
            g2b_ref[place, :] = g2.astype(bf16)
            red_ref[0:1, :] += jnp.sum(grad * hat, axis=0, keepdims=True)
            red_ref[1:2, :] += jnp.sum(grad, axis=0, keepdims=True)
            red_ref[2:3, :] += jnp.sum(g2, axis=0, keepdims=True)
            return carry

        lax.fori_loop(0, rows // tile, one_tile, 0)


def ffn(lengths, first_b, ud_all, up_bias, hat1, cotangent, norm_params, bias_rows):
    rows, width = first_b.shape
    parts, dp_parts, _, part_rows, block_n = ud_all.shape
    weight = lambda which: pl.BlockSpec(
        (2, dp_parts, 1, part_rows, block_n), lambda t: (t, 0, which, 0, 0)
    )
    block = pl.BlockSpec((1, rows, 2 * block_n), lambda t: (t, 0, 0))
    return pl.pallas_call(
        ffn_kernel,
        grid=(parts // 2,),
        in_specs=[
            SMEM_SPEC,
            whole_spec(first_b.shape),
            weight(0),
            weight(1),
            pl.BlockSpec((1, 1, 2 * block_n), lambda t: (t, 0, 0)),
            whole_spec(hat1.shape),
            whole_spec(cotangent.shape),
            whole_spec(norm_params.shape),
            whole_spec(bias_rows.shape),
        ],
        out_specs=[
            block,
            block,
            whole_spec((rows, width)),
            whole_spec((rows, width)),
            whole_spec((rows, width)),
            whole_spec((8, width)),
        ],
        out_shape=[
            struct((parts // 2, rows, 2 * block_n), bf16),
            struct((parts // 2, rows, 2 * block_n), bf16),
            struct((rows, width), bf16),
            struct((rows, width), f32),
            struct((rows, width), bf16),
            struct((8, width), f32),
        ],
        scratch_shapes=[pltpu.VMEM((rows, width), f32)],
        name="ffn",
    )(lengths, first_b, ud_all, ud_all, up_bias, hat1, cotangent, norm_params, bias_rows)


def ffn_back_kernel(
    me_ref,
    first_ref,
    g2b_ref,
    up_ref,
    down_ref,
    act_ref,
    slope_ref,
    g2_ref,
    hat_ref,
    inv_ref,
    norm_ref,
    keep_up_ref,
    keep_down_ref,
    send_up_ref,
    send_down_ref,
    ub_ref,
    g1_ref,
    g1b_ref,
    red_ref,
    acc_ref,
    first_t_ref,
    g2_t_ref,
    grad_ref,
):
    step = pl.program_id(0)
    rows, width = first_ref.shape
    _, dp_parts, _, part_rows, block_n = up_ref.shape
    mine = me_ref[1]

    @pl.when(step == 0)
    def _():
        first_t_ref[...] = jnp.transpose(first_ref[...])
        g2_t_ref[...] = jnp.transpose(g2b_ref[...])

    grad_act = dot_nn(g2b_ref[...], joined(down_ref, width))
    grad_pre = (slope_ref[0].astype(f32) * grad_act).astype(bf16)
    ub_ref[0] = jnp.sum(grad_pre.astype(f32), axis=0, keepdims=True)
    grad_ref[0] = dot_nn(first_t_ref[...], grad_pre).astype(bf16)
    grad_ref[1] = dot_nn(g2_t_ref[...], act_ref[0]).astype(bf16)
    for slot in range(dp_parts):
        place = pl.ds(pl.multiple_of((mine ^ slot) * part_rows, 16), part_rows)
        targets = (send_up_ref, send_down_ref) if slot % 2 else (keep_up_ref, keep_down_ref)
        for which, target in enumerate(targets):
            for g in range(2):
                target[(me_ref[0] & 1) ^ g, slot // 2] = grad_ref[
                    which, place, g * block_n : (g + 1) * block_n
                ]
    piece = dot_nt(grad_pre, joined(up_ref, width))

    @pl.when(step == 0)
    def _():
        acc_ref[...] = piece

    @pl.when(step > 0)
    def _():
        acc_ref[...] += piece

    @pl.when(step == pl.num_programs(0) - 1)
    def _():
        tile = LANES
        red_ref[...] = jnp.zeros(red_ref.shape, f32)

        def one_tile(i, carry):
            place = pl.ds(pl.multiple_of(i * tile, tile), tile)
            grad = g2_ref[place, :] + acc_ref[place, :]
            hat = hat_ref[place, :]
            scaled = grad * norm_ref[0:1, :]
            g1 = inv_ref[place, :] * (
                scaled - row_mean(scaled) - hat * row_mean(scaled * hat)
            )
            g1b = g1.astype(bf16)
            g1_ref[place, :] = g1
            g1b_ref[place, :] = g1b
            red_ref[0:1, :] += jnp.sum(grad * hat, axis=0, keepdims=True)
            red_ref[1:2, :] += jnp.sum(grad, axis=0, keepdims=True)
            red_ref[2:3, :] += jnp.sum(g1b.astype(f32), axis=0, keepdims=True)
            return carry

        lax.fori_loop(0, rows // tile, one_tile, 0)


def ffn_back(me, first_b, g2b, ud_all, act, slope, g2, hat1, inv1, norm_params):
    rows, width = first_b.shape
    parts, dp_parts, _, part_rows, block_n = ud_all.shape
    weight = lambda which: pl.BlockSpec(
        (2, dp_parts, 1, part_rows, block_n), lambda t, me: (t, 0, which, 0, 0)
    )
    block = pl.BlockSpec((1, rows, 2 * block_n), lambda t, me: (t, 0, 0))
    half = pl.BlockSpec(
        (2, dp_parts // 2, part_rows, block_n), lambda t, me: (t ^ (me[0] >> 1), 0, 0, 0)
    )
    half_shape = struct((parts, dp_parts // 2, part_rows, block_n), bf16)
    return pl.pallas_call(
        ffn_back_kernel,
        grid_spec=pltpu.PrefetchScalarGridSpec(
            num_scalar_prefetch=1,
            grid=(parts // 2,),
            in_specs=[
                whole_spec(first_b.shape),
                whole_spec(g2b.shape),
                weight(0),
                weight(1),
                block,
                block,
                whole_spec(g2.shape),
                whole_spec(hat1.shape),
                whole_spec(inv1.shape),
                whole_spec(norm_params.shape),
            ],
            out_specs=[
                half,
                half,
                half,
                half,
                pl.BlockSpec((1, 1, 2 * block_n), lambda t, me: (t, 0, 0)),
                whole_spec((rows, width)),
                whole_spec((rows, width)),
                whole_spec((8, width)),
            ],
            scratch_shapes=[
                pltpu.VMEM((rows, width), f32),
                pltpu.VMEM((width, rows), bf16),
                pltpu.VMEM((width, rows), bf16),
                pltpu.VMEM((2, width, 2 * block_n), bf16),
            ],
        ),
        out_shape=[
            half_shape,
            half_shape,
            half_shape,
            half_shape,
            struct((parts // 2, 1, 2 * block_n), f32),
            struct((rows, width), f32),
            struct((rows, width), bf16),
            struct((8, width), f32),
        ],
        name="ffn_back",
    )(me, first_b, g2b, ud_all, ud_all, act, slope, g2, hat1, inv1, norm_params)


def qkv_grad_kernel(me_ref, mixed_ref, ctx_ref, g1b_ref, dq_ref, dk_ref, dv_ref, dq2_ref, dk2_ref, dv2_ref, vgrad_ref, keep_a_ref, keep_b_ref, send_a_ref, send_b_ref, gq_ref, go_ref, *, qkv_n, part_rows, vis_n):
    width = mixed_ref.shape[1]
    parts, halves, cut, block_n = keep_a_ref.shape
    out_n = block_n - qkv_n
    groups = block_n // vis_n
    group_rows = cut + keep_b_ref.shape[2] - part_rows
    mixed_t = jnp.transpose(mixed_ref[...])
    for part, refs in enumerate(((dq_ref, dq2_ref), (dk_ref, dk2_ref), (dv_ref, dv2_ref))):
        right = jnp.concatenate([ref[...] for ref in refs], axis=1)
        gq_ref[:, part * width : (part + 1) * width] = dot_nn(mixed_t, right).astype(bf16)
    go_ref[...] = dot_tn(ctx_ref[...], g1b_ref[...]).astype(bf16)
    my_t = me_ref[0]
    my_d = me_ref[1]

    def one_half(s, carry):
        for core, targets in enumerate(((keep_a_ref, keep_b_ref), (send_a_ref, send_b_ref))):
            owner = my_d ^ (2 * s + core)
            for target, first, count in zip(targets, (0, cut), (cut, part_rows - cut)):
                place = pl.ds(pl.multiple_of(owner * part_rows + first, 16), count)
                for t in range(parts):
                    slot = my_t ^ t
                    target[slot, s, :count, :qkv_n] = gq_ref[place, t * qkv_n : (t + 1) * qkv_n]
                    target[slot, s, :count, qkv_n:] = go_ref[place, t * out_n : (t + 1) * out_n]
            for g in range(groups):
                first = owner * (group_rows * groups) + g * group_rows
                place = pl.ds(pl.multiple_of(first, 8), group_rows)
                for t in range(parts):
                    columns = slice(g * vis_n, (g + 1) * vis_n)
                    targets[1][my_t ^ t, s, part_rows - cut :, columns] = vgrad_ref[
                        place, t * vis_n : (t + 1) * vis_n
                    ].astype(bf16)
        return carry

    lax.fori_loop(0, halves, one_half, 0)


def qkv_gradient(me, mixed_b, context, g1b, heads, vgrad, parts, dp_parts, qkv_n, block_n, cut):
    rows, width = mixed_b.shape
    part_rows = width // dp_parts
    vis_n = width // parts
    group_rows = vgrad.shape[0] // dp_parts // (block_n // vis_n)
    half = [
        (parts, dp_parts // 2, count, block_n) for count in (cut, part_rows + group_rows - cut)
    ] * 2
    return pl.pallas_call(
        functools.partial(qkv_grad_kernel, qkv_n=qkv_n, part_rows=part_rows, vis_n=vis_n),
        grid=(1,),
        in_specs=[SMEM_SPEC]
        + [whole_spec((rows, width))] * 3
        + [whole_spec((rows, width // 2))] * 6
        + [whole_spec(vgrad.shape)],
        out_specs=[whole_spec(shape) for shape in half],
        out_shape=[struct(shape, bf16) for shape in half],
        scratch_shapes=[pltpu.VMEM((width, 3 * width), bf16), pltpu.VMEM((width, width), bf16)],
        name="qkv_gradient",
    )(me, mixed_b, context, g1b, *heads, vgrad)


def tail_kernel(
    lens_ref,
    dq_ref,
    dk_ref,
    dv_ref,
    dq2_ref,
    dk2_ref,
    dv2_ref,
    wqkv_ref,
    g1_ref,
    vis_ref,
    normed_ref,
    hat_ref,
    grad_ref,
    vgrad_ref,
    red_ref,
    bn_ref,
):
    step = pl.program_id(0)
    tile, width = g1_ref.shape
    ends = doc_ends(lens_ref)
    grad = g1_ref[...]
    heads = [
        jnp.concatenate([a[...], b[...]], axis=1)
        for a, b in ((dq_ref, dq2_ref), (dk_ref, dk2_ref), (dv_ref, dv2_ref))
    ]
    for part, left in enumerate(heads):
        grad = grad + dot_nt(left, wqkv_ref[:, part * width : (part + 1) * width])
    grad_ref[...] = grad
    rows = lax.broadcasted_iota(jnp.int32, (tile, width), 0) + step * tile
    grad_b = jnp.where(visual_mask(rows, ends), grad, 0.0).astype(bf16)

    @pl.when(step == 0)
    def _():
        red_ref[...] = jnp.zeros(red_ref.shape, f32)
        bn_ref[...] = jnp.zeros(bn_ref.shape, f32)
        vgrad_ref[...] = jnp.zeros(vgrad_ref.shape, f32)

    vgrad_ref[...] += dot_tn(normed_ref[...], grad_b)
    back = dot_nt(grad_b, vis_ref[...])
    bn_ref[0:1, :] += jnp.sum(back * hat_ref[...], axis=0, keepdims=True)
    bn_ref[1:2, :] += jnp.sum(back, axis=0, keepdims=True)
    red_ref[0:1, :] += jnp.sum(grad_b.astype(f32), axis=0, keepdims=True)
    red_ref[1:2, :] += jnp.sum(heads[0].astype(f32), axis=0, keepdims=True)
    red_ref[2:3, :] += jnp.sum(heads[2].astype(f32), axis=0, keepdims=True)


def tail(lengths, heads, w_qkv, g1, vis_full, normed, hat_v):
    rows, width = g1.shape
    channels = normed.shape[1]
    tile = rows // 3
    row_block = lambda n: pl.BlockSpec((tile, n), lambda i: (i, 0))
    return pl.pallas_call(
        tail_kernel,
        grid=(rows // tile,),
        in_specs=[
            SMEM_SPEC,
            *([row_block(width // 2)] * 6),
            whole_spec(w_qkv.shape),
            row_block(width),
            whole_spec(vis_full.shape),
            row_block(channels),
            row_block(channels),
        ],
        out_specs=[
            row_block(width),
            whole_spec((channels, width)),
            whole_spec((8, width)),
            whole_spec((8, channels)),
        ],
        out_shape=[
            struct((rows, width), f32),
            struct((channels, width), f32),
            struct((8, width), f32),
            struct((8, channels), f32),
        ],
        name="tail",
    )(lengths, *heads, w_qkv, g1, vis_full, normed, hat_v)


def axis_bits(name, first=0):
    return [(name, bit) for bit in range(first, (lax.axis_size(name) - 1).bit_length())]


class Collection:
    def __init__(self, value, cut):
        tensor_bits = axis_bits("tensor")
        head = axis_bits("dp", 1) + tensor_bits[:1]
        self.rest = tensor_bits[:0:-1]
        self.heads = [head, head[-1:] + head[:-1]]
        self.core = [("dp", 0)] * 2
        self.cut = cut
        self.whole = value
        self.names = [[], []]
        self.mine = None

    def left(self):
        return len(self.rest) + len(self.heads[0]) + len(self.core) // 2

    def sends(self):
        if self.rest:
            self.bits = self.rest[:1]
            return [self.whole]
        if self.mine is None:
            self.mine = [self.whole[..., : self.cut, :], self.whole[..., self.cut :, :]]
        self.bits = [order[0] for order in self.heads] if self.heads[0] else self.core
        return self.mine

    def arrive(self, values):
        if len(values) == 1:
            self.rest = self.rest[1:]
            self.whole = jnp.stack([self.whole, values[0]])
            self.names = [self.bits + names for names in self.names]
        elif self.heads[0]:
            self.mine = [jnp.stack(pair) for pair in zip(self.mine, values)]
            self.names = [[bit] + names for bit, names in zip(self.bits, self.names)]
            self.heads = [order[1:] for order in self.heads]
        else:
            self.core = []
            self.other = values


class Reduction:
    def __init__(self, keeps, receiveds):
        tensor_bits = axis_bits("tensor")
        dp_bits = axis_bits("dp", 1)
        names = tensor_bits[::-1] + dp_bits[::-1]
        head = dp_bits + tensor_bits[:1]
        self.heads = [head, head[-1:] + head[:-1]]
        self.rest = tensor_bits[1:]
        self.cut = keeps[0].shape[2]
        shape = lambda v: v.reshape([2] * len(names) + list(v.shape[2:]))
        self.pieces = [
            [shape(keep), shape(received), list(names)]
            for keep, received in zip(keeps, receiveds)
        ]

    def left(self):
        return len(self.heads[0]) + len(self.rest)

    def split(self, piece, bit):
        keep, received, names = piece
        place = names.index(bit)
        halves = [
            (
                lax.index_in_dim(keep, side, place, keepdims=False).astype(f32)
                + lax.index_in_dim(received, side, place, keepdims=False).astype(f32)
            ).astype(bf16)
            for side in range(2)
        ]
        piece[0] = halves[0]
        piece[2] = names[:place] + names[place + 1 :]
        return halves[1]

    def sends(self):
        if self.heads[0]:
            self.bits = [order[0] for order in self.heads]
            self.heads = [order[1:] for order in self.heads]
            return [self.split(piece, bit) for piece, bit in zip(self.pieces, self.bits)]
        self.bits = self.rest[:1]
        self.rest = self.rest[1:]
        return [jnp.concatenate([self.split(piece, self.bits[0]) for piece in self.pieces], axis=-2)]

    def arrive(self, values):
        self.received = values[0]
        if len(values) == 1:
            values = [values[0][..., : self.cut, :], values[0][..., self.cut :, :]]
        for piece, value in zip(self.pieces, values):
            piece[1] = value


def flip_permute(values, axis_bit):
    name, bit = axis_bit
    return lax.ppermute(
        values, name, [(i, i ^ (1 << bit)) for i in range(lax.axis_size(name))]
    )


def beside(sums, work, anchor, extra=()):
    sums = [one for one in sums if one.left()]
    sent = [one.sends() for one in sums]
    counts = [len(values) for values in sent]
    sending = sum(sent, []) + [value for value, _ in extra]
    bits = sum([one.bits for one in sums], []) + [bit for _, bit in extra]
    sending, anchor = lax.optimization_barrier((sending, anchor))
    arrived = [flip_permute(value, bit) for value, bit in zip(sending, bits)]
    result = work(anchor)
    arrived, result = lax.optimization_barrier((arrived, result))
    for one, count in zip(sums, counts):
        one.arrive(arrived[:count])
        arrived = arrived[count:]
    return result, arrived


def spread(values):
    count = lax.axis_size("dp") * lax.axis_size("tensor")
    copies = jnp.broadcast_to(values[None], (count,) + values.shape)
    return lax.all_to_all(copies, ("dp", "tensor"), 0, 0, tiled=True)


def lamb_direction(weight, first_moment, second_moment, gradient):
    first_moment = beta_first * first_moment + (1.0 - beta_first) * gradient
    second_moment = beta_second * second_moment + (1.0 - beta_second) * gradient * gradient
    direction = (
        first_moment
        / (1.0 - beta_first**STEP)
        / (jnp.sqrt(second_moment / (1.0 - beta_second**STEP)) + adam_eps)
        + weight_decay * weight
    )
    return first_moment, second_moment, direction


def sum_all(values):
    return jnp.sum(jnp.sum(values, axis=1, keepdims=True), axis=0, keepdims=True)


def up_down_pieces(total, part_rows):
    return [total[:part_rows], total[part_rows:]]


def qkv_out_vis_pieces(total, part_rows, qkv_n, vis_n):
    block = total[:part_rows]
    rest = total[part_rows:]
    vis = [rest[:, g * vis_n : (g + 1) * vis_n] for g in range(total.shape[1] // vis_n)]
    return [block[:, :qkv_n], block[:, qkv_n:], jnp.concatenate(vis, axis=0)]


def lamb_first_kernel(left_ref, right_ref, received_ref, *refs, pieces, lanes_of, shared):
    count = len(lanes_of)
    total = jnp.concatenate(
        [left_ref[...].astype(f32), right_ref[...].astype(f32)], axis=0
    ) + received_ref[...].astype(f32)
    lane = lax.broadcasted_iota(jnp.int32, (1, LANES), 1)
    extra, refs = refs[: 2 * shared], refs[2 * shared :]
    sums = extra[1][...] if shared else jnp.zeros((1, LANES), f32)
    ins, outs = refs[: 2 * count], refs[2 * count :]
    for number, gradient in enumerate(pieces(total)):
        weight_ref, moments_ref = ins[2 * number : 2 * number + 2]
        grad_ref, new_ref, direction_ref = outs[3 * number : 3 * number + 3]
        weight = weight_ref[...]
        first, second, direction = lamb_direction(weight, moments_ref[0], moments_ref[1], gradient)
        grad_ref[...] = gradient
        new_ref[0] = first
        new_ref[1] = second
        direction_ref[...] = direction
        place = lanes_of[number]
        sums = jnp.where(lane == place, sum_all(weight * weight), sums)
        sums = jnp.where(lane == place + 16, sum_all(direction * direction), sums)
    if shared:
        arrived = extra[0]
        own = arrived[0]
        for k in range(1, arrived.shape[0]):
            own = own + arrived[k]
        piece_n = own.shape[1]
        outs[-1][:, :, :piece_n] = jnp.broadcast_to(own[None], arrived.shape)
        outs[-1][:, :, piece_n:] = jnp.broadcast_to(sums[None], (arrived.shape[0], 1, LANES))
    else:
        outs[-1][...] = sums


def lamb_first(reduction, arrays, pieces, lanes_of, shared=()):
    (left, _, _), (right, _, _) = reduction.pieces
    received = reduction.received
    flat = sum([list(pair) for pair in arrays], [])
    shapes = []
    for weight, moments in arrays:
        shapes += [struct(weight.shape, f32), struct(moments.shape, f32), struct(weight.shape, f32)]
    if shared:
        count, _, piece_n = shared[0].shape
        shapes.append(struct((count, 1, piece_n + LANES), f32))
    else:
        shapes.append(struct((1, LANES), f32))
    made = pl.pallas_call(
        functools.partial(
            lamb_first_kernel, pieces=pieces, lanes_of=lanes_of, shared=bool(shared)
        ),
        out_shape=shapes,
        name="lamb_first",
    )(left, right, received, *shared, *flat)
    return [made[3 * k : 3 * k + 3] for k in range(len(arrays))], made[-1]


def pack_kernel(up_ref, bn_ref, red1_ref, red2_ref, red3_ref, mix_ref, *refs, parts):
    xy_refs, diag_refs, out_ref = refs[:parts], refs[parts : 2 * parts], refs[2 * parts]
    width = out_ref.shape[2]
    rows = diag_refs[0].shape[2] // 2
    delta = lax.broadcasted_iota(jnp.int32, (2 * rows, LANES), 0) - (rows - 1)
    column = lax.broadcasted_iota(jnp.int32, (2 * rows, LANES), 1)
    hot = (bucket_index(delta, REL1, EDGES1) == column).astype(f32)
    exact = functools.partial(
        jnp.dot, precision=lax.Precision.HIGHEST, preferred_element_type=f32
    )
    sums_xy = jnp.concatenate([jnp.sum(ref[...], axis=1) for ref in xy_refs], axis=0)
    sums_diag = jnp.concatenate([jnp.sum(ref[...], axis=1) for ref in diag_refs], axis=0)
    lin = exact(sums_diag, hot)[:, :REL1]
    table = jnp.concatenate([lin, exact(sums_xy, mix_ref[...])], axis=1)
    out_ref[...] = jnp.zeros(out_ref.shape, f32)
    channels = bn_ref.shape[1]
    sources = [(up_ref[k : k + 1, :], width) for k in range(up_ref.shape[0])]
    sources += [(bn_ref[k : k + 1, :], channels) for k in range(2)]
    sources += [(ref[k : k + 1, :], width) for ref in (red1_ref, red2_ref) for k in range(2)]
    sources += [(red3_ref[k : k + 1, :], width) for k in range(3)]
    sources += [(ref[2:3, :], width) for ref in (red1_ref, red2_ref)]
    sources += [(table[k : k + 1, :], table.shape[1]) for k in range(HEADS)]
    for row, (value, columns) in enumerate(sources):
        out_ref[row, :, :columns] = value


def pack_small(up_part, red_bn, red1, red2, red3, made, total_rows):
    mix = jnp.asarray(table_mix())
    return pl.pallas_call(
        functools.partial(pack_kernel, parts=len(made)),
        out_shape=struct((total_rows, 1, red1.shape[1]), f32),
        name="pack_small",
    )(up_part, red_bn, red1, red2, red3, mix, *[one[0] for one in made], *[one[1] for one in made])


def lamb_last_kernel(totals_ref, shared_ref, *refs, cuts, big, split):
    small = len(cuts)
    lane = lax.broadcasted_iota(jnp.int32, (1, LANES), 1)
    piece_n = shared_ref.shape[2] - LANES
    sums = shared_ref[0, :, piece_n:]
    for k in range(1, shared_ref.shape[0]):
        sums = sums + shared_ref[k, :, piece_n:]
    squares = jnp.where(lane < big, sums, 0.0)
    moved = jnp.where(lane < big, pltpu.roll(sums, LANES - 16, 1), 0.0)
    ins = refs[: 2 * small + 2 * big]
    outs = refs[2 * small + 2 * big :]
    kept = []
    for k, (row, height, columns) in enumerate(cuts):
        weight_ref, moments_ref = ins[2 * k : 2 * k + 2]
        gradient = [totals_ref[row + r, :, :columns] for r in range(height)]
        gradient = jnp.concatenate(gradient, axis=1 if weight_ref.shape[0] == 1 else 0)
        weight = weight_ref[...]
        pair = [moments_ref[m] if split[k] else moments_ref[:, m, :] for m in range(2)]
        first, second, direction = lamb_direction(weight, pair[0], pair[1], gradient)
        outs[4 * k][...] = gradient
        for m, value in enumerate((first, second)):
            if split[k]:
                outs[4 * k + 2][m] = value
            else:
                outs[4 * k + 2][:, m, :] = value
        squares = jnp.where(lane == big + k, sum_all(weight * weight), squares)
        moved = jnp.where(lane == big + k, sum_all(direction * direction), moved)
        kept.append((weight, direction))
    weight_norms = jnp.sqrt(squares)
    update_norms = jnp.sqrt(moved)
    ratios = weight_norms / jnp.where(lane < big + small, update_norms, 1.0)
    norms = jnp.concatenate([weight_norms, update_norms, ratios], axis=0)
    outs[-1][...] = norms[:, : big + small]

    def step_of(k):
        return learn_rate * jnp.sum(jnp.where(lane == k, ratios, 0.0), axis=1, keepdims=True)

    for k, (weight, direction) in enumerate(kept):
        new = weight - step_of(big + k) * direction
        outs[4 * k + 1][...] = new
        outs[4 * k + 3][...] = new.astype(bf16)
    for k in range(big):
        weight_ref, direction_ref = ins[2 * small + 2 * k : 2 * small + 2 * k + 2]
        new = weight_ref[...] - step_of(k) * direction_ref[...]
        outs[4 * small + 2 * k][...] = new
        outs[4 * small + 2 * k + 1][...] = new.astype(bf16)


def lamb_last(totals, shared, small, cuts, split, big):
    shapes = []
    for weight, moments in small:
        shapes += [
            struct(weight.shape, f32),
            struct(weight.shape, f32),
            struct(moments.shape, f32),
            struct(weight.shape, bf16),
        ]
    for weight, _ in big:
        shapes += [struct(weight.shape, f32), struct(weight.shape, bf16)]
    shapes.append(struct((3, len(small) + len(big)), f32))
    flat = sum([list(pair) for pair in small + big], [])
    return pl.pallas_call(
        functools.partial(lamb_last_kernel, cuts=cuts, big=len(big), split=split),
        out_shape=shapes,
        name="lamb_last",
    )(totals, shared, *flat)


def shards(
    hidden_in,
    visual_maps,
    lengths,
    box_x,
    box_y,
    cotangent,
    vis_weight,
    vis_moments,
    qkv_weight,
    qkv_moments,
    out_weight,
    out_moments,
    up_weight,
    up_moments,
    down_weight,
    down_moments,
    up_bias,
    up_bias_moments,
    bn_params,
    bn_moments,
    norm_params,
    norm_moments,
    bias_rows,
    bias_moments,
    rel_tables,
    table_moments,
):
    rows, width = hidden_in.shape
    channels = visual_maps.shape[1]
    dp_parts = lax.axis_size("dp")
    parts = lax.axis_size("tensor")
    device_total = dp_parts * parts
    part_rows, qkv_n = qkv_weight.shape
    out_n = out_weight.shape[1]
    block_n = qkv_n + out_n
    vis_rows, vis_n = vis_weight.shape
    groups = block_n // vis_n
    group_rows = vis_rows // groups
    me = jnp.stack([lax.axis_index("tensor"), lax.axis_index("dp")]).astype(jnp.int32)
    box_x = box_x.reshape(1, rows)
    box_y = box_y.reshape(1, rows)

    vis_b = vis_weight.astype(bf16)
    qo_shard = jnp.concatenate(
        [
            jnp.concatenate([qkv_weight.astype(bf16), out_weight.astype(bf16)], axis=1),
            jnp.concatenate(
                [vis_b[g * group_rows : (g + 1) * group_rows] for g in range(groups)], axis=1
            ),
        ],
        axis=0,
    )
    ud_shard = jnp.stack([up_weight.astype(bf16), down_weight.astype(bf16).T])
    ud_all = lax.all_gather(ud_shard, ("tensor", "dp"), axis=0, tiled=False).reshape(
        parts, dp_parts, 2, part_rows, block_n
    )
    visual_value = visual_maps.astype(f32)
    sums = jnp.stack([jnp.sum(visual_value, axis=0), jnp.sum(visual_value * visual_value, axis=0)])

    tiles = rows // LANES
    marks = [0, tiles // 3, tiles // 2, tiles - tiles // 6, tiles]
    collection = Collection(qo_shard, (part_rows + group_rows) // 32 * 16)
    (order, spot), _ = beside([collection], lambda x: table_plan(x, box_y), box_x)
    ((bias, near), stats), _ = beside(
        [collection],
        lambda v: (
            relative_bias(lengths, box_x, box_y, rel_tables, 0, marks[1]),
            jnp.sum(spread(v), axis=0),
        ),
        sums,
    )
    for first, last in zip(marks[1:-1], marks[2:]):
        bias, _ = beside(
            [collection],
            lambda b: relative_bias(
                lengths, box_x, box_y, rel_tables, first, last - first, (near, b)
            ),
            bias,
        )
    while collection.left():
        beside([collection], lambda v: v, bias)
    flat = lambda v: v.reshape((-1,) + v.shape[-2:])
    mixed, mixed_b, projected, w_qkv, w_out, vis_full, normed, hat_v = front(
        lengths,
        me,
        hidden_in,
        visual_maps,
        stats,
        bn_params,
        [
            flat(value)
            for pair in zip(collection.mine, collection.other)
            for value in pair
        ],
        collection.names,
        bias_rows,
        float(visual_maps.shape[0] * device_total),
        qkv_n,
        part_rows,
        parts,
    )
    context, probs = attend(projected, bias, rows, width)
    first_b, hat1, inv1 = after_attention(context, mixed, w_out, bias_rows, norm_params)
    act, slope, block_out, g2, g2b, red2 = ffn(
        lengths,
        first_b,
        ud_all,
        up_bias.reshape(parts // 2, 1, 2 * block_n),
        hat1,
        cotangent,
        norm_params,
        bias_rows,
    )
    keep_up, keep_down, send_up, send_down, up_bias_part, g1, g1b, red1 = ffn_back(
        me, first_b, g2b, ud_all, act, slope, g2, hat1, inv1, norm_params
    )
    core = ("dp", 0)
    pairs = width // LANES
    cut = (part_rows + group_rows) // 32 * 16

    def first_half(g):
        grad = dot_nt(g, w_out).astype(bf16)
        return grad, attend_back(projected, context, grad, probs, 0, pairs // 2)

    (grad_context, back_a), received = beside(
        [], first_half, g1b, [(send_up, core), (send_down, core)]
    )
    ud_sum = Reduction((keep_up, keep_down), received)

    def second_half(g):
        back = attend_back(projected, context, g, probs, pairs // 2, pairs // 2)
        heads = tuple(back_a[:3]) + tuple(back[:3])
        return back, heads, tail(lengths, heads, w_qkv, g1, vis_full, normed, hat_v)

    (back_b, heads, (grad_mixed, vgrad, red3, red_bn)), _ = beside(
        [ud_sum], second_half, grad_context
    )
    (keep_a, keep_b, send_a, send_b), _ = beside(
        [ud_sum],
        lambda h: qkv_gradient(
            me, mixed_b, context, g1b, h, vgrad, parts, dp_parts, qkv_n, block_n, cut
        ),
        heads,
    )
    half_heads = HEADS // 2
    thirds = half_heads // 3
    table_parts = []

    def table_step(sums, back, first, count, extra=()):
        made, received = beside(
            sums, lambda g: table_sums(order, spot, g, first, count), back[3], extra
        )
        table_parts.append(made)
        return received

    received = table_step([ud_sum], back_a, 0, thirds, [(send_a, core), (send_b, core)])
    qo_sum = Reduction((keep_a, keep_b), received)
    both = [ud_sum, qo_sum]
    table_step(both, back_a, thirds, half_heads - thirds)
    for part in range(3):
        table_step(both, back_b, part * thirds, thirds)

    by_row = lambda v: v.transpose(1, 0, 2)
    small = [
        (up_bias.reshape(1, -1), up_bias_moments[None]),
        (bn_params, bn_moments),
        (norm_params, norm_moments),
        (bias_rows, by_row(bias_moments)),
        (rel_tables, by_row(table_moments)),
    ]
    split = (False, True, True, False, False)
    ff_rows = up_bias.shape[0] // width
    cuts = []
    total_rows = 0
    for height, columns in [(ff_rows, width)] + [pair[0].shape for pair in small[1:]]:
        cuts.append((total_rows, height, columns))
        total_rows += height
    total_rows = -(-total_rows // 32) * 32

    def small_sum(made):
        packed = pack_small(
            up_bias_part.reshape(ff_rows, width), red_bn, red1, red2, red3, made, total_rows
        )
        packed = packed.reshape(device_total, 1, -1)
        return lax.all_to_all(packed, ("dp", "tensor"), 0, 0, tiled=True)

    arrived, _ = beside([ud_sum, qo_sum], small_sum, table_parts)
    for one in (ud_sum, qo_sum):
        while one.left():
            beside([one], lambda v: v, arrived)
    ud_made, ud_squares = lamb_first(
        ud_sum,
        [(up_weight, up_moments), (down_weight.T, down_moments.transpose(0, 2, 1))],
        functools.partial(up_down_pieces, part_rows=part_rows),
        (3, 4),
    )
    qo_made, copies = lamb_first(
        qo_sum,
        [(qkv_weight, qkv_moments), (out_weight, out_moments), (vis_weight, vis_moments)],
        functools.partial(qkv_out_vis_pieces, part_rows=part_rows, qkv_n=qkv_n, vis_n=vis_n),
        (1, 2, 0),
        (arrived, ud_squares),
    )
    shared = lax.all_to_all(copies, ("dp", "tensor"), 0, 0, tiled=True)
    piece_n = arrived.shape[2]
    if piece_n == width:
        totals = shared
    else:
        totals = shared[:, :, :piece_n].reshape(-1, 1, width)
    made_big = [qo_made[2], qo_made[0], qo_made[1], ud_made[0], ud_made[1]]
    weights = [vis_weight, qkv_weight, out_weight, up_weight, down_weight.T]
    made = lamb_last(
        totals,
        shared,
        small,
        cuts,
        split,
        [(weight, one[2]) for weight, one in zip(weights, made_big)],
    )
    outputs = [block_out, grad_mixed, made[-1]]
    for k in range(5):
        group = [made_big[k][0], made[20 + 2 * k], made_big[k][1], made[20 + 2 * k + 1]]
        if k == 4:
            group = [jnp.swapaxes(value, -1, -2) for value in group]
        outputs += group
    outputs += [made[0].reshape(-1), made[1].reshape(-1), made[2][0], made[3].reshape(-1)]
    for k in range(1, 5):
        group = list(made[4 * k : 4 * k + 4])
        if not split[k]:
            group[2] = by_row(group[2])
        outputs += group
    return tuple(outputs)


def solution(mesh):
    in_specs = (
        P(("dp", "tensor"), None),
        P(("dp", "tensor"), None),
        P(("dp", "tensor"), None),
        P(("dp", "tensor")),
        P(("dp", "tensor")),
        P(("dp", "tensor"), None),
        P("dp", "tensor"),
        P(None, "dp", "tensor"),
        P("dp", "tensor"),
        P(None, "dp", "tensor"),
        P("dp", "tensor"),
        P(None, "dp", "tensor"),
        P("dp", "tensor"),
        P(None, "dp", "tensor"),
        P("tensor", "dp"),
        P(None, "tensor", "dp"),
        P(),
        P(),
        P(),
        P(),
        P(),
        P(),
        P(),
        P(),
        P(),
        P(),
    )
    out_specs = (
        P(("dp", "tensor"), None),
        P(("dp", "tensor"), None),
        P(),
        P("dp", "tensor"),
        P("dp", "tensor"),
        P(None, "dp", "tensor"),
        P("dp", "tensor"),
        P("dp", "tensor"),
        P("dp", "tensor"),
        P(None, "dp", "tensor"),
        P("dp", "tensor"),
        P("dp", "tensor"),
        P("dp", "tensor"),
        P(None, "dp", "tensor"),
        P("dp", "tensor"),
        P("dp", "tensor"),
        P("dp", "tensor"),
        P(None, "dp", "tensor"),
        P("dp", "tensor"),
        P("tensor", "dp"),
        P("tensor", "dp"),
        P(None, "tensor", "dp"),
        P("tensor", "dp"),
        P(),
        P(),
        P(),
        P(),
        P(),
        P(),
        P(),
        P(),
        P(),
        P(),
        P(),
        P(),
        P(),
        P(),
        P(),
        P(),
        P(),
        P(),
        P(),
        P(),
    )
    return jax.shard_map(shards, mesh=mesh, in_specs=in_specs, out_specs=out_specs, check_vma=False)
```

```python
import functools
import math

import jax
import jax.numpy as jnp
import numpy as np
from jax import lax
from jax.experimental import pallas as pl
from jax.experimental.pallas import tpu as pltpu
from jax.sharding import PartitionSpec as P

HEADS = 12
HDIM = 64
PATCHES = 49
REL1 = 32
REL2 = 64
DIST1 = 128
DIST2 = 256
STEP = 10
LANES = 128

layer_eps = 1e-06
batch_eps = 1e-05
beta_first = 0.9
beta_second = 0.999
adam_eps = 1e-06
weight_decay = 0.01
learn_rate = 0.4
masked_score = -1000000000.0
f32 = jnp.float32
bf16 = jnp.bfloat16
SMEM_SPEC = pl.BlockSpec(memory_space=pltpu.SMEM)


def dot_nn(left, right):
    return lax.dot_general(left, right, (((1,), (0,)), ((), ())), preferred_element_type=f32)


def dot_nt(left, right):
    return lax.dot_general(left, right, (((1,), (1,)), ((), ())), preferred_element_type=f32)


def dot_tn(left, right):
    return lax.dot_general(left, right, (((0,), (0,)), ((), ())), preferred_element_type=f32)


def whole_spec(shape):
    zeros = (0,) * len(shape)
    return pl.BlockSpec(tuple(shape), lambda *_: zeros)


def struct(shape, dtype):
    return jax.ShapeDtypeStruct(tuple(shape), dtype)


def bucket_edges(bucket_count, max_distance):
    half = bucket_count // 2
    exact = half // 2
    edges = []
    for level in range(1, half):
        if level < exact:
            edges.append(level)
        else:
            found = max_distance
            for distance in range(exact, max_distance + 1):
                if (
                    exact
                    + int(
                        math.log(distance / exact) / math.log(max_distance / exact) * (half - exact)
                    )
                    >= level
                ):
                    found = distance
                    break
            edges.append(found)
    return edges


EDGES1 = bucket_edges(REL1, DIST1)
EDGES2 = bucket_edges(REL2, DIST2)


def bucket_index(delta, bucket_count, edges):
    half = bucket_count // 2
    exact = half // 2
    distance = jnp.abs(delta)
    level = jnp.minimum(distance, exact)
    for edge in edges[exact:]:
        level = level + (distance >= edge).astype(jnp.int32)
    return jnp.where(delta > 0, half, 0) + level


def doc_ends(lens_ref):
    ends = []
    total = None
    for k in range(lens_ref.shape[1]):
        total = lens_ref[0, k] if total is None else total + lens_ref[0, k]
        ends.append(total)
    return ends


def doc_of(rows, ends):
    found = jnp.zeros(rows.shape, jnp.int32)
    for end in ends:
        found = found + (rows >= end).astype(jnp.int32)
    return found


def visual_mask(rows, ends):
    hit = None
    for end in ends:
        inside = (rows >= end - PATCHES) & (rows < end)
        hit = inside if hit is None else hit | inside
    return hit


def column_of(row_block):
    return jnp.transpose(jnp.broadcast_to(row_block, (LANES, LANES)))


def bias_kernel(lens_ref, xs_ref, ys_ref, xt_ref, yt_ref, tab_ref, *refs, first):
    near_ref, out_ref = (refs[1], refs[0]) if first == 0 else (refs[0], refs[2])
    x_ref, y_ref = refs[-2:]
    tile = out_ref.shape[1]
    cols_total = out_ref.shape[2]
    ends = doc_ends(lens_ref)
    step = pl.program_id(0) + first
    table = tab_ref[...]
    table_lin = jnp.concatenate(
        [table[:, :REL1], jnp.zeros((HEADS, LANES - REL1), f32)], axis=1
    )
    table_xy = table[:, REL1:]
    lanes = lax.broadcasted_iota(jnp.int32, (8, LANES), 1)
    subs = lax.broadcasted_iota(jnp.int32, (8, LANES), 0)

    def lookup(flat, h, index):
        return jnp.take_along_axis(
            jnp.broadcast_to(flat[h : h + 1, :], (8, LANES)), index, axis=1
        )

    @pl.when(step == 0)
    def _():
        def one_group(g, carry):
            place = pl.ds(pl.multiple_of(g * 8, 8), 8)
            for o in range(3):
                delta = lanes + (o - 1) * LANES - subs - g * 8
                lin = bucket_index(delta, REL1, EDGES1)
                for h in range(HEADS):
                    near_ref[h, o, place, :] = lookup(table_lin, h, lin)
            return carry

        lax.fori_loop(0, tile // 8, one_group, 0)

    x_ref[...] = column_of(xt_ref[...])
    y_ref[...] = column_of(yt_ref[...])
    far = [
        [jnp.broadcast_to(table[h : h + 1, b : b + 1], (8, LANES)) for h in range(HEADS)]
        for b in (REL1 // 2 - 1, REL1 - 1)
    ]

    def one_group(g, carry):
        place = pl.ds(pl.multiple_of(g * 8, 8), 8)
        row_doc = doc_of(subs + (step * tile + g * 8), ends)
        x_col = x_ref[place, :]
        y_col = y_ref[place, :]
        for c in range(cols_total // LANES):
            piece = slice(c * LANES, (c + 1) * LANES)
            across = bucket_index(xs_ref[:, piece] - x_col, REL2, EDGES2)
            down = bucket_index(ys_ref[:, piece] - y_col, REL2, EDGES2) + REL2
            same = row_doc == doc_of(lanes + c * LANES, ends)
            offset = jnp.clip(c - step, -1, 1) + 1
            close = jnp.abs(c - step) <= 1
            got_x = [lookup(table_xy, h, across) for h in range(HEADS)]
            got_y = [lookup(table_xy, h, down) for h in range(HEADS)]
            for h in range(HEADS):
                beyond = jnp.where(c > step, far[1][h], far[0][h])
                lin = jnp.where(close, near_ref[h, offset, place, :], beyond)
                out_ref[h, place, piece] = jnp.where(
                    same, got_x[h] + got_y[h] + lin, masked_score
                )
        return carry

    lax.fori_loop(0, tile // 8, one_group, 0)


def relative_bias(lengths, box_x, box_y, tables, first, count, before=()):
    rows = box_x.shape[1]
    tile = LANES
    row_spec = pl.BlockSpec((1, tile), lambda i: (0, first + i))
    near_shape = (HEADS, 3, tile, LANES)
    out_spec = pl.BlockSpec((HEADS, tile, rows), lambda i: (0, first + i, 0))
    out_shape = struct((HEADS, rows, rows), f32)
    return pl.pallas_call(
        functools.partial(bias_kernel, first=first),
        grid=(count,),
        in_specs=[
            SMEM_SPEC,
            whole_spec((1, rows)),
            whole_spec((1, rows)),
            row_spec,
            row_spec,
            whole_spec(tables.shape),
        ]
        + ([whole_spec(near_shape), pl.BlockSpec(memory_space=pl.ANY)] if before else []),
        out_specs=out_spec if before else [out_spec, whole_spec(near_shape)],
        out_shape=out_shape if before else [out_shape, struct(near_shape, f32)],
        scratch_shapes=[pltpu.VMEM((tile, LANES), jnp.int32)] * 2,
        input_output_aliases={7: 0} if before else {},
        name="relative_bias",
    )(lengths, box_x, box_y, box_x, box_y, tables, *before)


def front_kernel(
    lens_ref,
    me_ref,
    hidden_ref,
    maps_ref,
    stats_ref,
    bn_ref,
    a_mine_ref,
    a_other_ref,
    b_mine_ref,
    b_other_ref,
    bias_ref,
    mixed_ref,
    mixed_b_ref,
    proj_ref,
    wqkv_ref,
    wout_ref,
    vis_ref,
    normed_ref,
    hat_ref,
    *,
    total_rows,
    qkv_n,
    part_rows,
    parts,
    names,
):
    tile = hidden_ref.shape[0]
    width = hidden_ref.shape[1]
    cut, block_n = a_mine_ref.shape[1:]
    out_n = block_n - qkv_n
    vis_n = width // parts
    groups = block_n // vis_n
    group_rows = cut + b_mine_ref.shape[1] - part_rows
    dp_half = 2 * a_mine_ref.shape[0] // parts

    def place_of(order, tensor_slot, dp_slot):
        index = 0
        for name, bit in order:
            slot = tensor_slot if name == "tensor" else dp_slot
            index = 2 * index + ((slot >> bit) & 1)
        return index

    @pl.when(pl.program_id(0) == 0)
    def _():
        def one_part(d, carry):
            for core in range(2):
                dp_slot = 2 * d + core
                owner = me_ref[1] ^ dp_slot
                refs = ((a_mine_ref, a_other_ref)[core], (b_mine_ref, b_other_ref)[core])
                for t in range(parts):
                    for ref, order, first, count in zip(
                        refs, names, (0, cut), (cut, part_rows - cut)
                    ):
                        block = ref[place_of(order, me_ref[0] ^ t, dp_slot)]
                        place = pl.ds(pl.multiple_of(owner * part_rows + first, 16), count)
                        wqkv_ref[place, t * qkv_n : (t + 1) * qkv_n] = block[:count, :qkv_n]
                        wout_ref[place, t * out_n : (t + 1) * out_n] = block[:count, qkv_n:]
                    for g in range(groups):
                        first = owner * (group_rows * groups) + g * group_rows
                        place = pl.ds(pl.multiple_of(first, group_rows), group_rows)
                        vis_ref[place, t * vis_n : (t + 1) * vis_n] = block[
                            part_rows - cut :, g * vis_n : (g + 1) * vis_n
                        ]
            return carry

        lax.fori_loop(0, dp_half // 2, one_part, 0)

    ends = doc_ends(lens_ref)
    start = pl.program_id(0) * tile
    visual_total, channels = maps_ref.shape
    rows = lax.broadcasted_iota(jnp.int32, (tile, visual_total), 0) + start
    slots = lax.broadcasted_iota(jnp.int32, (tile, visual_total), 1)
    target = slots
    for k, end in enumerate(ends):
        target = jnp.where(slots >= k * PATCHES, slots - (k + 1) * PATCHES + end, target)
    select = (rows == target).astype(f32).astype(bf16)
    picked = dot_nn(select, maps_ref[...])
    is_visual = visual_mask(
        lax.broadcasted_iota(jnp.int32, (tile, channels), 0) + start, ends
    )
    mean = stats_ref[0:1, :] / total_rows
    var = stats_ref[1:2, :] / total_rows - mean * mean
    hat = (picked - mean) * lax.rsqrt(var + batch_eps)
    hat = jnp.where(is_visual, hat, 0.0)
    hat_ref[...] = hat
    normed = jnp.where(is_visual, hat * bn_ref[0:1, :] + bn_ref[1:2, :], 0.0).astype(bf16)
    normed_ref[...] = normed
    embedded = dot_nn(normed, vis_ref[...]) + bias_ref[0:1, :]
    row_visual = visual_mask(lax.broadcasted_iota(jnp.int32, (tile, width), 0) + start, ends)
    mixed = hidden_ref[...].astype(f32) + jnp.where(row_visual, embedded, 0.0)
    mixed_ref[...] = mixed
    mixed_b = mixed.astype(bf16)
    mixed_b_ref[...] = mixed_b
    for part in range(3):
        columns = slice(part * width, (part + 1) * width)
        piece = dot_nn(mixed_b, wqkv_ref[:, columns])
        if part == 0:
            piece = piece + bias_ref[1:2, :]
        if part == 2:
            piece = piece + bias_ref[2:3, :]
        proj_ref[:, columns] = piece.astype(bf16)


def front(lengths, me, hidden, maps, stats, bn_params, shards_of, names, bias_rows, total_rows, qkv_n, part_rows, parts):
    rows, width = hidden.shape
    channels = maps.shape[1]
    tile = rows // 3 if rows % 384 == 0 else rows
    row_block = lambda n: pl.BlockSpec((tile, n), lambda i: (i, 0))
    return pl.pallas_call(
        functools.partial(
            front_kernel,
            total_rows=total_rows,
            qkv_n=qkv_n,
            part_rows=part_rows,
            parts=parts,
            names=names,
        ),
        grid=(rows // tile,),
        in_specs=[
            SMEM_SPEC,
            SMEM_SPEC,
            row_block(width),
            whole_spec(maps.shape),
            whole_spec(stats.shape),
            whole_spec(bn_params.shape),
            *[whole_spec(piece.shape) for piece in shards_of],
            whole_spec(bias_rows.shape),
        ],
        out_specs=[
            row_block(width),
            row_block(width),
            row_block(3 * width),
            whole_spec((width, 3 * width)),
            whole_spec((width, width)),
            whole_spec((channels, width)),
            row_block(channels),
            row_block(channels),
        ],
        out_shape=[
            struct((rows, width), f32),
            struct((rows, width), bf16),
            struct((rows, 3 * width), bf16),
            struct((width, 3 * width), bf16),
            struct((width, width), bf16),
            struct((channels, width), bf16),
            struct((rows, channels), bf16),
            struct((rows, channels), f32),
        ],
        name="front",
    )(lengths, me, hidden, maps, stats, bn_params, *shards_of, bias_rows)


def pair_mask(shape, h):
    lane = lax.broadcasted_iota(jnp.int32, shape, len(shape) - 1)
    return (lane >= HDIM) if h else (lane < HDIM)


def attend_kernel(q_ref, k_ref, v_ref, bias_ref, ctx_ref, exps_ref, inv_ref):
    queries = q_ref[...].astype(f32) * (HDIM**-0.5)
    context = None
    inverse = None
    for h in range(2):
        mask = pair_mask(queries.shape, h)
        query_h = jnp.where(mask, queries, 0.0).astype(bf16)
        scores = dot_nt(query_h, k_ref[...]) + bias_ref[h]
        exps = jnp.exp(scores - jnp.max(scores, axis=-1, keepdims=True))
        inv = jnp.broadcast_to(1.0 / jnp.sum(exps, axis=-1, keepdims=True), queries.shape)
        exps_b = exps.astype(bf16)
        exps_ref[h] = exps_b
        piece = dot_nn(exps_b, v_ref[...])
        context = piece if context is None else jnp.where(mask, piece, context)
        inverse = inv if inverse is None else jnp.where(mask, inv, inverse)
    inv_ref[...] = inverse
    ctx_ref[...] = (context * inverse).astype(bf16)


def attend(projected, bias, rows, width):
    pairs = width // LANES
    tile = rows // 3
    return pl.pallas_call(
        attend_kernel,
        grid=(pairs, rows // tile),
        in_specs=[
            pl.BlockSpec((tile, LANES), lambda p, i: (i, p)),
            pl.BlockSpec((rows, LANES), lambda p, i: (0, pairs + p)),
            pl.BlockSpec((rows, LANES), lambda p, i: (0, 2 * pairs + p)),
            pl.BlockSpec((2, tile, rows), lambda p, i: (p, i, 0)),
        ],
        out_specs=[
            pl.BlockSpec((tile, LANES), lambda p, i: (i, p)),
            pl.BlockSpec((2, tile, rows), lambda p, i: (p, i, 0)),
            pl.BlockSpec((tile, LANES), lambda p, i: (i, p)),
        ],
        out_shape=[
            struct((rows, width), bf16),
            struct((HEADS, rows, rows), bf16),
            struct((rows, width), f32),
        ],
        name="attend",
    )(projected, projected, projected, bias)


def attend_back_kernel(q_ref, k_ref, v_ref, ctx_ref, gctx_ref, inv_ref, exps_ref, dq_ref, dk_ref, dv_ref, gs_ref):
    rows = q_ref.shape[0]
    tile = rows // 3
    scale = HDIM**-0.5
    keys_h = []
    for h in range(2):
        mask = pair_mask(k_ref.shape, h)
        keys_h.append(jnp.where(mask, k_ref[...].astype(f32), 0.0).astype(bf16))
    grad_k = None
    grad_v = None
    for i in range(rows // tile):
        place = slice(i * tile, (i + 1) * tile)
        queries = q_ref[place, :].astype(f32) * scale
        grads = gctx_ref[place, :].astype(f32) * inv_ref[place, :]
        inner = grads * ctx_ref[place, :].astype(f32)
        grad_q = None
        for h in range(2):
            mask = pair_mask(queries.shape, h)
            query_h = jnp.where(mask, queries, 0.0).astype(bf16)
            grad_h = jnp.where(mask, grads, 0.0).astype(bf16)
            total = jnp.sum(jnp.where(mask, inner, 0.0), axis=-1, keepdims=True)
            grad_probs = dot_nt(grad_h, v_ref[...])
            exps = exps_ref[h, place, :]
            grad_scores = (exps.astype(f32) * (grad_probs - total)).astype(bf16)
            gs_ref[h, place, :] = grad_scores
            piece_q = dot_nn(grad_scores, keys_h[h])
            piece_k = dot_tn(grad_scores, query_h)
            piece_v = dot_tn(exps, grad_h)
            grad_q = piece_q if grad_q is None else grad_q + piece_q
            grad_k = piece_k if grad_k is None else grad_k + piece_k
            grad_v = piece_v if grad_v is None else grad_v + piece_v
        dq_ref[place, :] = (grad_q * scale).astype(bf16)
    dk_ref[...] = grad_k.astype(bf16)
    dv_ref[...] = grad_v.astype(bf16)


def attend_back(projected, context, grad_context, attended, first_pair, pair_count):
    rows, width = context.shape
    pairs = width // LANES
    column = lambda shift: pl.BlockSpec((rows, LANES), lambda p: (0, shift + first_pair + p))
    plain = pl.BlockSpec((rows, LANES), lambda p: (0, p))
    n = pair_count
    return pl.pallas_call(
        attend_back_kernel,
        grid=(n,),
        in_specs=[
            column(0),
            column(pairs),
            column(2 * pairs),
            column(0),
            column(0),
            column(0),
            pl.BlockSpec((2, rows, rows), lambda p: (first_pair + p, 0, 0)),
        ],
        out_specs=[plain, plain, plain, pl.BlockSpec((2, rows, rows), lambda p: (p, 0, 0))],
        out_shape=[
            struct((rows, n * LANES), bf16),
            struct((rows, n * LANES), bf16),
            struct((rows, n * LANES), bf16),
            struct((2 * n, rows, rows), bf16),
        ],
        name="attend_back",
    )(projected, projected, projected, context, grad_context, attended[1], attended[0])


def table_thetas():
    limits = list(EDGES2) + [1 - edge for edge in EDGES2]
    limits = limits + [5000] * (REL2 - len(limits))
    return np.asarray(limits + limits, np.int32)[None, :]


def table_mix():
    count = len(EDGES2)
    mix = np.zeros((2 * REL2, 2 * REL2), np.float32)
    for side in range(2):
        base = side * REL2
        every = base + 2 * count
        above = lambda m: base + m - 1
        below = lambda m: base + count + m - 1
        for m in range(1, count + 1):
            mix[above(m), base + REL2 // 2 + m] -= 1.0
            if m < count:
                mix[above(m + 1), base + REL2 // 2 + m] += 1.0
            else:
                mix[every, base + REL2 // 2 + m] += 1.0
            mix[below(m), base + m] += 1.0
            if m < count:
                mix[below(m + 1), base + m] -= 1.0
        mix[above(1), base] += 1.0
        mix[below(1), base] -= 1.0
    return mix


def table_plan_kernel(xs_ref, ys_ref, theta_ref, order_ref, spot_ref):
    rows = xs_ref.shape[1]
    chunks = rows // LANES
    lane = lax.broadcasted_iota(jnp.int32, (LANES, LANES), 1)
    sub = lax.broadcasted_iota(jnp.int32, (LANES, LANES), 0)
    wide = 8 * LANES
    for side, line_ref in enumerate((xs_ref, ys_ref)):
        line = line_ref[...]
        below = jnp.zeros((1, wide), f32)
        for c in range(chunks):
            column = column_of(line[:, c * LANES : (c + 1) * LANES])
            rank = jnp.zeros((LANES, 1), f32)
            for e in range(chunks):
                other = line[:, e * LANES : (e + 1) * LANES]
                earlier = (other < column) | (
                    (other == column) & (lane + e * LANES < sub + c * LANES)
                )
                rank = rank + jnp.sum(earlier.astype(f32), axis=1, keepdims=True)
            level = lax.broadcasted_iota(jnp.int32, (LANES, rows), 1).astype(f32)
            order_ref[c * LANES : (c + 1) * LANES, side * rows : (side + 1) * rows] = (
                (rank <= level).astype(f32).astype(bf16)
            )
            steps = lax.broadcasted_iota(jnp.int32, (LANES, wide), 1)
            wide_column = jnp.concatenate([column] * 8, axis=1)
            below = below + jnp.sum((wide_column < steps).astype(f32), axis=0, keepdims=True)
        below_i = below.astype(jnp.int32)
        for c in range(chunks):
            column = column_of(line[:, c * LANES : (c + 1) * LANES])
            limit = jnp.clip(column + theta_ref[...], 0, wide - 1)
            found = jnp.zeros((LANES, LANES), jnp.int32)
            for e in range(8):
                piece = jnp.broadcast_to(below_i[:, e * LANES : (e + 1) * LANES], (LANES, LANES))
                got = jnp.take_along_axis(piece, limit & (LANES - 1), axis=1)
                found = jnp.where((limit >> 7) == e, got, found)
            place = slice(c * LANES, (c + 1) * LANES)
            if side == 0:
                spot_ref[place, :] = found - 1
            else:
                spot_ref[place, :] = jnp.where(lane < REL2, spot_ref[place, :], found - 1)


def table_plan(box_x, box_y):
    rows = box_x.shape[1]
    thetas = jnp.asarray(table_thetas())
    return pl.pallas_call(
        table_plan_kernel,
        grid=(1,),
        in_specs=[whole_spec((1, rows)), whole_spec((1, rows)), whole_spec((1, LANES))],
        out_specs=[whole_spec((rows, 2 * rows)), whole_spec((rows, LANES))],
        out_shape=[struct((rows, 2 * rows), bf16), struct((rows, LANES), jnp.int32)],
        name="table_plan",
    )(box_x, box_y, thetas)


def table_kernel(order_ref, spot_ref, gs_ref, xy_ref, diag_ref, *prefix_refs):
    rows = gs_ref.shape[1]
    chunks = rows // LANES
    lane8 = lax.broadcasted_iota(jnp.int32, (8, LANES), 1)
    lane = lax.broadcasted_iota(jnp.int32, (LANES, LANES), 1)
    sub = lax.broadcasted_iota(jnp.int32, (LANES, LANES), 0)
    flip = (lane + sub == LANES - 1).astype(f32).astype(bf16)
    pad = jnp.zeros((LANES, LANES), f32)
    zero = jnp.zeros((8, LANES), f32)
    total = zero
    near = jnp.zeros((8, 4 * LANES), f32)
    far = [zero, zero]
    for c in range(chunks):
        prefix_refs[c][...] = dot_nn(gs_ref[0, c * LANES : (c + 1) * LANES, :], order_ref[...])
    for c in range(chunks):
        for g in range(LANES // 8):
            here = slice(g * 8, g * 8 + 8)
            spot = spot_ref[c * LANES + g * 8 : c * LANES + g * 8 + 8, :]
            low = spot & (LANES - 1)
            high = spot >> 7
            found = zero
            for e in range(chunks):
                got_x, got_y = [
                    jnp.take_along_axis(
                        prefix_refs[c][here, side + e * LANES : side + (e + 1) * LANES], low, axis=1
                    )
                    for side in (0, rows)
                ]
                found = jnp.where(high == e, jnp.where(lane8 < REL2, got_x, got_y), found)
            total = total + found
        place = slice(c * LANES, (c + 1) * LANES)
        left, right = max(c - 1, 0), min(c + 2, chunks)
        turned = [dot_nn(flip, gs_ref[0, place, left * LANES : right * LANES])]
        if c == 0:
            turned = [pad] + turned
        if right == c + 1:
            turned = turned + [pad]
        turned = pltpu.roll(
            jnp.concatenate(turned + [pad], axis=1), 0, 1, stride=1, stride_axis=0
        )
        near = near + jnp.sum(turned.reshape(LANES // 8, 8, 4 * LANES), axis=0)
        for e in range(chunks):
            if abs(e - c) > 1:
                piece = gs_ref[0, place, e * LANES : (e + 1) * LANES].astype(f32)
                far[e > c] = far[e > c] + jnp.sum(piece.reshape(LANES // 8, 8, LANES), axis=0)
    xy_ref[0] = total
    diag_ref[...] = jnp.zeros(diag_ref.shape, f32)
    diag_ref[0, :, rows - 2 * LANES : rows + 2 * LANES] = near
    diag_ref[0, :, :LANES] += far[0]
    diag_ref[0, :, 2 * rows - LANES :] += far[1]


def table_sums(order, spot, grad_scores, first, heads):
    rows = grad_scores.shape[1]
    return pl.pallas_call(
        table_kernel,
        grid=(heads,),
        in_specs=[
            whole_spec(order.shape),
            whole_spec(spot.shape),
            pl.BlockSpec((1, rows, rows), lambda h: (first + h, 0, 0)),
        ],
        out_specs=[
            pl.BlockSpec((1, 8, LANES), lambda h: (h, 0, 0)),
            pl.BlockSpec((1, 8, 2 * rows), lambda h: (h, 0, 0)),
        ],
        out_shape=[struct((heads, 8, LANES), f32), struct((heads, 8, 2 * rows), f32)],
        scratch_shapes=[pltpu.VMEM((LANES, 2 * rows), f32)] * (rows // LANES),
        name="table_sums",
    )(order, spot, grad_scores)


def row_mean(values):
    return jnp.mean(values, axis=-1, keepdims=True)


def after_kernel(ctx_ref, mixed_ref, wout_ref, bias_ref, norm_ref, first_ref, hat_ref, inv_ref):
    values = mixed_ref[...] + dot_nn(ctx_ref[...], wout_ref[...]) + bias_ref[3:4, :]
    centred = values - row_mean(values)
    inverse = lax.rsqrt(row_mean(centred * centred) + layer_eps)
    hat = centred * inverse
    hat_ref[...] = hat
    inv_ref[...] = inverse
    first_ref[...] = (hat * norm_ref[0:1, :] + norm_ref[1:2, :]).astype(bf16)


def after_attention(context, mixed, w_out, bias_rows, norm_params):
    rows, width = mixed.shape
    tile = rows // 3
    row_block = lambda n: pl.BlockSpec((tile, n), lambda i: (i, 0))
    return pl.pallas_call(
        after_kernel,
        grid=(rows // tile,),
        in_specs=[
            row_block(width),
            row_block(width),
            whole_spec(w_out.shape),
            whole_spec(bias_rows.shape),
            whole_spec(norm_params.shape),
        ],
        out_specs=[row_block(width), row_block(width), row_block(1)],
        out_shape=[
            struct((rows, width), bf16),
            struct((rows, width), f32),
            struct((rows, 1), f32),
        ],
        name="after_attention",
    )(context, mixed, w_out, bias_rows, norm_params)


def joined(ref, width):
    columns = ref.shape[-1]
    return jnp.concatenate([ref[g, :, 0].reshape(width, columns) for g in range(2)], axis=1)


def ffn_kernel(
    lens_ref,
    first_ref,
    up_ref,
    down_ref,
    ubias_ref,
    hat_ref,
    cot_ref,
    norm_ref,
    bias_ref,
    act_ref,
    slope_ref,
    out_ref,
    g2_ref,
    g2b_ref,
    red_ref,
    acc_ref,
):
    step = pl.program_id(0)
    rows, width = first_ref.shape
    block_n = up_ref.shape[-1]
    pre = dot_nn(first_ref[...], joined(up_ref, width)) + ubias_ref[0]
    cdf = 0.5 + 0.5 * lax.erf(pre * (2.0**-0.5))
    act = (pre * cdf).astype(bf16)
    act_ref[0] = act
    slope_ref[0] = (cdf + pre * (jnp.exp(-0.5 * pre * pre) * ((2.0 * math.pi) ** -0.5))).astype(
        bf16
    )
    piece = dot_nt(act, joined(down_ref, width))

    @pl.when(step == 0)
    def _():
        acc_ref[...] = piece

    @pl.when(step > 0)
    def _():
        acc_ref[...] += piece

    @pl.when(step == pl.num_programs(0) - 1)
    def _():
        ends = doc_ends(lens_ref)
        tile = LANES
        red_ref[...] = jnp.zeros(red_ref.shape, f32)

        def one_tile(i, carry):
            place = pl.ds(pl.multiple_of(i * tile, tile), tile)
            values = (
                hat_ref[place, :] * norm_ref[0:1, :]
                + norm_ref[1:2, :]
                + acc_ref[place, :]
                + bias_ref[4:5, :]
            )
            centred = values - row_mean(values)
            inverse = lax.rsqrt(row_mean(centred * centred) + layer_eps)
            hat = centred * inverse
            out_ref[place, :] = (hat * norm_ref[2:3, :] + norm_ref[3:4, :]).astype(bf16)
            row = lax.broadcasted_iota(jnp.int32, (tile, width), 0) + i * tile
            grad = jnp.where(row < ends[-1], cot_ref[place, :].astype(f32), 0.0)
            scaled = grad * norm_ref[2:3, :]
            g2 = inverse * (scaled - row_mean(scaled) - hat * row_mean(scaled * hat))
            g2_ref[place, :] = g2
            g2b_ref[place, :] = g2.astype(bf16)
            red_ref[0:1, :] += jnp.sum(grad * hat, axis=0, keepdims=True)
            red_ref[1:2, :] += jnp.sum(grad, axis=0, keepdims=True)
            red_ref[2:3, :] += jnp.sum(g2, axis=0, keepdims=True)
            return carry

        lax.fori_loop(0, rows // tile, one_tile, 0)


def ffn(lengths, first_b, ud_all, up_bias, hat1, cotangent, norm_params, bias_rows):
    rows, width = first_b.shape
    parts, dp_parts, _, part_rows, block_n = ud_all.shape
    weight = lambda which: pl.BlockSpec(
        (2, dp_parts, 1, part_rows, block_n), lambda t: (t, 0, which, 0, 0)
    )
    block = pl.BlockSpec((1, rows, 2 * block_n), lambda t: (t, 0, 0))
    return pl.pallas_call(
        ffn_kernel,
        grid=(parts // 2,),
        in_specs=[
            SMEM_SPEC,
            whole_spec(first_b.shape),
            weight(0),
            weight(1),
            pl.BlockSpec((1, 1, 2 * block_n), lambda t: (t, 0, 0)),
            whole_spec(hat1.shape),
            whole_spec(cotangent.shape),
            whole_spec(norm_params.shape),
            whole_spec(bias_rows.shape),
        ],
        out_specs=[
            block,
            block,
            whole_spec((rows, width)),
            whole_spec((rows, width)),
            whole_spec((rows, width)),
            whole_spec((8, width)),
        ],
        out_shape=[
            struct((parts // 2, rows, 2 * block_n), bf16),
            struct((parts // 2, rows, 2 * block_n), bf16),
            struct((rows, width), bf16),
            struct((rows, width), f32),
            struct((rows, width), bf16),
            struct((8, width), f32),
        ],
        scratch_shapes=[pltpu.VMEM((rows, width), f32)],
        name="ffn",
    )(lengths, first_b, ud_all, ud_all, up_bias, hat1, cotangent, norm_params, bias_rows)


def ffn_back_kernel(
    me_ref,
    first_ref,
    g2b_ref,
    up_ref,
    down_ref,
    act_ref,
    slope_ref,
    g2_ref,
    hat_ref,
    inv_ref,
    norm_ref,
    keep_up_ref,
    keep_down_ref,
    send_up_ref,
    send_down_ref,
    ub_ref,
    g1_ref,
    g1b_ref,
    red_ref,
    acc_ref,
    first_t_ref,
    g2_t_ref,
    grad_ref,
):
    step = pl.program_id(0)
    rows, width = first_ref.shape
    _, dp_parts, _, part_rows, block_n = up_ref.shape
    mine = me_ref[1]

    @pl.when(step == 0)
    def _():
        first_t_ref[...] = jnp.transpose(first_ref[...])
        g2_t_ref[...] = jnp.transpose(g2b_ref[...])

    grad_act = dot_nn(g2b_ref[...], joined(down_ref, width))
    grad_pre = (slope_ref[0].astype(f32) * grad_act).astype(bf16)
    ub_ref[0] = jnp.sum(grad_pre.astype(f32), axis=0, keepdims=True)
    grad_ref[0] = dot_nn(first_t_ref[...], grad_pre).astype(bf16)
    grad_ref[1] = dot_nn(g2_t_ref[...], act_ref[0]).astype(bf16)
    for slot in range(dp_parts):
        place = pl.ds(pl.multiple_of((mine ^ slot) * part_rows, 16), part_rows)
        targets = (send_up_ref, send_down_ref) if slot % 2 else (keep_up_ref, keep_down_ref)
        for which, target in enumerate(targets):
            for g in range(2):
                target[(me_ref[0] & 1) ^ g, slot // 2] = grad_ref[
                    which, place, g * block_n : (g + 1) * block_n
                ]
    piece = dot_nt(grad_pre, joined(up_ref, width))

    @pl.when(step == 0)
    def _():
        acc_ref[...] = piece

    @pl.when(step > 0)
    def _():
        acc_ref[...] += piece

    @pl.when(step == pl.num_programs(0) - 1)
    def _():
        tile = LANES
        red_ref[...] = jnp.zeros(red_ref.shape, f32)

        def one_tile(i, carry):
            place = pl.ds(pl.multiple_of(i * tile, tile), tile)
            grad = g2_ref[place, :] + acc_ref[place, :]
            hat = hat_ref[place, :]
            scaled = grad * norm_ref[0:1, :]
            g1 = inv_ref[place, :] * (
                scaled - row_mean(scaled) - hat * row_mean(scaled * hat)
            )
            g1b = g1.astype(bf16)
            g1_ref[place, :] = g1
            g1b_ref[place, :] = g1b
            red_ref[0:1, :] += jnp.sum(grad * hat, axis=0, keepdims=True)
            red_ref[1:2, :] += jnp.sum(grad, axis=0, keepdims=True)
            red_ref[2:3, :] += jnp.sum(g1b.astype(f32), axis=0, keepdims=True)
            return carry

        lax.fori_loop(0, rows // tile, one_tile, 0)


def ffn_back(me, first_b, g2b, ud_all, act, slope, g2, hat1, inv1, norm_params):
    rows, width = first_b.shape
    parts, dp_parts, _, part_rows, block_n = ud_all.shape
    weight = lambda which: pl.BlockSpec(
        (2, dp_parts, 1, part_rows, block_n), lambda t, me: (t, 0, which, 0, 0)
    )
    block = pl.BlockSpec((1, rows, 2 * block_n), lambda t, me: (t, 0, 0))
    half = pl.BlockSpec(
        (2, dp_parts // 2, part_rows, block_n), lambda t, me: (t ^ (me[0] >> 1), 0, 0, 0)
    )
    half_shape = struct((parts, dp_parts // 2, part_rows, block_n), bf16)
    return pl.pallas_call(
        ffn_back_kernel,
        grid_spec=pltpu.PrefetchScalarGridSpec(
            num_scalar_prefetch=1,
            grid=(parts // 2,),
            in_specs=[
                whole_spec(first_b.shape),
                whole_spec(g2b.shape),
                weight(0),
                weight(1),
                block,
                block,
                whole_spec(g2.shape),
                whole_spec(hat1.shape),
                whole_spec(inv1.shape),
                whole_spec(norm_params.shape),
            ],
            out_specs=[
                half,
                half,
                half,
                half,
                pl.BlockSpec((1, 1, 2 * block_n), lambda t, me: (t, 0, 0)),
                whole_spec((rows, width)),
                whole_spec((rows, width)),
                whole_spec((8, width)),
            ],
            scratch_shapes=[
                pltpu.VMEM((rows, width), f32),
                pltpu.VMEM((width, rows), bf16),
                pltpu.VMEM((width, rows), bf16),
                pltpu.VMEM((2, width, 2 * block_n), bf16),
            ],
        ),
        out_shape=[
            half_shape,
            half_shape,
            half_shape,
            half_shape,
            struct((parts // 2, 1, 2 * block_n), f32),
            struct((rows, width), f32),
            struct((rows, width), bf16),
            struct((8, width), f32),
        ],
        name="ffn_back",
    )(me, first_b, g2b, ud_all, ud_all, act, slope, g2, hat1, inv1, norm_params)


def qkv_grad_kernel(me_ref, mixed_ref, ctx_ref, g1b_ref, dq_ref, dk_ref, dv_ref, dq2_ref, dk2_ref, dv2_ref, vgrad_ref, keep_a_ref, keep_b_ref, send_a_ref, send_b_ref, gq_ref, go_ref, *, qkv_n, part_rows, vis_n):
    width = mixed_ref.shape[1]
    parts, halves, cut, block_n = keep_a_ref.shape
    out_n = block_n - qkv_n
    groups = block_n // vis_n
    group_rows = cut + keep_b_ref.shape[2] - part_rows
    mixed_t = jnp.transpose(mixed_ref[...])
    for part, refs in enumerate(((dq_ref, dq2_ref), (dk_ref, dk2_ref), (dv_ref, dv2_ref))):
        right = jnp.concatenate([ref[...] for ref in refs], axis=1)
        gq_ref[:, part * width : (part + 1) * width] = dot_nn(mixed_t, right).astype(bf16)
    go_ref[...] = dot_tn(ctx_ref[...], g1b_ref[...]).astype(bf16)
    my_t = me_ref[0]
    my_d = me_ref[1]

    def one_half(s, carry):
        for core, targets in enumerate(((keep_a_ref, keep_b_ref), (send_a_ref, send_b_ref))):
            owner = my_d ^ (2 * s + core)
            for target, first, count in zip(targets, (0, cut), (cut, part_rows - cut)):
                place = pl.ds(pl.multiple_of(owner * part_rows + first, 16), count)
                for t in range(parts):
                    slot = my_t ^ t
                    target[slot, s, :count, :qkv_n] = gq_ref[place, t * qkv_n : (t + 1) * qkv_n]
                    target[slot, s, :count, qkv_n:] = go_ref[place, t * out_n : (t + 1) * out_n]
            for g in range(groups):
                first = owner * (group_rows * groups) + g * group_rows
                place = pl.ds(pl.multiple_of(first, 8), group_rows)
                for t in range(parts):
                    columns = slice(g * vis_n, (g + 1) * vis_n)
                    targets[1][my_t ^ t, s, part_rows - cut :, columns] = vgrad_ref[
                        place, t * vis_n : (t + 1) * vis_n
                    ].astype(bf16)
        return carry

    lax.fori_loop(0, halves, one_half, 0)


def qkv_gradient(me, mixed_b, context, g1b, heads, vgrad, parts, dp_parts, qkv_n, block_n, cut):
    rows, width = mixed_b.shape
    part_rows = width // dp_parts
    vis_n = width // parts
    group_rows = vgrad.shape[0] // dp_parts // (block_n // vis_n)
    half = [
        (parts, dp_parts // 2, count, block_n) for count in (cut, part_rows + group_rows - cut)
    ] * 2
    return pl.pallas_call(
        functools.partial(qkv_grad_kernel, qkv_n=qkv_n, part_rows=part_rows, vis_n=vis_n),
        grid=(1,),
        in_specs=[SMEM_SPEC]
        + [whole_spec((rows, width))] * 3
        + [whole_spec((rows, width // 2))] * 6
        + [whole_spec(vgrad.shape)],
        out_specs=[whole_spec(shape) for shape in half],
        out_shape=[struct(shape, bf16) for shape in half],
        scratch_shapes=[pltpu.VMEM((width, 3 * width), bf16), pltpu.VMEM((width, width), bf16)],
        name="qkv_gradient",
    )(me, mixed_b, context, g1b, *heads, vgrad)


def tail_kernel(
    lens_ref,
    dq_ref,
    dk_ref,
    dv_ref,
    dq2_ref,
    dk2_ref,
    dv2_ref,
    wqkv_ref,
    g1_ref,
    vis_ref,
    normed_ref,
    hat_ref,
    grad_ref,
    vgrad_ref,
    red_ref,
    bn_ref,
):
    step = pl.program_id(0)
    tile, width = g1_ref.shape
    ends = doc_ends(lens_ref)
    grad = g1_ref[...]
    heads = [
        jnp.concatenate([a[...], b[...]], axis=1)
        for a, b in ((dq_ref, dq2_ref), (dk_ref, dk2_ref), (dv_ref, dv2_ref))
    ]
    for part, left in enumerate(heads):
        grad = grad + dot_nt(left, wqkv_ref[:, part * width : (part + 1) * width])
    grad_ref[...] = grad
    rows = lax.broadcasted_iota(jnp.int32, (tile, width), 0) + step * tile
    grad_b = jnp.where(visual_mask(rows, ends), grad, 0.0).astype(bf16)

    @pl.when(step == 0)
    def _():
        red_ref[...] = jnp.zeros(red_ref.shape, f32)
        bn_ref[...] = jnp.zeros(bn_ref.shape, f32)
        vgrad_ref[...] = jnp.zeros(vgrad_ref.shape, f32)

    vgrad_ref[...] += dot_tn(normed_ref[...], grad_b)
    back = dot_nt(grad_b, vis_ref[...])
    bn_ref[0:1, :] += jnp.sum(back * hat_ref[...], axis=0, keepdims=True)
    bn_ref[1:2, :] += jnp.sum(back, axis=0, keepdims=True)
    red_ref[0:1, :] += jnp.sum(grad_b.astype(f32), axis=0, keepdims=True)
    red_ref[1:2, :] += jnp.sum(heads[0].astype(f32), axis=0, keepdims=True)
    red_ref[2:3, :] += jnp.sum(heads[2].astype(f32), axis=0, keepdims=True)


def tail(lengths, heads, w_qkv, g1, vis_full, normed, hat_v):
    rows, width = g1.shape
    channels = normed.shape[1]
    tile = rows // 3
    row_block = lambda n: pl.BlockSpec((tile, n), lambda i: (i, 0))
    return pl.pallas_call(
        tail_kernel,
        grid=(rows // tile,),
        in_specs=[
            SMEM_SPEC,
            *([row_block(width // 2)] * 6),
            whole_spec(w_qkv.shape),
            row_block(width),
            whole_spec(vis_full.shape),
            row_block(channels),
            row_block(channels),
        ],
        out_specs=[
            row_block(width),
            whole_spec((channels, width)),
            whole_spec((8, width)),
            whole_spec((8, channels)),
        ],
        out_shape=[
            struct((rows, width), f32),
            struct((channels, width), f32),
            struct((8, width), f32),
            struct((8, channels), f32),
        ],
        name="tail",
    )(lengths, *heads, w_qkv, g1, vis_full, normed, hat_v)


def axis_bits(name, first=0):
    return [(name, bit) for bit in range(first, (lax.axis_size(name) - 1).bit_length())]


class Collection:
    def __init__(self, value, cut):
        tensor_bits = axis_bits("tensor")
        head = axis_bits("dp", 1) + tensor_bits[:1]
        self.rest = tensor_bits[:0:-1]
        self.heads = [head, head[-1:] + head[:-1]]
        self.core = [("dp", 0)] * 2
        self.cut = cut
        self.whole = value
        self.names = [[], []]
        self.mine = None

    def left(self):
        return len(self.rest) + len(self.heads[0]) + len(self.core) // 2

    def sends(self):
        if self.rest:
            self.bits = self.rest[:1]
            return [self.whole]
        if self.mine is None:
            self.mine = [self.whole[..., : self.cut, :], self.whole[..., self.cut :, :]]
        self.bits = [order[0] for order in self.heads] if self.heads[0] else self.core
        return self.mine

    def arrive(self, values):
        if len(values) == 1:
            self.rest = self.rest[1:]
            self.whole = jnp.stack([self.whole, values[0]])
            self.names = [self.bits + names for names in self.names]
        elif self.heads[0]:
            self.mine = [jnp.stack(pair) for pair in zip(self.mine, values)]
            self.names = [[bit] + names for bit, names in zip(self.bits, self.names)]
            self.heads = [order[1:] for order in self.heads]
        else:
            self.core = []
            self.other = values


class Reduction:
    def __init__(self, keeps, receiveds):
        tensor_bits = axis_bits("tensor")
        dp_bits = axis_bits("dp", 1)
        names = tensor_bits[::-1] + dp_bits[::-1]
        head = dp_bits + tensor_bits[:1]
        self.heads = [head, head[-1:] + head[:-1]]
        self.rest = tensor_bits[1:]
        self.cut = keeps[0].shape[2]
        shape = lambda v: v.reshape([2] * len(names) + list(v.shape[2:]))
        self.pieces = [
            [shape(keep), shape(received), list(names)]
            for keep, received in zip(keeps, receiveds)
        ]

    def left(self):
        return len(self.heads[0]) + len(self.rest)

    def split(self, piece, bit):
        keep, received, names = piece
        place = names.index(bit)
        halves = [
            (
                lax.index_in_dim(keep, side, place, keepdims=False).astype(f32)
                + lax.index_in_dim(received, side, place, keepdims=False).astype(f32)
            ).astype(bf16)
            for side in range(2)
        ]
        piece[0] = halves[0]
        piece[2] = names[:place] + names[place + 1 :]
        return halves[1]

    def sends(self):
        if self.heads[0]:
            self.bits = [order[0] for order in self.heads]
            self.heads = [order[1:] for order in self.heads]
            return [self.split(piece, bit) for piece, bit in zip(self.pieces, self.bits)]
        self.bits = self.rest[:1]
        self.rest = self.rest[1:]
        return [jnp.concatenate([self.split(piece, self.bits[0]) for piece in self.pieces], axis=-2)]

    def arrive(self, values):
        self.received = values[0]
        if len(values) == 1:
            values = [values[0][..., : self.cut, :], values[0][..., self.cut :, :]]
        for piece, value in zip(self.pieces, values):
            piece[1] = value


def flip_permute(values, axis_bit):
    name, bit = axis_bit
    return lax.ppermute(
        values, name, [(i, i ^ (1 << bit)) for i in range(lax.axis_size(name))]
    )


def beside(sums, work, anchor, extra=()):
    sums = [one for one in sums if one.left()]
    sent = [one.sends() for one in sums]
    counts = [len(values) for values in sent]
    sending = sum(sent, []) + [value for value, _ in extra]
    bits = sum([one.bits for one in sums], []) + [bit for _, bit in extra]
    sending, anchor = lax.optimization_barrier((sending, anchor))
    arrived = [flip_permute(value, bit) for value, bit in zip(sending, bits)]
    result = work(anchor)
    arrived, result = lax.optimization_barrier((arrived, result))
    for one, count in zip(sums, counts):
        one.arrive(arrived[:count])
        arrived = arrived[count:]
    return result, arrived


def spread(values):
    count = lax.axis_size("dp") * lax.axis_size("tensor")
    copies = jnp.broadcast_to(values[None], (count,) + values.shape)
    return lax.all_to_all(copies, ("dp", "tensor"), 0, 0, tiled=True)


def lamb_direction(weight, first_moment, second_moment, gradient):
    first_moment = beta_first * first_moment + (1.0 - beta_first) * gradient
    second_moment = beta_second * second_moment + (1.0 - beta_second) * gradient * gradient
    direction = (
        first_moment
        / (1.0 - beta_first**STEP)
        / (jnp.sqrt(second_moment / (1.0 - beta_second**STEP)) + adam_eps)
        + weight_decay * weight
    )
    return first_moment, second_moment, direction


def sum_all(values):
    return jnp.sum(jnp.sum(values, axis=1, keepdims=True), axis=0, keepdims=True)


def up_down_pieces(total, part_rows):
    return [total[:part_rows], total[part_rows:]]


def qkv_out_vis_pieces(total, part_rows, qkv_n, vis_n):
    block = total[:part_rows]
    rest = total[part_rows:]
    vis = [rest[:, g * vis_n : (g + 1) * vis_n] for g in range(total.shape[1] // vis_n)]
    return [block[:, :qkv_n], block[:, qkv_n:], jnp.concatenate(vis, axis=0)]


def lamb_first_kernel(left_ref, right_ref, received_ref, *refs, pieces, lanes_of, shared):
    count = len(lanes_of)
    total = jnp.concatenate(
        [left_ref[...].astype(f32), right_ref[...].astype(f32)], axis=0
    ) + received_ref[...].astype(f32)
    lane = lax.broadcasted_iota(jnp.int32, (1, LANES), 1)
    extra, refs = refs[: 2 * shared], refs[2 * shared :]
    sums = extra[1][...] if shared else jnp.zeros((1, LANES), f32)
    ins, outs = refs[: 2 * count], refs[2 * count :]
    for number, gradient in enumerate(pieces(total)):
        weight_ref, moments_ref = ins[2 * number : 2 * number + 2]
        grad_ref, new_ref, direction_ref = outs[3 * number : 3 * number + 3]
        weight = weight_ref[...]
        first, second, direction = lamb_direction(weight, moments_ref[0], moments_ref[1], gradient)
        grad_ref[...] = gradient
        new_ref[0] = first
        new_ref[1] = second
        direction_ref[...] = direction
        place = lanes_of[number]
        sums = jnp.where(lane == place, sum_all(weight * weight), sums)
        sums = jnp.where(lane == place + 16, sum_all(direction * direction), sums)
    if shared:
        arrived = extra[0]
        own = arrived[0]
        for k in range(1, arrived.shape[0]):
            own = own + arrived[k]
        piece_n = own.shape[1]
        outs[-1][:, :, :piece_n] = jnp.broadcast_to(own[None], arrived.shape)
        outs[-1][:, :, piece_n:] = jnp.broadcast_to(sums[None], (arrived.shape[0], 1, LANES))
    else:
        outs[-1][...] = sums


def lamb_first(reduction, arrays, pieces, lanes_of, shared=()):
    (left, _, _), (right, _, _) = reduction.pieces
    received = reduction.received
    flat = sum([list(pair) for pair in arrays], [])
    shapes = []
    for weight, moments in arrays:
        shapes += [struct(weight.shape, f32), struct(moments.shape, f32), struct(weight.shape, f32)]
    if shared:
        count, _, piece_n = shared[0].shape
        shapes.append(struct((count, 1, piece_n + LANES), f32))
    else:
        shapes.append(struct((1, LANES), f32))
    made = pl.pallas_call(
        functools.partial(
            lamb_first_kernel, pieces=pieces, lanes_of=lanes_of, shared=bool(shared)
        ),
        out_shape=shapes,
        name="lamb_first",
    )(left, right, received, *shared, *flat)
    return [made[3 * k : 3 * k + 3] for k in range(len(arrays))], made[-1]


def pack_kernel(up_ref, bn_ref, red1_ref, red2_ref, red3_ref, mix_ref, *refs, parts):
    xy_refs, diag_refs, out_ref = refs[:parts], refs[parts : 2 * parts], refs[2 * parts]
    width = out_ref.shape[2]
    rows = diag_refs[0].shape[2] // 2
    delta = lax.broadcasted_iota(jnp.int32, (2 * rows, LANES), 0) - (rows - 1)
    column = lax.broadcasted_iota(jnp.int32, (2 * rows, LANES), 1)
    hot = (bucket_index(delta, REL1, EDGES1) == column).astype(f32)
    exact = functools.partial(
        jnp.dot, precision=lax.Precision.HIGHEST, preferred_element_type=f32
    )
    sums_xy = jnp.concatenate([jnp.sum(ref[...], axis=1) for ref in xy_refs], axis=0)
    sums_diag = jnp.concatenate([jnp.sum(ref[...], axis=1) for ref in diag_refs], axis=0)
    lin = exact(sums_diag, hot)[:, :REL1]
    table = jnp.concatenate([lin, exact(sums_xy, mix_ref[...])], axis=1)
    out_ref[...] = jnp.zeros(out_ref.shape, f32)
    channels = bn_ref.shape[1]
    sources = [(up_ref[k : k + 1, :], width) for k in range(up_ref.shape[0])]
    sources += [(bn_ref[k : k + 1, :], channels) for k in range(2)]
    sources += [(ref[k : k + 1, :], width) for ref in (red1_ref, red2_ref) for k in range(2)]
    sources += [(red3_ref[k : k + 1, :], width) for k in range(3)]
    sources += [(ref[2:3, :], width) for ref in (red1_ref, red2_ref)]
    sources += [(table[k : k + 1, :], table.shape[1]) for k in range(HEADS)]
    for row, (value, columns) in enumerate(sources):
        out_ref[row, :, :columns] = value


def pack_small(up_part, red_bn, red1, red2, red3, made, total_rows):
    mix = jnp.asarray(table_mix())
    return pl.pallas_call(
        functools.partial(pack_kernel, parts=len(made)),
        out_shape=struct((total_rows, 1, red1.shape[1]), f32),
        name="pack_small",
    )(up_part, red_bn, red1, red2, red3, mix, *[one[0] for one in made], *[one[1] for one in made])


def lamb_last_kernel(totals_ref, shared_ref, *refs, cuts, big, split):
    small = len(cuts)
    lane = lax.broadcasted_iota(jnp.int32, (1, LANES), 1)
    piece_n = shared_ref.shape[2] - LANES
    sums = shared_ref[0, :, piece_n:]
    for k in range(1, shared_ref.shape[0]):
        sums = sums + shared_ref[k, :, piece_n:]
    squares = jnp.where(lane < big, sums, 0.0)
    moved = jnp.where(lane < big, pltpu.roll(sums, LANES - 16, 1), 0.0)
    ins = refs[: 2 * small + 2 * big]
    outs = refs[2 * small + 2 * big :]
    kept = []
    for k, (row, height, columns) in enumerate(cuts):
        weight_ref, moments_ref = ins[2 * k : 2 * k + 2]
        gradient = [totals_ref[row + r, :, :columns] for r in range(height)]
        gradient = jnp.concatenate(gradient, axis=1 if weight_ref.shape[0] == 1 else 0)
        weight = weight_ref[...]
        pair = [moments_ref[m] if split[k] else moments_ref[:, m, :] for m in range(2)]
        first, second, direction = lamb_direction(weight, pair[0], pair[1], gradient)
        outs[4 * k][...] = gradient
        for m, value in enumerate((first, second)):
            if split[k]:
                outs[4 * k + 2][m] = value
            else:
                outs[4 * k + 2][:, m, :] = value
        squares = jnp.where(lane == big + k, sum_all(weight * weight), squares)
        moved = jnp.where(lane == big + k, sum_all(direction * direction), moved)
        kept.append((weight, direction))
    weight_norms = jnp.sqrt(squares)
    update_norms = jnp.sqrt(moved)
    ratios = weight_norms / jnp.where(lane < big + small, update_norms, 1.0)
    norms = jnp.concatenate([weight_norms, update_norms, ratios], axis=0)
    outs[-1][...] = norms[:, : big + small]

    def step_of(k):
        return learn_rate * jnp.sum(jnp.where(lane == k, ratios, 0.0), axis=1, keepdims=True)

    for k, (weight, direction) in enumerate(kept):
        new = weight - step_of(big + k) * direction
        outs[4 * k + 1][...] = new
        outs[4 * k + 3][...] = new.astype(bf16)
    for k in range(big):
        weight_ref, direction_ref = ins[2 * small + 2 * k : 2 * small + 2 * k + 2]
        new = weight_ref[...] - step_of(k) * direction_ref[...]
        outs[4 * small + 2 * k][...] = new
        outs[4 * small + 2 * k + 1][...] = new.astype(bf16)


def lamb_last(totals, shared, small, cuts, split, big):
    shapes = []
    for weight, moments in small:
        shapes += [
            struct(weight.shape, f32),
            struct(weight.shape, f32),
            struct(moments.shape, f32),
            struct(weight.shape, bf16),
        ]
    for weight, _ in big:
        shapes += [struct(weight.shape, f32), struct(weight.shape, bf16)]
    shapes.append(struct((3, len(small) + len(big)), f32))
    flat = sum([list(pair) for pair in small + big], [])
    return pl.pallas_call(
        functools.partial(lamb_last_kernel, cuts=cuts, big=len(big), split=split),
        out_shape=shapes,
        name="lamb_last",
    )(totals, shared, *flat)


def shards(
    hidden_in,
    visual_maps,
    lengths,
    box_x,
    box_y,
    cotangent,
    vis_weight,
    vis_moments,
    qkv_weight,
    qkv_moments,
    out_weight,
    out_moments,
    up_weight,
    up_moments,
    down_weight,
    down_moments,
    up_bias,
    up_bias_moments,
    bn_params,
    bn_moments,
    norm_params,
    norm_moments,
    bias_rows,
    bias_moments,
    rel_tables,
    table_moments,
):
    rows, width = hidden_in.shape
    channels = visual_maps.shape[1]
    dp_parts = lax.axis_size("dp")
    parts = lax.axis_size("tensor")
    device_total = dp_parts * parts
    part_rows, qkv_n = qkv_weight.shape
    out_n = out_weight.shape[1]
    block_n = qkv_n + out_n
    vis_rows, vis_n = vis_weight.shape
    groups = block_n // vis_n
    group_rows = vis_rows // groups
    me = jnp.stack([lax.axis_index("tensor"), lax.axis_index("dp")]).astype(jnp.int32)
    box_x = box_x.reshape(1, rows)
    box_y = box_y.reshape(1, rows)

    vis_b = vis_weight.astype(bf16)
    qo_shard = jnp.concatenate(
        [
            jnp.concatenate([qkv_weight.astype(bf16), out_weight.astype(bf16)], axis=1),
            jnp.concatenate(
                [vis_b[g * group_rows : (g + 1) * group_rows] for g in range(groups)], axis=1
            ),
        ],
        axis=0,
    )
    ud_shard = jnp.stack([up_weight.astype(bf16), down_weight.astype(bf16).T])
    ud_all = lax.all_gather(ud_shard, ("tensor", "dp"), axis=0, tiled=False).reshape(
        parts, dp_parts, 2, part_rows, block_n
    )
    visual_value = visual_maps.astype(f32)
    sums = jnp.stack([jnp.sum(visual_value, axis=0), jnp.sum(visual_value * visual_value, axis=0)])

    tiles = rows // LANES
    marks = [0, 1, 2, 3, tiles]
    collection = Collection(qo_shard, (part_rows + group_rows) // 32 * 16)
    ((bias, near), stats), _ = beside(
        [collection],
        lambda v: (
            relative_bias(lengths, box_x, box_y, rel_tables, 0, marks[1]),
            jnp.sum(spread(v), axis=0),
        ),
        sums,
    )
    for first, last in zip(marks[1:-1], marks[2:]):
        bias, _ = beside(
            [collection],
            lambda b: relative_bias(
                lengths, box_x, box_y, rel_tables, first, last - first, (near, b)
            ),
            bias,
        )
    (bias, order, spot), _ = beside(
        [collection], lambda v: (v[1], *table_plan(v[0], box_y)), (box_x, bias)
    )
    while collection.left():
        beside([collection], lambda v: v, bias)
    flat = lambda v: v.reshape((-1,) + v.shape[-2:])
    mixed, mixed_b, projected, w_qkv, w_out, vis_full, normed, hat_v = front(
        lengths,
        me,
        hidden_in,
        visual_maps,
        stats,
        bn_params,
        [
            flat(value)
            for pair in zip(collection.mine, collection.other)
            for value in pair
        ],
        collection.names,
        bias_rows,
        float(visual_maps.shape[0] * device_total),
        qkv_n,
        part_rows,
        parts,
    )
    context, *attended = attend(projected, bias, rows, width)
    first_b, hat1, inv1 = after_attention(context, mixed, w_out, bias_rows, norm_params)
    act, slope, block_out, g2, g2b, red2 = ffn(
        lengths,
        first_b,
        ud_all,
        up_bias.reshape(parts // 2, 1, 2 * block_n),
        hat1,
        cotangent,
        norm_params,
        bias_rows,
    )
    keep_up, keep_down, send_up, send_down, up_bias_part, g1, g1b, red1 = ffn_back(
        me, first_b, g2b, ud_all, act, slope, g2, hat1, inv1, norm_params
    )
    core = ("dp", 0)
    pairs = width // LANES
    cut = (part_rows + group_rows) // 32 * 16

    def first_half(g):
        grad = dot_nt(g, w_out).astype(bf16)
        return grad, attend_back(projected, context, grad, attended, 0, pairs // 2)

    (grad_context, back_a), received = beside(
        [], first_half, g1b, [(send_up, core), (send_down, core)]
    )
    ud_sum = Reduction((keep_up, keep_down), received)

    def second_half(g):
        back = attend_back(projected, context, g, attended, pairs // 2, pairs // 2)
        heads = tuple(back_a[:3]) + tuple(back[:3])
        return back, heads, tail(lengths, heads, w_qkv, g1, vis_full, normed, hat_v)

    (back_b, heads, (grad_mixed, vgrad, red3, red_bn)), _ = beside(
        [ud_sum], second_half, grad_context
    )
    (keep_a, keep_b, send_a, send_b), _ = beside(
        [ud_sum],
        lambda h: qkv_gradient(
            me, mixed_b, context, g1b, h, vgrad, parts, dp_parts, qkv_n, block_n, cut
        ),
        heads,
    )
    half_heads = HEADS // 2
    thirds = half_heads // 3
    table_parts = []

    def table_step(sums, back, first, count, extra=()):
        made, received = beside(
            sums, lambda g: table_sums(order, spot, g, first, count), back[3], extra
        )
        table_parts.append(made)
        return received

    received = table_step([ud_sum], back_a, 0, thirds, [(send_a, core), (send_b, core)])
    qo_sum = Reduction((keep_a, keep_b), received)
    both = [ud_sum, qo_sum]
    table_step(both, back_a, thirds, half_heads - thirds)
    for part in range(3):
        table_step(both, back_b, part * thirds, thirds)

    by_row = lambda v: v.transpose(1, 0, 2)
    small = [
        (up_bias.reshape(1, -1), up_bias_moments[None]),
        (bn_params, bn_moments),
        (norm_params, norm_moments),
        (bias_rows, by_row(bias_moments)),
        (rel_tables, by_row(table_moments)),
    ]
    split = (False, True, True, False, False)
    ff_rows = up_bias.shape[0] // width
    cuts = []
    total_rows = 0
    for height, columns in [(ff_rows, width)] + [pair[0].shape for pair in small[1:]]:
        cuts.append((total_rows, height, columns))
        total_rows += height
    total_rows = -(-total_rows // 32) * 32

    def small_sum(made):
        packed = pack_small(
            up_bias_part.reshape(ff_rows, width), red_bn, red1, red2, red3, made, total_rows
        )
        packed = packed.reshape(device_total, 1, -1)
        return lax.all_to_all(packed, ("dp", "tensor"), 0, 0, tiled=True)

    arrived, _ = beside([ud_sum, qo_sum], small_sum, table_parts)
    for one in (ud_sum, qo_sum):
        while one.left():
            beside([one], lambda v: v, arrived)
    ud_made, ud_squares = lamb_first(
        ud_sum,
        [(up_weight, up_moments), (down_weight.T, down_moments.transpose(0, 2, 1))],
        functools.partial(up_down_pieces, part_rows=part_rows),
        (3, 4),
    )
    qo_made, copies = lamb_first(
        qo_sum,
        [(qkv_weight, qkv_moments), (out_weight, out_moments), (vis_weight, vis_moments)],
        functools.partial(qkv_out_vis_pieces, part_rows=part_rows, qkv_n=qkv_n, vis_n=vis_n),
        (1, 2, 0),
        (arrived, ud_squares),
    )
    shared = lax.all_to_all(copies, ("dp", "tensor"), 0, 0, tiled=True)
    piece_n = arrived.shape[2]
    if piece_n == width:
        totals = shared
    else:
        totals = shared[:, :, :piece_n].reshape(-1, 1, width)
    made_big = [qo_made[2], qo_made[0], qo_made[1], ud_made[0], ud_made[1]]
    weights = [vis_weight, qkv_weight, out_weight, up_weight, down_weight.T]
    made = lamb_last(
        totals,
        shared,
        small,
        cuts,
        split,
        [(weight, one[2]) for weight, one in zip(weights, made_big)],
    )
    outputs = [block_out, grad_mixed, made[-1]]
    for k in range(5):
        group = [made_big[k][0], made[20 + 2 * k], made_big[k][1], made[20 + 2 * k + 1]]
        if k == 4:
            group = [jnp.swapaxes(value, -1, -2) for value in group]
        outputs += group
    outputs += [made[0].reshape(-1), made[1].reshape(-1), made[2][0], made[3].reshape(-1)]
    for k in range(1, 5):
        group = list(made[4 * k : 4 * k + 4])
        if not split[k]:
            group[2] = by_row(group[2])
        outputs += group
    return tuple(outputs)


def solution(mesh):
    in_specs = (
        P(("dp", "tensor"), None),
        P(("dp", "tensor"), None),
        P(("dp", "tensor"), None),
        P(("dp", "tensor")),
        P(("dp", "tensor")),
        P(("dp", "tensor"), None),
        P("dp", "tensor"),
        P(None, "dp", "tensor"),
        P("dp", "tensor"),
        P(None, "dp", "tensor"),
        P("dp", "tensor"),
        P(None, "dp", "tensor"),
        P("dp", "tensor"),
        P(None, "dp", "tensor"),
        P("tensor", "dp"),
        P(None, "tensor", "dp"),
        P(),
        P(),
        P(),
        P(),
        P(),
        P(),
        P(),
        P(),
        P(),
        P(),
    )
    out_specs = (
        P(("dp", "tensor"), None),
        P(("dp", "tensor"), None),
        P(),
        P("dp", "tensor"),
        P("dp", "tensor"),
        P(None, "dp", "tensor"),
        P("dp", "tensor"),
        P("dp", "tensor"),
        P("dp", "tensor"),
        P(None, "dp", "tensor"),
        P("dp", "tensor"),
        P("dp", "tensor"),
        P("dp", "tensor"),
        P(None, "dp", "tensor"),
        P("dp", "tensor"),
        P("dp", "tensor"),
        P("dp", "tensor"),
        P(None, "dp", "tensor"),
        P("dp", "tensor"),
        P("tensor", "dp"),
        P("tensor", "dp"),
        P(None, "tensor", "dp"),
        P("tensor", "dp"),
        P(),
        P(),
        P(),
        P(),
        P(),
        P(),
        P(),
        P(),
        P(),
        P(),
        P(),
        P(),
        P(),
        P(),
        P(),
        P(),
        P(),
        P(),
        P(),
        P(),
    )
    return jax.shard_map(shards, mesh=mesh, in_specs=in_specs, out_specs=out_specs, check_vma=False)
```
